512 devices in a mesh: rng: 16 (over y, z_hi), azi: 32 (over x, z_lo, core).
Axes of the slice: x: 4, y: 4, z: 16 (z_hi: 4, z_lo: 4; z = z_hi * 4 + z_lo), core: 2. Of those that a mesh axis runs over, the one named last changes fastest.
Arguments:
- observed: float32 [2048, 8192], P('rng', 'azi'), may hold values from -6 to 6
- psf_tiles: float32 [16, 64, 121], P('rng', 'azi'), may hold values from 0.002 to 0.02
Outputs:
- estimate: float32 [2048, 8192], P('rng', 'azi')
- residual: float32 [2048, 8192], P('rng', 'azi')
The draws below stay inside these ranges and needn't reach their ends.
All inputs are finite; a program needn't handle non-finite values.
Results may differ from the reference program's by a relative error of at most 0.00035.
Values sent between devices are 32-bit elements; how exact they have to be, the bound alone decides.
A program may use at most 64 MiB of HBM per device.

```python
import math
import jax
import jax.numpy as jnp
from jax import lax

TILE = 128
KSIZE = 11
ITERS = 2
RADIUS = 5
IMG_ROWS = 2048
IMG_COLS = 8192


def level_of(rng, extent, split, low, high):
    factor_of, own = 1.0, jax.random.fold_in(rng, 6)
    for position, parts in split:
        draws = jnp.exp(jax.random.uniform(jax.random.fold_in(own, position), (parts,), jnp.float32, low / len(split), high / len(split)))
        factor_of = factor_of * jnp.repeat(draws, extent[position] // parts).reshape([-1 if axis == position else 1 for axis in range(len(extent))])
    return factor_of


def centred(rng, shape, deviation, limit, cuts=(), dtype=jnp.bfloat16):
    result = jax.random.normal(rng, shape, jnp.float32) * deviation
    if len(cuts) > 0:
        result = level_of(rng, shape, cuts, -0.22, 0.18) * result
    return jnp.clip(result, min=-limit, max=limit).astype(dtype)


def setup_inputs(seed: int = 0) -> dict:
    key_list = jax.random.split(jax.random.key(seed), 3)
    observed = centred(key_list[0], (IMG_ROWS, IMG_COLS), 1.0, 6.0, ((0, 16), (1, 32)), jnp.float32)
    psf_tiles = jnp.clip(jnp.exp(math.log(0.02) - 2.30258502 * jax.random.uniform(key_list[1], (IMG_ROWS // TILE, IMG_COLS // TILE, KSIZE * KSIZE), jnp.float32) ** level_of(key_list[1], (IMG_ROWS // TILE, IMG_COLS // TILE, KSIZE * KSIZE), ((0, 16), (1, 32)), -0.2, 0.2)), 0.002, 0.02)
    return {"observed": observed, "psf_tiles": psf_tiles}


def blur(field, psf_tiles):
    tiles_r = IMG_ROWS // TILE
    tiles_c = IMG_COLS // TILE
    padded = jnp.pad(field, RADIUS)

    def add_tap(tap, summed):
        tap_index = jnp.asarray(tap).astype(jnp.int32)
        row_off = tap_index // KSIZE
        col_off = tap_index % KSIZE
        piece = lax.dynamic_slice(padded, (row_off, col_off), (IMG_ROWS, IMG_COLS))
        weight = lax.dynamic_index_in_dim(psf_tiles, tap_index, 2, keepdims=False)
        return summed + piece.reshape(tiles_r, TILE, tiles_c, TILE) * weight[:, None, :, None]

    start = jnp.zeros((tiles_r, TILE, tiles_c, TILE), jnp.float32)
    summed = lax.fori_loop(0, KSIZE * KSIZE, add_tap, start)
    return summed.reshape(IMG_ROWS, IMG_COLS)


def blur_adjoint(field, psf_tiles):
    tiles_r = IMG_ROWS // TILE
    tiles_c = IMG_COLS // TILE
    shaped = field.reshape(tiles_r, TILE, tiles_c, TILE)

    def add_tap(tap, extended):
        tap_index = jnp.asarray(tap).astype(jnp.int32)
        row_off = tap_index // KSIZE
        col_off = tap_index % KSIZE
        weight = lax.dynamic_index_in_dim(psf_tiles, tap_index, 2, keepdims=False)
        term = (shaped * weight[:, None, :, None]).reshape(IMG_ROWS, IMG_COLS)
        current = lax.dynamic_slice(extended, (row_off, col_off), (IMG_ROWS, IMG_COLS))
        return lax.dynamic_update_slice(extended, current + term, (row_off, col_off))

    start = jnp.zeros((IMG_ROWS + 2 * RADIUS, IMG_COLS + 2 * RADIUS), jnp.float32)
    extended = lax.fori_loop(0, KSIZE * KSIZE, add_tap, start)
    return extended[RADIUS:RADIUS + IMG_ROWS, RADIUS:RADIUS + IMG_COLS]


def reference(observed, psf_tiles):
    estimate = jnp.zeros_like(observed)
    residual = observed
    gradient = blur_adjoint(residual, psf_tiles)
    direction = gradient
    gamma = jnp.sum(gradient * gradient)
    for step in range(ITERS):
        image = blur(direction, psf_tiles)
        delta = jnp.sum(image * image)
        alpha = gamma / delta
        estimate = estimate + alpha * direction
        residual = residual - alpha * image
        if step + 1 < ITERS:
            gradient = blur_adjoint(residual, psf_tiles)
            gamma_new = jnp.sum(gradient * gradient)
            direction = gradient + (gamma_new / gamma) * direction
            gamma = gamma_new
    return estimate, residual
```

```python
import itertools

import jax
import jax.numpy as jnp
from jax import lax
from jax.experimental import pallas as pl
from jax.experimental.pallas import tpu as pltpu
from jax.sharding import PartitionSpec as P

TILE = 128
KSIZE = 11
RADIUS = 5
RIM = 2 * RADIUS
ROWS = 128
COLS = 256
EXT_ROWS = 144
EXT_COLS = 384
PAD = 16
WIDE = KSIZE * TILE
MESH = pl.DeviceIdType.MESH
F32 = jnp.float32
BF16 = jnp.bfloat16

PARTS = {"y": 4, "zh": 4, "x": 4, "zl": 4, "c": 2}
PHASES = (("x", "y", "c"), ("zh", "zl"))
NEIGHBOURS = tuple(
    (dr, da) for dr in (-1, 0, 1) for da in (-1, 0, 1) if (dr, da) != (0, 0)
)


def group_offsets(axes):
    ranges = [range(PARTS[axis]) for axis in axes]
    return [dict(zip(axes, o)) for o in itertools.product(*ranges) if any(o)]


OFFSETS = tuple(group_offsets(axes) for axes in PHASES)


def halves(x):
    high = x.astype(BF16)
    low = (x - high.astype(F32)).astype(BF16)
    return high, low


def kernel(
    obs_ref,
    psf_ref,
    est_ref,
    res_ref,
    taps,
    spread_w,
    gather_w,
    wide,
    tall,
    spill,
    field,
    image,
    grad,
    sides,
    got_rows,
    got_sides,
    got_corners,
    moments,
    got_a,
    got_b,
    halo_send,
    halo_recv,
    sum_send,
    sum_recv,
):
    rng = lax.axis_index("rng")
    azi = lax.axis_index("azi")
    place = {
        "y": rng // 4,
        "zh": rng % 4,
        "x": azi // 8,
        "zl": (azi // 2) % 4,
        "c": azi % 2,
    }

    def member(offset):
        at = {
            axis: lax.rem(place[axis] + offset[axis], PARTS[axis])
            if axis in offset
            else place[axis]
            for axis in PARTS
        }
        return (at["y"] * 4 + at["zh"], at["x"] * 8 + at["zl"] * 2 + at["c"])

    def neighbour(dr, da):
        return (lax.rem(rng + dr + 16, 16), lax.rem(azi + da + 32, 32))

    barrier = pltpu.get_barrier_semaphore()
    partners = [neighbour(*d) for d in NEIGHBOURS]
    partners += [member(o) for offsets in OFFSETS for o in offsets]
    for partner in partners:
        pl.semaphore_signal(barrier, inc=1, device_id=partner, device_id_type=MESH)

    lane = lax.broadcasted_iota(jnp.int32, (TILE, TILE), 1)
    row = lax.broadcasted_iota(jnp.int32, (TILE, TILE), 0)

    taps[...] = jnp.zeros_like(taps)
    taps[0:2, 0 : KSIZE * KSIZE] = psf_ref[0]
    for t in range(2):
        gather_w[t, 3 * TILE :, :] = jnp.zeros((TILE, WIDE), BF16)

        def build(u, packed, t=t):
            line = jnp.broadcast_to(taps[t : t + 1, :], (TILE, TILE))
            line = pltpu.roll(line, lax.rem(2 * TILE - KSIZE * u, TILE), 1)
            line = jnp.where(lane < KSIZE, line, 0.0)
            band = pltpu.roll(line, 0, 1, stride=1, stride_axis=0)
            block = pl.ds(pl.multiple_of(u * TILE, TILE), TILE)
            high, low = halves(jnp.where(lane >= row, band, 0.0))
            spread_w[t, 0:TILE, block] = high
            spread_w[t, TILE : 2 * TILE, block] = high
            spread_w[t, 2 * TILE :, block] = low
            turned = band.T
            high, low = halves(jnp.where(row >= lane, turned, 0.0))
            gather_w[t, 0:TILE, block] = high
            gather_w[t, TILE : 2 * TILE, block] = high
            gather_w[t, 2 * TILE : 3 * TILE, block] = low
            edge = jnp.where(row < lane, turned, 0.0)[0:PAD]
            high, low = halves(edge)
            gather_w[t, 3 * TILE : 3 * TILE + PAD, block] = high
            gather_w[t, 3 * TILE + PAD : 3 * TILE + 2 * PAD, block] = high
            gather_w[t, 3 * TILE + 2 * PAD : 3 * TILE + 3 * PAD, block] = low
            over = jnp.where(lane < row, band, 0.0)
            return packed + pltpu.roll(over, RIM * u, 1)

        packed = lax.fori_loop(0, KSIZE, build, jnp.zeros((TILE, TILE), F32))
        high, low = halves(packed)
        spread_w[t, 0:TILE, WIDE:] = high
        spread_w[t, TILE : 2 * TILE, WIDE:] = high
        spread_w[t, 2 * TILE :, WIDE:] = low
        wide[t, 0:PAD, :] = jnp.zeros((PAD, WIDE + TILE), F32)
        wide[t, PAD + ROWS :, :] = jnp.zeros((PAD, WIDE + TILE), F32)

    def spread(source, out):
        tall_lane = lax.broadcasted_iota(jnp.int32, (EXT_ROWS, TILE), 1)
        over = None
        for t in range(2):
            high, low = halves(source[:, t * TILE : (t + 1) * TILE])
            left = jnp.concatenate([high, low, high], axis=1)
            for n in range(0, WIDE + TILE, 256):
                wide[t, PAD : PAD + ROWS, n : n + 256] = jnp.dot(
                    left, spread_w[t, :, n : n + 256], preferred_element_type=F32
                )
            total = over
            spare = None
            for u in range(KSIZE):
                rows = pl.ds(PAD - u, EXT_ROWS)
                piece = wide[t, rows, u * TILE : (u + 1) * TILE]
                total = piece if total is None else total + piece
                piece = wide[t, rows, WIDE:]
                if u:
                    piece = pltpu.roll(piece, TILE - RIM * u, 1)
                spare = piece if spare is None else spare + piece
            out[:, t * TILE : (t + 1) * TILE] = total
            over = jnp.where(tall_lane < RIM, spare, 0.0)
        out[:, 2 * TILE :] = over

    def gather(source, t):
        tall_lane = lax.broadcasted_iota(jnp.int32, (EXT_ROWS, TILE), 1)
        high, low = halves(source[:, t * TILE : (t + 1) * TILE])
        edge = jnp.where(tall_lane < RIM, source[:, (t + 1) * TILE : (t + 2) * TILE], 0.0)
        edge_high = edge.astype(BF16).astype(F32)
        edge_low = edge - edge_high
        edge = edge_high + pltpu.roll(edge_low, PAD, 1) + pltpu.roll(edge_high, 2 * PAD, 1)
        left = jnp.concatenate([high, low, high, edge.astype(BF16)], axis=1)
        total = None
        for n in range(0, WIDE, 256):
            width = min(256, WIDE - n)
            tall[t, :, n : n + width] = jnp.dot(
                left, gather_w[t, :, n : n + width], preferred_element_type=F32
            )
        for u in range(KSIZE):
            piece = tall[t, pl.ds(u, ROWS), u * TILE : (u + 1) * TILE]
            total = piece if total is None else total + piece
        return total

    def pack(strip):
        out = None
        for k in range(8):
            part = jnp.concatenate(
                [
                    strip[8 * (k + 8 * j) : 8 * (k + 8 * j) + 8]
                    if 8 * (k + 8 * j) < EXT_ROWS
                    else jnp.zeros((8, TILE), F32)
                    for j in range(3)
                ],
                axis=0,
            )
            part = jnp.where(lane[0:24] < PAD, part, 0.0)
            part = pltpu.roll(part, PAD * k, 1) if k else part
            out = part if out is None else out + part
        return out

    def unpack(packed):
        parts = []
        for k in range(8):
            part = pltpu.roll(packed, TILE - PAD * k, 1) if k else packed
            parts.append(jnp.where(lane[0:24] < RIM, part, 0.0))
        return jnp.concatenate(
            [parts[g % 8][8 * (g // 8) : 8 * (g // 8) + 8] for g in range(EXT_ROWS // 8)],
            axis=0,
        )

    def start_exchange(turn):
        out = spill.at[turn]
        sides[turn, 0] = pack(spill[turn, :, 0:TILE])
        sides[turn, 1] = pack(spill[turn, :, 2 * TILE :])
        low, high = pl.ds(0, PAD), pl.ds(ROWS, PAD)
        first, last = pl.ds(0, TILE), pl.ds(2 * TILE, TILE)
        plan = {
            (-1, 0): (out.at[low, :], got_rows.at[turn, 0]),
            (1, 0): (out.at[high, :], got_rows.at[turn, 1]),
            (0, -1): (sides.at[turn, 0], got_sides.at[turn, 0]),
            (0, 1): (sides.at[turn, 1], got_sides.at[turn, 1]),
            (-1, -1): (out.at[low, first], got_corners.at[turn, 0]),
            (-1, 1): (out.at[low, last], got_corners.at[turn, 1]),
            (1, -1): (out.at[high, first], got_corners.at[turn, 2]),
            (1, 1): (out.at[high, last], got_corners.at[turn, 3]),
        }
        copies = []
        for i, d in enumerate(NEIGHBOURS):
            source, target = plan[d]
            copy = pltpu.make_async_remote_copy(
                src_ref=source,
                dst_ref=target,
                send_sem=halo_send.at[turn, i],
                recv_sem=halo_recv.at[turn, i],
                device_id=neighbour(*d),
                device_id_type=MESH,
            )
            copy.start()
            copies.append(copy)
        return copies

    above = jnp.where(rng > 0, 1.0, 0.0)
    below = jnp.where(rng < 15, 1.0, 0.0)
    left_of = jnp.where(azi > 0, 1.0, 0.0)
    right_of = jnp.where(azi < 31, 1.0, 0.0)

    def finish_exchange(turn, copies):
        for copy in copies:
            copy.wait()
        ext = field.at[turn]
        ext[...] = spill[turn]
        strip_row = lax.broadcasted_iota(jnp.int32, (PAD, EXT_COLS), 0)
        strip_lane = lax.broadcasted_iota(jnp.int32, (PAD, TILE), 1)
        corner_row = strip_row[:, 0:TILE]
        ext[:, 0:TILE] += unpack(got_sides[turn, 1]) * left_of
        ext[:, 2 * TILE :] += unpack(got_sides[turn, 0]) * right_of
        ext[0:PAD, :] += jnp.where(strip_row < RIM, got_rows[turn, 1], 0.0) * above
        ext[ROWS:, :] += jnp.where(strip_row < RIM, got_rows[turn, 0], 0.0) * below
        corner = (corner_row < RIM) & (strip_lane < RIM)
        ext[0:PAD, 0:TILE] += jnp.where(corner, got_corners[turn, 3], 0.0) * (above * left_of)
        ext[0:PAD, 2 * TILE :] += jnp.where(corner, got_corners[turn, 2], 0.0) * (above * right_of)
        ext[ROWS:, 0:TILE] += jnp.where(corner, got_corners[turn, 1], 0.0) * (below * left_of)
        ext[ROWS:, 2 * TILE :] += jnp.where(corner, got_corners[turn, 0], 0.0) * (below * right_of)
        r = lax.broadcasted_iota(jnp.int32, (EXT_ROWS, EXT_COLS), 0)
        c = lax.broadcasted_iota(jnp.int32, (EXT_ROWS, EXT_COLS), 1)
        inside = (
            (r >= jnp.where(rng == 0, RADIUS, 0))
            & (r < jnp.where(rng == 15, ROWS + RADIUS, EXT_ROWS))
            & (c >= jnp.where(azi == 0, RADIUS, 0))
            & (c < jnp.where(azi == 31, COLS + RADIUS, EXT_COLS))
        )
        ext[...] = jnp.where(inside, ext[...], 0.0)

    def square_sum(x):
        return jnp.sum(jnp.sum(x * x, axis=0, keepdims=True), axis=1, keepdims=True)

    def own_squares(turn):
        r = lax.broadcasted_iota(jnp.int32, (EXT_ROWS, EXT_COLS), 0)
        c = lax.broadcasted_iota(jnp.int32, (EXT_ROWS, EXT_COLS), 1)
        own = (r >= RADIUS) & (r < ROWS + RADIUS) & (c >= RADIUS) & (c < COLS + RADIUS)
        return square_sum(jnp.where(own, field[turn], 0.0))

    def own_block(turn):
        grad[turn] = pltpu.roll(field[turn], EXT_COLS - RADIUS, 1)[:, 0:COLS]

    spread(obs_ref[...], spill.at[0])
    pl.semaphore_wait(barrier, len(partners))
    first = start_exchange(0)
    finish_exchange(0, first)
    for t in range(2):
        image[0, :, t * TILE : (t + 1) * TILE] = gather(field.at[0], t)
    spread(image[0], spill.at[1])
    second = start_exchange(1)
    gamma = own_squares(0)
    delta = square_sum(image[0])
    own_block(0)
    finish_exchange(1, second)
    for t in range(2):
        image[1, :, t * TILE : (t + 1) * TILE] = gather(field.at[1], t)
    omega = own_squares(1)
    pi = square_sum(image[1])
    line = lane[0:1]
    moments[0] = jnp.where(
        line == 0, gamma, jnp.where(line == 1, delta, jnp.where(line == 2, omega, pi))
    )
    for phase, got in enumerate((got_a, got_b)):
        for i, o in enumerate(OFFSETS[phase]):
            pltpu.make_async_remote_copy(
                src_ref=moments.at[phase],
                dst_ref=got.at[i],
                send_sem=sum_send.at[phase],
                recv_sem=sum_recv.at[phase],
                device_id=member(o),
                device_id_type=MESH,
            ).start()
        if phase == 0:
            own_block(1)
        pltpu.make_async_copy(got, got, sum_recv.at[phase]).wait()
        moments[phase + 1] = moments[phase] + jnp.sum(got[...], axis=0)
    total = moments[2]
    gamma, delta, omega, pi = (total[:, i : i + 1] for i in range(4))
    alpha = gamma / delta
    rise = alpha * (omega / delta)
    alpha_1 = (omega - delta * (delta / gamma)) / (pi - omega * (omega / delta))
    near = alpha + alpha_1 * rise
    far = alpha * alpha_1
    own = pl.ds(RADIUS, ROWS)
    est_ref[...] = near * grad[0, own, :] - far * grad[1, own, :]
    res_ref[...] = obs_ref[...] - near * image[0] + far * image[1]
    for phase, got in enumerate((got_a, got_b)):
        pltpu.make_async_copy(got, got, sum_send.at[phase]).wait()


def body(observed, psf_tiles):
    block = jax.ShapeDtypeStruct((ROWS, COLS), F32)
    vmem = pl.BlockSpec(memory_space=pltpu.VMEM)
    return pl.pallas_call(
        kernel,
        out_shape=(block, block),
        in_specs=[vmem, vmem],
        out_specs=(vmem, vmem),
        scratch_shapes=[
            pltpu.VMEM((8, TILE), F32),
            pltpu.VMEM((2, 3 * TILE, WIDE + TILE), BF16),
            pltpu.VMEM((2, 4 * TILE, WIDE), BF16),
            pltpu.VMEM((2, ROWS + 2 * PAD, WIDE + TILE), F32),
            pltpu.VMEM((2, EXT_ROWS, WIDE), F32),
            pltpu.VMEM((2, EXT_ROWS, EXT_COLS), F32),
            pltpu.VMEM((2, EXT_ROWS, EXT_COLS), F32),
            pltpu.VMEM((2, ROWS, COLS), F32),
            pltpu.VMEM((2, EXT_ROWS, COLS), F32),
            pltpu.VMEM((2, 2, 24, TILE), F32),
            pltpu.VMEM((2, 2, PAD, EXT_COLS), F32),
            pltpu.VMEM((2, 2, 24, TILE), F32),
            pltpu.VMEM((2, 4, PAD, TILE), F32),
            pltpu.VMEM((3, 1, TILE), F32),
            pltpu.VMEM((len(OFFSETS[0]), 1, TILE), F32),
            pltpu.VMEM((len(OFFSETS[1]), 1, TILE), F32),
            pltpu.SemaphoreType.DMA((2, 8)),
            pltpu.SemaphoreType.DMA((2, 8)),
            pltpu.SemaphoreType.DMA((2,)),
            pltpu.SemaphoreType.DMA((2,)),
        ],
        compiler_params=pltpu.CompilerParams(
            collective_id=0, has_side_effects=True, vmem_limit_bytes=48 << 20
        ),
    )(observed, psf_tiles)


def solution(mesh):
    return jax.shard_map(
        body,
        mesh=mesh,
        in_specs=(P("rng", "azi"), P("rng", "azi", None)),
        out_specs=(P("rng", "azi"), P("rng", "azi")),
        check_vma=False,
    )
```

```python
import itertools

import jax
import jax.numpy as jnp
from jax import lax
from jax.experimental import pallas as pl
from jax.experimental.pallas import tpu as pltpu
from jax.sharding import PartitionSpec as P

TILE = 128
KSIZE = 11
RADIUS = 5
RIM = 2 * RADIUS
ROWS = 128
COLS = 256
EXT_ROWS = 144
EXT_COLS = 384
PAD = 16
WIDE = KSIZE * TILE
MESH = pl.DeviceIdType.MESH
F32 = jnp.float32
BF16 = jnp.bfloat16

PARTS = {"x": 4, "y": 4, "z": 16, "c": 2}
PHASES = (("x", "y", "c"), ("z",))
NEIGHBOURS = tuple(
    (dr, da) for dr in (-1, 0, 1) for da in (-1, 0, 1) if (dr, da) != (0, 0)
)


def group_offsets(axes):
    ranges = [range(PARTS[axis]) for axis in axes]
    offsets = [dict(zip(axes, o)) for o in itertools.product(*ranges) if any(o)]
    return sorted(
        offsets,
        key=lambda o: -sum(min(n, PARTS[a] - n) for a, n in o.items() if a != "c"),
    )


OFFSETS = tuple(group_offsets(axes) for axes in PHASES)


def halves(x):
    high = x.astype(BF16)
    low = (x - high.astype(F32)).astype(BF16)
    return high, low


def kernel(
    obs_hbm,
    psf_hbm,
    grad_hbm,
    image_hbm,
    factors,
    obs_ref,
    psf_ref,
    taps,
    spread_w,
    gather_w,
    wide,
    tall,
    spill,
    field,
    image,
    grad,
    shifted,
    sides,
    got_rows,
    got_sides,
    got_corners,
    moments,
    got_a,
    got_b,
    halo_send,
    halo_recv,
    sum_send,
    sum_recv,
    load,
):
    load_psf = pltpu.make_async_copy(psf_hbm, psf_ref, load.at[0])
    load_obs = pltpu.make_async_copy(obs_hbm, obs_ref, load.at[1])
    load_psf.start()
    load_obs.start()
    rng = lax.axis_index("rng")
    azi = lax.axis_index("azi")
    place = {
        "x": azi // 8,
        "y": rng // 4,
        "z": (rng % 4) * 4 + (azi // 2) % 4,
        "c": azi % 2,
    }

    def member(offset):
        at = {
            axis: lax.rem(place[axis] + offset[axis], PARTS[axis])
            if axis in offset
            else place[axis]
            for axis in PARTS
        }
        return (at["y"] * 4 + at["z"] // 4, at["x"] * 8 + (at["z"] % 4) * 2 + at["c"])

    def neighbour(dr, da):
        return (lax.rem(rng + dr + 16, 16), lax.rem(azi + da + 32, 32))

    barrier = pltpu.get_barrier_semaphore()
    partners = [neighbour(*d) for d in NEIGHBOURS]
    partners += [member(o) for offsets in OFFSETS for o in offsets]
    for partner in partners:
        pl.semaphore_signal(barrier, inc=1, device_id=partner, device_id_type=MESH)

    lane = lax.broadcasted_iota(jnp.int32, (TILE, TILE), 1)
    row = lax.broadcasted_iota(jnp.int32, (TILE, TILE), 0)

    taps[...] = jnp.zeros_like(taps)
    load_psf.wait()
    taps[0:2, 0 : KSIZE * KSIZE] = psf_ref[0]
    for t in range(2):
        gather_w[t, 3 * TILE :, :] = jnp.zeros((TILE, WIDE), BF16)

        def build(u, packed, t=t):
            line = jnp.broadcast_to(taps[t : t + 1, :], (TILE, TILE))
            line = pltpu.roll(line, lax.rem(2 * TILE - KSIZE * u, TILE), 1)
            line = jnp.where(lane < KSIZE, line, 0.0)
            band = pltpu.roll(line, 0, 1, stride=1, stride_axis=0)
            block = pl.ds(pl.multiple_of(u * TILE, TILE), TILE)
            high, low = halves(jnp.where(lane >= row, band, 0.0))
            spread_w[t, 0:TILE, block] = high
            spread_w[t, TILE : 2 * TILE, block] = high
            spread_w[t, 2 * TILE :, block] = low
            turned = band.T
            high, low = halves(jnp.where(row >= lane, turned, 0.0))
            gather_w[t, 0:TILE, block] = high
            gather_w[t, TILE : 2 * TILE, block] = high
            gather_w[t, 2 * TILE : 3 * TILE, block] = low
            edge = jnp.where(row < lane, turned, 0.0)[0:PAD]
            high, low = halves(edge)
            gather_w[t, 3 * TILE : 3 * TILE + PAD, block] = high
            gather_w[t, 3 * TILE + PAD : 3 * TILE + 2 * PAD, block] = high
            gather_w[t, 3 * TILE + 2 * PAD : 3 * TILE + 3 * PAD, block] = low
            over = jnp.where(lane < row, band, 0.0)
            return packed + pltpu.roll(over, RIM * u, 1)

        packed = lax.fori_loop(0, KSIZE, build, jnp.zeros((TILE, TILE), F32))
        high, low = halves(packed)
        spread_w[t, 0:TILE, WIDE:] = high
        spread_w[t, TILE : 2 * TILE, WIDE:] = high
        spread_w[t, 2 * TILE :, WIDE:] = low
        wide[t, 0:PAD, :] = jnp.zeros((PAD, WIDE + TILE), F32)
        wide[t, PAD + ROWS :, :] = jnp.zeros((PAD, WIDE + TILE), F32)

    def spread(source, out):
        tall_lane = lax.broadcasted_iota(jnp.int32, (EXT_ROWS, TILE), 1)
        over = None
        for t in range(2):
            high, low = halves(source[:, t * TILE : (t + 1) * TILE])
            left = jnp.concatenate([high, low, high], axis=1)
            for n in range(0, WIDE + TILE, 256):
                wide[t, PAD : PAD + ROWS, n : n + 256] = jnp.dot(
                    left, spread_w[t, :, n : n + 256], preferred_element_type=F32
                )
            total = over
            spare = None
            for u in range(KSIZE):
                rows = pl.ds(PAD - u, EXT_ROWS)
                piece = wide[t, rows, u * TILE : (u + 1) * TILE]
                total = piece if total is None else total + piece
                piece = wide[t, rows, WIDE:]
                if u:
                    piece = pltpu.roll(piece, TILE - RIM * u, 1)
                spare = piece if spare is None else spare + piece
            out[:, t * TILE : (t + 1) * TILE] = total
            over = jnp.where(tall_lane < RIM, spare, 0.0)
        out[:, 2 * TILE :] = over

    def gather(source, t):
        tall_lane = lax.broadcasted_iota(jnp.int32, (EXT_ROWS, TILE), 1)
        high, low = halves(source[:, t * TILE : (t + 1) * TILE])
        edge = jnp.where(tall_lane < RIM, source[:, (t + 1) * TILE : (t + 2) * TILE], 0.0)
        edge_high = edge.astype(BF16).astype(F32)
        edge_low = edge - edge_high
        edge = edge_high + pltpu.roll(edge_low, PAD, 1) + pltpu.roll(edge_high, 2 * PAD, 1)
        left = jnp.concatenate([high, low, high, edge.astype(BF16)], axis=1)
        total = None
        for n in range(0, WIDE, 256):
            width = min(256, WIDE - n)
            tall[t, :, n : n + width] = jnp.dot(
                left, gather_w[t, :, n : n + width], preferred_element_type=F32
            )
        for u in range(KSIZE):
            piece = tall[t, pl.ds(u, ROWS), u * TILE : (u + 1) * TILE]
            total = piece if total is None else total + piece
        return total

    def pack(strip):
        out = None
        for k in range(8):
            part = jnp.concatenate(
                [
                    strip[8 * (k + 8 * j) : 8 * (k + 8 * j) + 8]
                    if 8 * (k + 8 * j) < EXT_ROWS
                    else jnp.zeros((8, TILE), F32)
                    for j in range(3)
                ],
                axis=0,
            )
            part = jnp.where(lane[0:24] < PAD, part, 0.0)
            part = pltpu.roll(part, PAD * k, 1) if k else part
            out = part if out is None else out + part
        return out

    def unpack(packed):
        parts = []
        for k in range(8):
            part = pltpu.roll(packed, TILE - PAD * k, 1) if k else packed
            parts.append(jnp.where(lane[0:24] < RIM, part, 0.0))
        return jnp.concatenate(
            [parts[g % 8][8 * (g // 8) : 8 * (g // 8) + 8] for g in range(EXT_ROWS // 8)],
            axis=0,
        )

    def start_exchange(turn):
        out = spill.at[turn]
        sides[turn, 0] = pack(spill[turn, :, 0:TILE])
        sides[turn, 1] = pack(spill[turn, :, 2 * TILE :])
        low, high = pl.ds(0, PAD), pl.ds(ROWS, PAD)
        first, last = pl.ds(0, TILE), pl.ds(2 * TILE, TILE)
        plan = {
            (-1, 0): (out.at[low, :], got_rows.at[turn, 0]),
            (1, 0): (out.at[high, :], got_rows.at[turn, 1]),
            (0, -1): (sides.at[turn, 0], got_sides.at[turn, 0]),
            (0, 1): (sides.at[turn, 1], got_sides.at[turn, 1]),
            (-1, -1): (out.at[low, first], got_corners.at[turn, 0]),
            (-1, 1): (out.at[low, last], got_corners.at[turn, 1]),
            (1, -1): (out.at[high, first], got_corners.at[turn, 2]),
            (1, 1): (out.at[high, last], got_corners.at[turn, 3]),
        }
        copies = []
        for i, d in enumerate(NEIGHBOURS):
            source, target = plan[d]
            copy = pltpu.make_async_remote_copy(
                src_ref=source,
                dst_ref=target,
                send_sem=halo_send.at[turn, i],
                recv_sem=halo_recv.at[turn, i],
                device_id=neighbour(*d),
                device_id_type=MESH,
            )
            copy.start()
            copies.append(copy)
        return copies

    above = jnp.where(rng > 0, 1.0, 0.0)
    below = jnp.where(rng < 15, 1.0, 0.0)
    left_of = jnp.where(azi > 0, 1.0, 0.0)
    right_of = jnp.where(azi < 31, 1.0, 0.0)

    def finish_exchange(turn, copies):
        for copy in copies:
            copy.wait()
        ext = field.at[turn]
        ext[...] = spill[turn]
        strip_row = lax.broadcasted_iota(jnp.int32, (PAD, EXT_COLS), 0)
        strip_lane = lax.broadcasted_iota(jnp.int32, (PAD, TILE), 1)
        corner_row = strip_row[:, 0:TILE]
        ext[:, 0:TILE] += unpack(got_sides[turn, 1]) * left_of
        ext[:, 2 * TILE :] += unpack(got_sides[turn, 0]) * right_of
        ext[0:PAD, :] += jnp.where(strip_row < RIM, got_rows[turn, 1], 0.0) * above
        ext[ROWS:, :] += jnp.where(strip_row < RIM, got_rows[turn, 0], 0.0) * below
        corner = (corner_row < RIM) & (strip_lane < RIM)
        ext[0:PAD, 0:TILE] += jnp.where(corner, got_corners[turn, 3], 0.0) * (above * left_of)
        ext[0:PAD, 2 * TILE :] += jnp.where(corner, got_corners[turn, 2], 0.0) * (above * right_of)
        ext[ROWS:, 0:TILE] += jnp.where(corner, got_corners[turn, 1], 0.0) * (below * left_of)
        ext[ROWS:, 2 * TILE :] += jnp.where(corner, got_corners[turn, 0], 0.0) * (below * right_of)
        r = lax.broadcasted_iota(jnp.int32, (EXT_ROWS, EXT_COLS), 0)
        c = lax.broadcasted_iota(jnp.int32, (EXT_ROWS, EXT_COLS), 1)
        inside = (
            (r >= jnp.where(rng == 0, RADIUS, 0))
            & (r < jnp.where(rng == 15, ROWS + RADIUS, EXT_ROWS))
            & (c >= jnp.where(azi == 0, RADIUS, 0))
            & (c < jnp.where(azi == 31, COLS + RADIUS, EXT_COLS))
        )
        ext[...] = jnp.where(inside, ext[...], 0.0)

    def inner(x, y):
        z = x * y
        z = z[:, 0:TILE] + z[:, TILE:]
        while z.shape[0] > 8:
            half = z.shape[0] // 2
            z = z[0:half] + z[half:]
        return jnp.sum(jnp.sum(z, axis=0, keepdims=True), axis=1, keepdims=True)

    def own_block(turn):
        shifted[...] = pltpu.roll(field[turn], EXT_COLS - RADIUS, 1)[:, 0:COLS]
        grad[turn] = shifted[pl.ds(RADIUS, ROWS), :]

    load_obs.wait()
    spread(obs_ref[...], spill.at[0])
    pl.semaphore_wait(barrier, len(partners))
    first = start_exchange(0)
    finish_exchange(0, first)
    for t in range(2):
        image[0, :, t * TILE : (t + 1) * TILE] = gather(field.at[0], t)
    spread(image[0], spill.at[1])
    second = start_exchange(1)
    own_block(0)
    sums = [inner(grad[0], grad[0]), inner(image[0], image[0])]
    finish_exchange(1, second)
    for t in range(2):
        image[1, :, t * TILE : (t + 1) * TILE] = gather(field.at[1], t)
    own_block(1)
    store_grad = pltpu.make_async_copy(grad, grad_hbm, load.at[0])
    store_grad.start()
    sums += [inner(grad[1], grad[1]), inner(grad[0], grad[1])]
    sums += [inner(image[1], image[1]), inner(image[0], image[1])]
    store_image = pltpu.make_async_copy(image, image_hbm, load.at[1])
    store_image.start()
    line = lane[0:1]
    moments[0] = sum(jnp.where(line == i, x, 0.0) for i, x in enumerate(sums))
    for phase, got in enumerate((got_a, got_b)):
        for i, o in enumerate(OFFSETS[phase]):
            pltpu.make_async_remote_copy(
                src_ref=moments.at[phase],
                dst_ref=got.at[i],
                send_sem=sum_send.at[phase],
                recv_sem=sum_recv.at[phase],
                device_id=member(o),
                device_id_type=MESH,
            ).start()
        pltpu.make_async_copy(got, got, sum_recv.at[phase]).wait()
        moments[phase + 1] = moments[phase] + jnp.sum(got[...], axis=0)
    total = moments[2]
    gg, qq, ww, gw, pp, qp = (total[:, i : i + 1] for i in range(6))
    alpha = gg / qq
    gamma_1 = (gg - alpha * gw) - alpha * (gw - alpha * ww)
    rise = 1.0 + gamma_1 / gg
    delta_1 = rise * (rise * qq - alpha * qp) - alpha * (rise * qp - alpha * pp)
    alpha_1 = gamma_1 / delta_1
    near = alpha + alpha_1 * rise
    far = alpha * alpha_1
    factors[...] = jnp.where(line == 0, near, far)
    for phase, got in enumerate((got_a, got_b)):
        pltpu.make_async_copy(got, got, sum_send.at[phase]).wait()
    store_grad.wait()
    store_image.wait()


def finish(grad_hbm, image_hbm, obs_hbm, factors_hbm, est_hbm, res_hbm, grad, image, obs, factors, sems):
    ins = ((factors_hbm, factors), (grad_hbm, grad), (image_hbm, image), (obs_hbm, obs))
    loads = [pltpu.make_async_copy(a, b, sems.at[i]) for i, (a, b) in enumerate(ins)]
    for load in loads:
        load.start()
    loads[0].wait()
    loads[1].wait()
    near, far = factors[:, 0:1], factors[:, 1:2]
    grad[0] = near * grad[0] - far * grad[1]
    store_est = pltpu.make_async_copy(grad.at[0], est_hbm, sems.at[4])
    store_est.start()
    loads[2].wait()
    loads[3].wait()
    image[0] = obs[...] - near * image[0] + far * image[1]
    store_res = pltpu.make_async_copy(image.at[0], res_hbm, sems.at[5])
    store_res.start()
    store_est.wait()
    store_res.wait()


def body(observed, psf_tiles):
    pair = jax.ShapeDtypeStruct((2, ROWS, COLS), F32)
    hbm = pl.BlockSpec(memory_space=pltpu.HBM)
    grads, images, factors = pl.pallas_call(
        kernel,
        out_shape=(pair, pair, jax.ShapeDtypeStruct((1, TILE), F32)),
        in_specs=[hbm, hbm],
        out_specs=(hbm, hbm, pl.BlockSpec(memory_space=pltpu.VMEM)),
        scratch_shapes=[
            pltpu.VMEM((ROWS, COLS), F32),
            pltpu.VMEM((1, 2, KSIZE * KSIZE), F32),
            pltpu.VMEM((8, TILE), F32),
            pltpu.VMEM((2, 3 * TILE, WIDE + TILE), BF16),
            pltpu.VMEM((2, 4 * TILE, WIDE), BF16),
            pltpu.VMEM((2, ROWS + 2 * PAD, WIDE + TILE), F32),
            pltpu.VMEM((2, EXT_ROWS, WIDE), F32),
            pltpu.VMEM((2, EXT_ROWS, EXT_COLS), F32),
            pltpu.VMEM((2, EXT_ROWS, EXT_COLS), F32),
            pltpu.VMEM((2, ROWS, COLS), F32),
            pltpu.VMEM((2, ROWS, COLS), F32),
            pltpu.VMEM((EXT_ROWS, COLS), F32),
            pltpu.VMEM((2, 2, 24, TILE), F32),
            pltpu.VMEM((2, 2, PAD, EXT_COLS), F32),
            pltpu.VMEM((2, 2, 24, TILE), F32),
            pltpu.VMEM((2, 4, PAD, TILE), F32),
            pltpu.VMEM((3, 1, TILE), F32),
            pltpu.VMEM((len(OFFSETS[0]), 1, TILE), F32),
            pltpu.VMEM((len(OFFSETS[1]), 1, TILE), F32),
            pltpu.SemaphoreType.DMA((2, 8)),
            pltpu.SemaphoreType.DMA((2, 8)),
            pltpu.SemaphoreType.DMA((2,)),
            pltpu.SemaphoreType.DMA((2,)),
            pltpu.SemaphoreType.DMA((2,)),
        ],
        compiler_params=pltpu.CompilerParams(
            collective_id=0, has_side_effects=True, vmem_limit_bytes=61 << 20
        ),
    )(observed, psf_tiles)
    block = jax.ShapeDtypeStruct((ROWS, COLS), F32)
    return pl.pallas_call(
        finish,
        out_shape=(block, block),
        in_specs=[pl.BlockSpec(memory_space=pltpu.HBM)] * 4,
        out_specs=(pl.BlockSpec(memory_space=pltpu.HBM),) * 2,
        scratch_shapes=[
            pltpu.VMEM((2, ROWS, COLS), F32),
            pltpu.VMEM((2, ROWS, COLS), F32),
            pltpu.VMEM((ROWS, COLS), F32),
            pltpu.VMEM((1, TILE), F32),
            pltpu.SemaphoreType.DMA((6,)),
        ],
        compiler_params=pltpu.CompilerParams(vmem_limit_bytes=61 << 20),
    )(grads, images, observed, factors)


def solution(mesh):
    return jax.shard_map(
        body,
        mesh=mesh,
        in_specs=(P("rng", "azi"), P("rng", "azi", None)),
        out_specs=(P("rng", "azi"), P("rng", "azi")),
        check_vma=False,
    )
```

```python
import itertools

import jax
import jax.numpy as jnp
from jax import lax
from jax.experimental import pallas as pl
from jax.experimental.pallas import tpu as pltpu
from jax.sharding import PartitionSpec as P

TILE = 128
KSIZE = 11
RADIUS = 5
RIM = 2 * RADIUS
ROWS = 128
COLS = 256
EXT_ROWS = 144
EXT_COLS = 384
TALL_ROWS = 176
PAD = 16
GROUPS = KSIZE * PAD
WIDE = KSIZE * TILE
MESH = pl.DeviceIdType.MESH
F32 = jnp.float32
BF16 = jnp.bfloat16

PARTS = {"x": 4, "y": 4, "z": 16, "c": 2}
PHASES = (("x", "y", "c"), ("z",))
NEIGHBOURS = tuple(
    (dr, da) for dr in (-1, 0, 1) for da in (-1, 0, 1) if (dr, da) != (0, 0)
)


def group_offsets(axes):
    ranges = [range(PARTS[axis]) for axis in axes]
    offsets = [dict(zip(axes, o)) for o in itertools.product(*ranges) if any(o)]
    return sorted(
        offsets,
        key=lambda o: -sum(min(n, PARTS[a] - n) for a, n in o.items() if a != "c"),
    )


OFFSETS = tuple(group_offsets(axes) for axes in PHASES)


def band_group(n):
    return (n * 373) >> 12


def split_rows(x):
    high = x.astype(BF16).astype(F32)
    return high, x - high


def iota(shape, dim):
    return lax.broadcasted_iota(jnp.int32, shape, dim)


def orders(taps):
    a, b = iota((TILE, TILE), 0), iota((TILE, TILE), 1)
    last = KSIZE * KSIZE - 1

    def turned(n):
        return KSIZE * (n - KSIZE * band_group(n)) + band_group(n)

    back = last - b
    wanted = (back, turned(b), jnp.where(back >= 0, turned(jnp.maximum(back, 0)), -1))
    pick = [jnp.where((a == w) & (b <= last), 1.0, 0.0).astype(BF16) for w in wanted]
    first = taps.astype(BF16)
    rest = taps - first.astype(F32)
    second = rest.astype(BF16)
    third = (rest - second.astype(F32)).astype(BF16)
    parts = jnp.concatenate([first, second, third], axis=1)
    out = [taps]
    for p in pick:
        out.append(jnp.dot(parts, jnp.concatenate([p] * 3, axis=0), preferred_element_type=F32))
    row = iota((8, TILE), 0)
    total = out[0]
    for k in range(1, 4):
        total = jnp.where((row >= 2 * k) & (row < 2 * k + 2), pltpu.roll(out[k], 2 * k, 0), total)
    return total


def sloped(line, shift, rows):
    base = pltpu.roll(jnp.broadcast_to(line, (8, TILE)), shift, 1)
    return pltpu.roll(jnp.concatenate([base] * (rows // 8), axis=0), 0, 1, stride=1, stride_axis=0)


def side_gather_weights(left, right):
    i, n = iota((40, TILE), 0), iota((40, TILE), 1)
    j = n - KSIZE * band_group(n)
    halves_ = []
    for kernel_row, start in ((left, 0), (right, 20)):
        band = sloped(kernel_row, TILE - RIM - start, 40)
        c = i - start
        keep = (c >= 0) & (c < 20) & (j < RIM) & (n < 121) & (c - j >= 0) & (c - j < KSIZE)
        halves_.append(jnp.where(keep, band, 0.0))
    high, low = split_rows(jnp.concatenate(halves_, axis=1))
    return jnp.concatenate([high, high, low, jnp.zeros((8, COLS), F32)], axis=0).astype(BF16)


def side_spread_weights(left, right):
    i, n = iota((24, TILE), 0), iota((24, TILE), 1)
    c = n - KSIZE * band_group(n)
    valid = (c < RIM) & (n < 121)
    halves_ = []
    for kernel_row, keep in (
        (left, valid & (i < RIM) & (c <= i)),
        (right, valid & (i >= RIM) & (i < 2 * RIM) & (c >= i - RIM)),
    ):
        band = sloped(kernel_row, TILE - RIM, 24)
        halves_.append(jnp.where(keep, band, 0.0))
    high, low = split_rows(jnp.concatenate(halves_, axis=1))
    return jnp.concatenate([high, high, low, jnp.zeros((TILE - 72, COLS), F32)], axis=0).astype(BF16)


def flat_gather_weights(kernel_row, low_row, high_row):
    lane, row = iota((PAD, TILE), 1), iota((PAD, TILE), 0)
    blocks = []
    for v in range(KSIZE):
        line = jnp.broadcast_to(kernel_row, (PAD, TILE))
        line = pltpu.roll(line, TILE - KSIZE * v, 1) if v else line
        line = jnp.where(lane < KSIZE, line, 0.0)
        blocks.append(pltpu.roll(line, 0, 1, stride=1, stride_axis=0))
    band = jnp.concatenate(blocks, axis=0)
    r = jnp.concatenate([row] * KSIZE, axis=0)
    high, low = split_rows(jnp.where((r >= low_row) & (r < high_row), band, 0.0))
    return (high + pltpu.roll(high, 32, 1) + pltpu.roll(low, 64, 1)).astype(BF16)


def flat_spread_weights(kernel_row, shift):
    lane = iota((PAD, TILE), 1)
    blocks = []
    for v in range(KSIZE):
        line = jnp.broadcast_to(kernel_row, (PAD, TILE))
        line = pltpu.roll(line, (2 * TILE - (KSIZE * KSIZE - KSIZE) + KSIZE * v) % TILE, 1)
        line = pltpu.roll(jnp.where(lane < KSIZE, line, 0.0), shift % TILE, 1)
        line = pltpu.roll(line, 0, 1, stride=1, stride_axis=0)
        blocks.append(jnp.where(lane < PAD, line, 0.0))
    high, low = split_rows(jnp.concatenate(blocks, axis=0))
    return (high + pltpu.roll(high, PAD, 1) + pltpu.roll(low, 2 * PAD, 1)).astype(BF16)


def side_fields(near, far):
    lane = iota(near.shape, 1)
    left = jnp.where(lane >= TILE - RIM, far, jnp.where(lane < RIM, near, 0.0))
    right = jnp.where(lane < 20, far, 0.0)
    x = pltpu.roll(left, RIM, 1) + pltpu.roll(right, 20, 1)
    high, low = split_rows(x)
    return (high + pltpu.roll(low, 40, 1) + pltpu.roll(high, 80, 1)).astype(BF16)


def picked(x, places, width):
    n = iota((TILE, width), 0)
    j = n - KSIZE * band_group(n)
    lane = iota((TILE, width), 1)
    blocks = [
        jnp.where((j < RIM) & (n < 121) & (lane == j + place), 1.0, 0.0).astype(BF16)
        for place in places
    ]
    pick = jnp.concatenate(blocks, axis=0)
    high, low = halves(x)
    return jnp.dot(jnp.concatenate([high, low], axis=1), jnp.concatenate([pick, pick], axis=0), preferred_element_type=F32)


def halves(x):
    high = x.astype(BF16)
    low = (x - high.astype(F32)).astype(BF16)
    return high, low


def kernel(
    obs_hbm,
    psf_hbm,
    grad_hbm,
    image_hbm,
    factors,
    obs_ref,
    psf_ref,
    taps,
    spread_w,
    gather_w,
    wide,
    tall,
    spill,
    tall_field,
    field,
    image,
    grad,
    shifted,
    stage_side,
    stage_down,
    stage_up,
    got_side,
    got_down,
    got_up,
    got_corner_down,
    got_corner_up,
    side_out,
    side_back,
    moments,
    got_a,
    got_b,
    halo_send,
    halo_recv,
    sum_send,
    sum_recv,
    load,
):
    load_psf = pltpu.make_async_copy(psf_hbm, psf_ref, load.at[0])
    load_obs = pltpu.make_async_copy(obs_hbm, obs_ref, load.at[1])
    load_psf.start()
    load_obs.start()
    rng = lax.axis_index("rng")
    azi = lax.axis_index("azi")
    place = {
        "x": azi // 8,
        "y": rng // 4,
        "z": (rng % 4) * 4 + (azi // 2) % 4,
        "c": azi % 2,
    }

    def member(offset):
        at = {
            axis: lax.rem(place[axis] + offset[axis], PARTS[axis])
            if axis in offset
            else place[axis]
            for axis in PARTS
        }
        return (at["y"] * 4 + at["z"] // 4, at["x"] * 8 + (at["z"] % 4) * 2 + at["c"])

    def neighbour(dr, da):
        return (lax.rem(rng + dr + 16, 16), lax.rem(azi + da + 32, 32))

    barrier = pltpu.get_barrier_semaphore()
    partners = [neighbour(*d) for d in NEIGHBOURS]
    partners += [member(o) for offsets in OFFSETS for o in offsets]
    for partner in partners:
        pl.semaphore_signal(barrier, inc=1, device_id=partner, device_id_type=MESH)

    lane = lax.broadcasted_iota(jnp.int32, (TILE, TILE), 1)
    row = lax.broadcasted_iota(jnp.int32, (TILE, TILE), 0)

    taps[...] = jnp.zeros_like(taps)
    load_psf.wait()
    taps[0:2, 0 : KSIZE * KSIZE] = psf_ref[0]
    for t in range(2):
        gather_w[t, 3 * TILE :, :] = jnp.zeros((TILE, WIDE), BF16)

        def build(u, packed, t=t):
            line = jnp.broadcast_to(taps[t : t + 1, :], (TILE, TILE))
            line = pltpu.roll(line, lax.rem(2 * TILE - KSIZE * u, TILE), 1)
            line = jnp.where(lane < KSIZE, line, 0.0)
            band = pltpu.roll(line, 0, 1, stride=1, stride_axis=0)
            block = pl.ds(pl.multiple_of(u * TILE, TILE), TILE)
            high, low = halves(jnp.where(lane >= row, band, 0.0))
            spread_w[t, 0:TILE, block] = high
            spread_w[t, TILE : 2 * TILE, block] = high
            spread_w[t, 2 * TILE :, block] = low
            turned = band.T
            high, low = halves(jnp.where(row >= lane, turned, 0.0))
            gather_w[t, 0:TILE, block] = high
            gather_w[t, TILE : 2 * TILE, block] = high
            gather_w[t, 2 * TILE : 3 * TILE, block] = low
            edge = jnp.where(row < lane, turned, 0.0)[0:PAD]
            high, low = halves(edge)
            gather_w[t, 3 * TILE : 3 * TILE + PAD, block] = high
            gather_w[t, 3 * TILE + PAD : 3 * TILE + 2 * PAD, block] = high
            gather_w[t, 3 * TILE + 2 * PAD : 3 * TILE + 3 * PAD, block] = low
            over = jnp.where(lane < row, band, 0.0)
            return packed + pltpu.roll(over, RIM * u, 1)

        packed = lax.fori_loop(0, KSIZE, build, jnp.zeros((TILE, TILE), F32))
        high, low = halves(packed)
        spread_w[t, 0:TILE, WIDE:] = high
        spread_w[t, TILE : 2 * TILE, WIDE:] = high
        spread_w[t, 2 * TILE :, WIDE:] = low
        wide[t, 0:PAD, :] = jnp.zeros((PAD, WIDE + TILE), F32)
        wide[t, PAD + ROWS :, :] = jnp.zeros((PAD, WIDE + TILE), F32)

    def spread(source, out):
        tall_lane = lax.broadcasted_iota(jnp.int32, (EXT_ROWS, TILE), 1)
        over = None
        for t in range(2):
            high, low = halves(source[:, t * TILE : (t + 1) * TILE])
            left = jnp.concatenate([high, low, high], axis=1)
            for n in range(0, WIDE + TILE, 256):
                wide[t, PAD : PAD + ROWS, n : n + 256] = jnp.dot(
                    left, spread_w[t, :, n : n + 256], preferred_element_type=F32
                )
            total = over
            spare = None
            for u in range(KSIZE):
                rows = pl.ds(PAD - u, EXT_ROWS)
                piece = wide[t, rows, u * TILE : (u + 1) * TILE]
                total = piece if total is None else total + piece
                piece = wide[t, rows, WIDE:]
                if u:
                    piece = pltpu.roll(piece, TILE - RIM * u, 1)
                spare = piece if spare is None else spare + piece
            out[:, t * TILE : (t + 1) * TILE] = total
            over = jnp.where(tall_lane < RIM, spare, 0.0)
        out[:, 2 * TILE :] = over

    def gather(source, row, t):
        tall_lane = lax.broadcasted_iota(jnp.int32, (EXT_ROWS, TILE), 1)
        high, low = halves(source[row : row + EXT_ROWS, t * TILE : (t + 1) * TILE])
        edge = source[row : row + EXT_ROWS, (t + 1) * TILE : (t + 2) * TILE]
        edge = jnp.where(tall_lane < RIM, edge, 0.0)
        edge_high = edge.astype(BF16).astype(F32)
        edge_low = edge - edge_high
        edge = edge_high + pltpu.roll(edge_low, PAD, 1) + pltpu.roll(edge_high, 2 * PAD, 1)
        left = jnp.concatenate([high, low, high, edge.astype(BF16)], axis=1)
        total = None
        for n in range(0, WIDE, 256):
            width = min(256, WIDE - n)
            tall[t, :, n : n + width] = jnp.dot(
                left, gather_w[t, :, n : n + width], preferred_element_type=F32
            )
        for u in range(KSIZE):
            piece = tall[t, pl.ds(u, ROWS), u * TILE : (u + 1) * TILE]
            total = piece if total is None else total + piece
        return total

    def start_exchange():
        side = iota((EXT_ROWS, TILE), 1)
        kernels = orders(taps[...])
        strips = (
            jnp.where(side < 20, spill[:, 0:TILE], 0.0),
            jnp.where(
                side >= TILE - RIM,
                spill[:, TILE : 2 * TILE],
                jnp.where(side < RIM, spill[:, 2 * TILE :], 0.0),
            ),
        )
        for i, strip in enumerate(strips):
            stage_side[i, 0:8] = kernels
            stage_side[i, 8 : 8 + EXT_ROWS] = strip
            stage_side[i, 8 + EXT_ROWS :] = kernels
        stage_down[0:32] = spill[EXT_ROWS - 32 :]
        stage_down[32:] = jnp.concatenate([kernels] * 3, axis=1)
        stage_up[0:8] = jnp.concatenate([kernels] * 3, axis=1)
        stage_up[8:] = spill[0:24]
        whole, head, tail = pl.ds(0, 8 + EXT_ROWS), pl.ds(0, 32), pl.ds(120, 40)
        plan = {
            (-1, 0): (stage_up, got_up),
            (1, 0): (stage_down, got_down),
            (0, -1): (stage_side.at[0, whole], got_side.at[0]),
            (0, 1): (stage_side.at[1, whole], got_side.at[1]),
            (-1, -1): (stage_side.at[0, head], got_corner_up.at[0]),
            (-1, 1): (stage_side.at[1, head], got_corner_up.at[1]),
            (1, -1): (stage_side.at[0, tail], got_corner_down.at[0]),
            (1, 1): (stage_side.at[1, tail], got_corner_down.at[1]),
        }
        copies = []
        for i, d in enumerate(NEIGHBOURS):
            source, target = plan[d]
            copies.append(
                pltpu.make_async_remote_copy(
                    src_ref=source,
                    dst_ref=target,
                    send_sem=halo_send.at[i],
                    recv_sem=halo_recv.at[i],
                    device_id=neighbour(*d),
                    device_id_type=MESH,
                )
            )
        return copies

    above = jnp.where(rng > 0, 1.0, 0.0)
    below = jnp.where(rng < 15, 1.0, 0.0)
    left_of = jnp.where(azi > 0, 1.0, 0.0)
    right_of = jnp.where(azi < 31, 1.0, 0.0)

    def assemble():
        first, last = slice(0, TILE), slice(2 * TILE, EXT_COLS)
        tall_field[0:PAD] = jnp.zeros((PAD, EXT_COLS), F32)
        tall_field[PAD : PAD + EXT_ROWS] = spill[...]
        tall_field[PAD + EXT_ROWS :] = jnp.zeros((PAD, EXT_COLS), F32)
        tall_field[0:32] += got_down[0:32] * above
        tall_field[144:168] += got_up[8:] * below

        def from_left(strip, rows, flag):
            lane = iota(strip.shape, 1)
            tall_field[rows, first] += jnp.where(lane < TILE // 2, strip, 0.0) * flag
            tall_field[rows, last] += jnp.where(lane < TILE // 2, 0.0, strip) * flag

        def from_right(strip, rows, flag):
            tall_field[rows, last] += strip * flag

        middle, top, bottom = slice(16, 160), slice(0, 32), slice(144, 168)
        from_right(got_side[0, 8:], middle, right_of)
        from_left(got_side[1, 8:], middle, left_of)
        from_right(got_corner_down[0, 0:32], top, above * right_of)
        from_left(got_corner_down[1, 0:32], top, above * left_of)
        from_right(got_corner_up[0, 8:], bottom, below * right_of)
        from_left(got_corner_up[1, 8:], bottom, below * left_of)
        r, c = iota((TALL_ROWS, EXT_COLS), 0), iota((TALL_ROWS, EXT_COLS), 1)
        inside = (
            (r >= jnp.where(rng == 0, PAD + RADIUS, 0))
            & (r < jnp.where(rng == 15, PAD + RADIUS + ROWS, TALL_ROWS))
            & (c >= jnp.where(azi == 0, RADIUS, 0))
            & (c < jnp.where(azi == 0, 320, EXT_COLS))
            & ((c < jnp.where(azi == 31, RADIUS + COLS, EXT_COLS)) | (c >= 320))
        )
        tall_field[...] = jnp.where(inside, tall_field[...], 0.0)

    def side_kernels(k):
        return (
            (got_corner_down[1, 33 + k : 34 + k] * (above * left_of), got_corner_down[0, 32 + k : 33 + k] * (above * right_of)),
            (got_side[1, 1 + k : 2 + k] * left_of, got_side[0, k : k + 1] * right_of),
            (got_corner_up[1, 1 + k : 2 + k] * (below * left_of), got_corner_up[0, k : k + 1] * (below * right_of)),
        )

    def side_frames():
        fields = side_fields(tall_field[:, 0:TILE], tall_field[:, 2 * TILE :])
        parts = ((0, 32, 144, 16), (16, 144, 0, 128), (144, 32, 176, 16))
        group = band_group(iota((1, COLS), 1) & (TILE - 1))
        sums = []
        for (start, count, at, rows), (left, right) in zip(parts, side_kernels(2)):
            side_out[at : at + count] = jnp.dot(
                fields[start : start + count], side_gather_weights(left, right), preferred_element_type=F32
            )
            total = jnp.zeros((rows, COLS), F32)
            for u in range(KSIZE):
                total = jnp.where(group == KSIZE - 1 - u, side_out[at + u : at + u + rows], total)
            sums.append(total)
        frames = picked(jnp.concatenate(sums, axis=0), (0, RIM), TILE)
        r = iota(frames.shape, 0)
        return jnp.where((r >= 6) & (r < 154), frames, 0.0)

    def side_spread(frames):
        high, low = split_rows(frames)
        packed = (high + pltpu.roll(low, 24, 1) + pltpu.roll(high, 48, 1)).astype(BF16)
        for (start, stop), (left, right) in zip(((0, 16), (16, 144), (144, 160)), side_kernels(0)):
            side_back[start:stop] = jnp.dot(
                packed[start:stop], side_spread_weights(left, right), preferred_element_type=F32
            )
        group = band_group(iota((1, COLS), 1) & (TILE - 1))
        total = jnp.zeros((EXT_ROWS, COLS), F32)
        for u in range(KSIZE):
            total = jnp.where(group == u, side_back[PAD - u : PAD - u + EXT_ROWS], total)
        out = picked(total, (0, TILE), COLS)
        return out[:, 0:TILE], out[:, TILE:]

    def flat_frames(rows, kernels, low_row):
        high, low = halves(tall_field[rows, :])
        right = jnp.concatenate([high, low, high, jnp.zeros((32, EXT_COLS), BF16)], axis=0)
        tiles = []
        for t in range(2):
            out = jnp.dot(
                flat_gather_weights(kernels[t], low_row, low_row + RIM),
                right[:, t * TILE : t * TILE + COLS],
                preferred_element_type=F32,
            )
            total = out[0:PAD]
            for v in range(1, KSIZE):
                total = total + pltpu.roll(out[PAD * v : PAD * v + PAD], COLS - v, 1)
            tiles.append(total[:, 0:TILE])
        return tiles

    def flat_spread(tiles, kernels, shift):
        outs = []
        for t in range(2):
            high, low = halves(tiles[t])
            right = jnp.concatenate([high, low, high, jnp.zeros((80, TILE), BF16)], axis=0)
            out = jnp.dot(flat_spread_weights(kernels[t], shift), right, preferred_element_type=F32)
            out = jnp.concatenate([out, jnp.zeros((GROUPS, TILE), F32)], axis=1)
            total = out[0:PAD]
            for v in range(1, KSIZE):
                total = total + pltpu.roll(out[PAD * v : PAD * v + PAD], v, 1)
            outs.append(total)
        return outs

    def inner(x, y):
        z = x * y
        z = z[:, 0:TILE] + z[:, TILE:]
        while z.shape[0] > 8:
            half = z.shape[0] // 2
            z = z[0:half] + z[half:]
        return jnp.sum(jnp.sum(z, axis=0, keepdims=True), axis=1, keepdims=True)

    def own_block(source, row):
        shifted[...] = pltpu.roll(source[row : row + EXT_ROWS, :], EXT_COLS - RADIUS, 1)[:, 0:COLS]
        return shifted[pl.ds(RADIUS, ROWS), :]

    load_obs.wait()
    spread(obs_ref[...], spill)
    copies = start_exchange()
    pl.semaphore_wait(barrier, len(partners))
    for copy in copies:
        copy.start()
    for copy in copies:
        copy.wait()
    assemble()
    for t in range(2):
        image[0, :, t * TILE : (t + 1) * TILE] = gather(tall_field, PAD, t)
    frames = side_frames()
    kernels_top = [got_down[36 + t : 37 + t, 0:TILE] * above for t in range(2)]
    kernels_bottom = [got_up[4 + t : 5 + t, 0:TILE] * below for t in range(2)]
    frames_top = flat_frames(slice(0, 32), kernels_top, 6)
    frames_bottom = flat_frames(slice(144, 176), kernels_bottom, 0)
    spread(image[0], field)
    grad[0] = own_block(tall_field, PAD)
    sums = [inner(grad[0], grad[0]), inner(image[0], image[0])]
    to_left, to_right = side_spread(frames)
    field[:, 0:TILE] += to_left
    field[:, 2 * TILE :] += to_right
    kernels_top = [got_down[38 + t : 39 + t, 0:TILE] * above for t in range(2)]
    kernels_bottom = [got_up[6 + t : 7 + t, 0:TILE] * below for t in range(2)]
    for t, out in enumerate(flat_spread(frames_top, kernels_top, 6)):
        field[0:PAD, t * TILE : t * TILE + COLS] += out
    for t, out in enumerate(flat_spread(frames_bottom, kernels_bottom, -RIM)):
        field[ROWS:, t * TILE : t * TILE + COLS] += out
    r, c = iota((EXT_ROWS, EXT_COLS), 0), iota((EXT_ROWS, EXT_COLS), 1)
    inside = (
        (r >= jnp.where(rng == 0, RADIUS, 0))
        & (r < jnp.where(rng == 15, ROWS + RADIUS, EXT_ROWS))
        & (c >= jnp.where(azi == 0, RADIUS, 0))
        & (c < jnp.where(azi == 31, COLS + RADIUS, EXT_COLS))
    )
    field[...] = jnp.where(inside, field[...], 0.0)
    for t in range(2):
        image[1, :, t * TILE : (t + 1) * TILE] = gather(field, 0, t)
    grad[1] = own_block(field, 0)
    store_grad = pltpu.make_async_copy(grad, grad_hbm, load.at[0])
    store_grad.start()
    sums += [inner(grad[1], grad[1]), inner(grad[0], grad[1])]
    sums += [inner(image[1], image[1]), inner(image[0], image[1])]
    store_image = pltpu.make_async_copy(image, image_hbm, load.at[1])
    store_image.start()
    line = lane[0:1]
    moments[0] = sum(jnp.where(line == i, x, 0.0) for i, x in enumerate(sums))
    for phase, got in enumerate((got_a, got_b)):
        for i, o in enumerate(OFFSETS[phase]):
            pltpu.make_async_remote_copy(
                src_ref=moments.at[phase],
                dst_ref=got.at[i],
                send_sem=sum_send.at[phase],
                recv_sem=sum_recv.at[phase],
                device_id=member(o),
                device_id_type=MESH,
            ).start()
        pltpu.make_async_copy(got, got, sum_recv.at[phase]).wait()
        moments[phase + 1] = moments[phase] + jnp.sum(got[...], axis=0)
    total = moments[2]
    gg, qq, ww, gw, pp, qp = (total[:, i : i + 1] for i in range(6))
    alpha = gg / qq
    gamma_1 = (gg - alpha * gw) - alpha * (gw - alpha * ww)
    rise = 1.0 + gamma_1 / gg
    delta_1 = rise * (rise * qq - alpha * qp) - alpha * (rise * qp - alpha * pp)
    alpha_1 = gamma_1 / delta_1
    near = alpha + alpha_1 * rise
    far = alpha * alpha_1
    factors[...] = jnp.where(line == 0, near, far)
    for phase, got in enumerate((got_a, got_b)):
        pltpu.make_async_copy(got, got, sum_send.at[phase]).wait()
    store_grad.wait()
    store_image.wait()


def finish(grad_hbm, image_hbm, obs_hbm, factors_hbm, est_hbm, res_hbm, grad, image, obs, factors, sems):
    ins = ((factors_hbm, factors), (grad_hbm, grad), (image_hbm, image), (obs_hbm, obs))
    loads = [pltpu.make_async_copy(a, b, sems.at[i]) for i, (a, b) in enumerate(ins)]
    for load in loads:
        load.start()
    loads[0].wait()
    loads[1].wait()
    near, far = factors[:, 0:1], factors[:, 1:2]
    grad[0] = near * grad[0] - far * grad[1]
    store_est = pltpu.make_async_copy(grad.at[0], est_hbm, sems.at[4])
    store_est.start()
    loads[2].wait()
    loads[3].wait()
    image[0] = obs[...] - near * image[0] + far * image[1]
    store_res = pltpu.make_async_copy(image.at[0], res_hbm, sems.at[5])
    store_res.start()
    store_est.wait()
    store_res.wait()


def body(observed, psf_tiles):
    pair = jax.ShapeDtypeStruct((2, ROWS, COLS), F32)
    hbm = pl.BlockSpec(memory_space=pltpu.HBM)
    grads, images, factors = pl.pallas_call(
        kernel,
        out_shape=(pair, pair, jax.ShapeDtypeStruct((1, TILE), F32)),
        in_specs=[hbm, hbm],
        out_specs=(hbm, hbm, pl.BlockSpec(memory_space=pltpu.VMEM)),
        scratch_shapes=[
            pltpu.VMEM((ROWS, COLS), F32),
            pltpu.VMEM((1, 2, KSIZE * KSIZE), F32),
            pltpu.VMEM((8, TILE), F32),
            pltpu.VMEM((2, 3 * TILE, WIDE + TILE), BF16),
            pltpu.VMEM((2, 4 * TILE, WIDE), BF16),
            pltpu.VMEM((2, ROWS + 2 * PAD, WIDE + TILE), F32),
            pltpu.VMEM((2, EXT_ROWS, WIDE), F32),
            pltpu.VMEM((EXT_ROWS, EXT_COLS), F32),
            pltpu.VMEM((TALL_ROWS, EXT_COLS), F32),
            pltpu.VMEM((EXT_ROWS, EXT_COLS), F32),
            pltpu.VMEM((2, ROWS, COLS), F32),
            pltpu.VMEM((2, ROWS, COLS), F32),
            pltpu.VMEM((EXT_ROWS, COLS), F32),
            pltpu.VMEM((2, EXT_ROWS + 16, TILE), F32),
            pltpu.VMEM((40, EXT_COLS), F32),
            pltpu.VMEM((32, EXT_COLS), F32),
            pltpu.VMEM((2, EXT_ROWS + 8, TILE), F32),
            pltpu.VMEM((40, EXT_COLS), F32),
            pltpu.VMEM((32, EXT_COLS), F32),
            pltpu.VMEM((2, 40, TILE), F32),
            pltpu.VMEM((2, 32, TILE), F32),
            pltpu.VMEM((208, COLS), F32),
            pltpu.VMEM((160, COLS), F32),
            pltpu.VMEM((3, 1, TILE), F32),
            pltpu.VMEM((len(OFFSETS[0]), 1, TILE), F32),
            pltpu.VMEM((len(OFFSETS[1]), 1, TILE), F32),
            pltpu.SemaphoreType.DMA((8,)),
            pltpu.SemaphoreType.DMA((8,)),
            pltpu.SemaphoreType.DMA((2,)),
            pltpu.SemaphoreType.DMA((2,)),
            pltpu.SemaphoreType.DMA((2,)),
        ],
        compiler_params=pltpu.CompilerParams(
            collective_id=0, has_side_effects=True, vmem_limit_bytes=61 << 20
        ),
    )(observed, psf_tiles)
    block = jax.ShapeDtypeStruct((ROWS, COLS), F32)
    return pl.pallas_call(
        finish,
        out_shape=(block, block),
        in_specs=[pl.BlockSpec(memory_space=pltpu.HBM)] * 4,
        out_specs=(pl.BlockSpec(memory_space=pltpu.HBM),) * 2,
        scratch_shapes=[
            pltpu.VMEM((2, ROWS, COLS), F32),
            pltpu.VMEM((2, ROWS, COLS), F32),
            pltpu.VMEM((ROWS, COLS), F32),
            pltpu.VMEM((1, TILE), F32),
            pltpu.SemaphoreType.DMA((6,)),
        ],
        compiler_params=pltpu.CompilerParams(vmem_limit_bytes=61 << 20),
    )(grads, images, observed, factors)


def solution(mesh):
    return jax.shard_map(
        body,
        mesh=mesh,
        in_specs=(P("rng", "azi"), P("rng", "azi", None)),
        out_specs=(P("rng", "azi"), P("rng", "azi")),
        check_vma=False,
    )
```

```python
import itertools

import jax
import jax.numpy as jnp
from jax import lax
from jax.experimental import pallas as pl
from jax.experimental.pallas import tpu as pltpu
from jax.sharding import PartitionSpec as P

TILE = 128
KSIZE = 11
RADIUS = 5
RIM = 2 * RADIUS
ROWS = 128
COLS = 256
EXT_ROWS = 144
EXT_COLS = 384
TALL_ROWS = 176
PAD = 16
GROUPS = KSIZE * PAD
WIDE = KSIZE * TILE
MESH = pl.DeviceIdType.MESH
F32 = jnp.float32
BF16 = jnp.bfloat16

PARTS = {"x": 4, "y": 4, "z": 16, "c": 2}
PHASES = (("x", "y", "c"), ("z",))
NEIGHBOURS = tuple(
    (dr, da) for dr in (-1, 0, 1) for da in (-1, 0, 1) if (dr, da) != (0, 0)
)


def group_offsets(axes):
    ranges = [range(PARTS[axis]) for axis in axes]
    offsets = [dict(zip(axes, o)) for o in itertools.product(*ranges) if any(o)]
    return sorted(
        offsets,
        key=lambda o: -sum(min(n, PARTS[a] - n) for a, n in o.items() if a != "c"),
    )


OFFSETS = tuple(group_offsets(axes) for axes in PHASES)


def band_group(n):
    return (n * 373) >> 12


def split_rows(x):
    high = x.astype(BF16).astype(F32)
    return high, x - high


def iota(shape, dim):
    return lax.broadcasted_iota(jnp.int32, shape, dim)


def orders(taps):
    a, b = iota((TILE, TILE), 0), iota((TILE, TILE), 1)
    last = KSIZE * KSIZE - 1

    def turned(n):
        return KSIZE * (n - KSIZE * band_group(n)) + band_group(n)

    back = last - b
    wanted = (back, turned(b), jnp.where(back >= 0, turned(jnp.maximum(back, 0)), -1))
    pick = [jnp.where((a == w) & (b <= last), 1.0, 0.0).astype(BF16) for w in wanted]
    first = taps.astype(BF16)
    rest = taps - first.astype(F32)
    second = rest.astype(BF16)
    third = (rest - second.astype(F32)).astype(BF16)
    parts = jnp.concatenate([first, second, third], axis=1)
    out = [taps]
    for p in pick:
        out.append(jnp.dot(parts, jnp.concatenate([p] * 3, axis=0), preferred_element_type=F32))
    row = iota((8, TILE), 0)
    total = out[0]
    for k in range(1, 4):
        total = jnp.where((row >= 2 * k) & (row < 2 * k + 2), pltpu.roll(out[k], 2 * k, 0), total)
    return total


def sloped(line, shift, rows):
    base = pltpu.roll(jnp.broadcast_to(line, (8, TILE)), shift, 1)
    return pltpu.roll(jnp.concatenate([base] * (rows // 8), axis=0), 0, 1, stride=1, stride_axis=0)


def side_gather_weights(left, right):
    i, n = iota((40, TILE), 0), iota((40, TILE), 1)
    j = n - KSIZE * band_group(n)
    halves_ = []
    for kernel_row, start in ((left, 0), (right, 20)):
        band = sloped(kernel_row, TILE - RIM - start, 40)
        c = i - start
        keep = (c >= 0) & (c < 20) & (j < RIM) & (n < 121) & (c - j >= 0) & (c - j < KSIZE)
        halves_.append(jnp.where(keep, band, 0.0))
    high, low = split_rows(jnp.concatenate(halves_, axis=1))
    return jnp.concatenate([high, high, low, jnp.zeros((8, COLS), F32)], axis=0).astype(BF16)


def side_spread_weights(left, right):
    i, n = iota((24, TILE), 0), iota((24, TILE), 1)
    c = n - KSIZE * band_group(n)
    valid = (c < RIM) & (n < 121)
    halves_ = []
    for kernel_row, keep in (
        (left, valid & (i < RIM) & (c <= i)),
        (right, valid & (i >= RIM) & (i < 2 * RIM) & (c >= i - RIM)),
    ):
        band = sloped(kernel_row, TILE - RIM, 24)
        halves_.append(jnp.where(keep, band, 0.0))
    high, low = split_rows(jnp.concatenate(halves_, axis=1))
    return jnp.concatenate([high, high, low, jnp.zeros((TILE - 72, COLS), F32)], axis=0).astype(BF16)


def flat_gather_weights(kernel_row, low_row, high_row):
    lane, row = iota((PAD, TILE), 1), iota((PAD, TILE), 0)
    blocks = []
    for v in range(KSIZE):
        line = jnp.broadcast_to(kernel_row, (PAD, TILE))
        line = pltpu.roll(line, TILE - KSIZE * v, 1) if v else line
        line = jnp.where(lane < KSIZE, line, 0.0)
        blocks.append(pltpu.roll(line, 0, 1, stride=1, stride_axis=0))
    band = jnp.concatenate(blocks, axis=0)
    r = jnp.concatenate([row] * KSIZE, axis=0)
    high, low = split_rows(jnp.where((r >= low_row) & (r < high_row), band, 0.0))
    return (high + pltpu.roll(high, 32, 1) + pltpu.roll(low, 64, 1)).astype(BF16)


def flat_spread_weights(kernel_row, shift):
    lane = iota((PAD, TILE), 1)
    blocks = []
    for v in range(KSIZE):
        line = jnp.broadcast_to(kernel_row, (PAD, TILE))
        line = pltpu.roll(line, (2 * TILE - (KSIZE * KSIZE - KSIZE) + KSIZE * v) % TILE, 1)
        line = pltpu.roll(jnp.where(lane < KSIZE, line, 0.0), shift % TILE, 1)
        line = pltpu.roll(line, 0, 1, stride=1, stride_axis=0)
        blocks.append(jnp.where(lane < PAD, line, 0.0))
    high, low = split_rows(jnp.concatenate(blocks, axis=0))
    return (high + pltpu.roll(high, PAD, 1) + pltpu.roll(low, 2 * PAD, 1)).astype(BF16)


def side_fields(near, far):
    lane = iota(near.shape, 1)
    left = jnp.where(lane >= TILE - RIM, far, jnp.where(lane < RIM, near, 0.0))
    right = jnp.where(lane < 20, far, 0.0)
    x = pltpu.roll(left, RIM, 1) + pltpu.roll(right, 20, 1)
    high, low = split_rows(x)
    return (high + pltpu.roll(low, 40, 1) + pltpu.roll(high, 80, 1)).astype(BF16)


def picked(x, places, width):
    n = iota((TILE, width), 0)
    j = n - KSIZE * band_group(n)
    lane = iota((TILE, width), 1)
    blocks = [
        jnp.where((j < RIM) & (n < 121) & (lane == j + place), 1.0, 0.0).astype(BF16)
        for place in places
    ]
    pick = jnp.concatenate(blocks, axis=0)
    high, low = halves(x)
    return jnp.dot(jnp.concatenate([high, low], axis=1), jnp.concatenate([pick, pick], axis=0), preferred_element_type=F32)


def halves(x):
    high = x.astype(BF16)
    low = (x - high.astype(F32)).astype(BF16)
    return high, low


def kernel(
    obs_hbm,
    psf_hbm,
    grad_hbm,
    image_hbm,
    factors,
    obs_ref,
    psf_ref,
    taps,
    spread_w,
    gather_w,
    wide,
    tall,
    spill,
    tall_field,
    field,
    image,
    grad,
    shifted,
    strips,
    send_side,
    send_up,
    send_down,
    send_up_corner,
    send_down_corner,
    got_side,
    got_up,
    got_down,
    got_up_corner,
    got_down_corner,
    side_out,
    side_back,
    moments,
    got_a,
    got_b,
    halo_send,
    halo_recv,
    sum_send,
    sum_recv,
    load,
):
    load_psf = pltpu.make_async_copy(psf_hbm, psf_ref, load.at[0])
    load_obs = pltpu.make_async_copy(obs_hbm, obs_ref, load.at[1])
    load_psf.start()
    load_obs.start()
    rng = lax.axis_index("rng")
    azi = lax.axis_index("azi")
    place = {
        "x": azi // 8,
        "y": rng // 4,
        "z": (rng % 4) * 4 + (azi // 2) % 4,
        "c": azi % 2,
    }

    def member(offset):
        at = {
            axis: lax.rem(place[axis] + offset[axis], PARTS[axis])
            if axis in offset
            else place[axis]
            for axis in PARTS
        }
        return (at["y"] * 4 + at["z"] // 4, at["x"] * 8 + (at["z"] % 4) * 2 + at["c"])

    def neighbour(dr, da):
        return (lax.rem(rng + dr + 16, 16), lax.rem(azi + da + 32, 32))

    barrier = pltpu.get_barrier_semaphore()
    partners = [neighbour(*d) for d in NEIGHBOURS]
    partners += [member(o) for offsets in OFFSETS for o in offsets]
    for partner in partners:
        pl.semaphore_signal(barrier, inc=1, device_id=partner, device_id_type=MESH)

    lane = lax.broadcasted_iota(jnp.int32, (TILE, TILE), 1)
    row = lax.broadcasted_iota(jnp.int32, (TILE, TILE), 0)

    edge_lane, edge_row = lane[0:PAD], row[0:PAD]

    def bands(line):
        return [
            jnp.concatenate(
                [pltpu.roll(part, 8 * g, 1) if g else part for g in range(TILE // 8)], axis=0
            )
            for part in (
                pltpu.roll(half, 0, 1, stride=1, stride_axis=0) for half in split_rows(line)
            )
        ]

    def taps_at(line, shift, back=0):
        line = pltpu.roll(jnp.broadcast_to(line, (8, TILE)), (2 * TILE - shift) % TILE, 1)
        line = jnp.where(lane[0:8] < KSIZE, line, 0.0)
        return pltpu.roll(line, back % TILE, 1) if back else line

    def build_spread():
        for t in range(2):
            packed = [jnp.zeros((PAD, TILE), F32)] * 2
            for u in range(KSIZE):
                block = slice(u * TILE, (u + 1) * TILE)
                for k, band in enumerate(bands(taps_at(taps[t : t + 1, :], KSIZE * u))):
                    edge = band[TILE - PAD :]
                    below = edge_lane < edge_row + (TILE - PAD)
                    over = jnp.where(below, edge, 0.0)
                    packed[k] += pltpu.roll(over, RIM * u, 1) if u else over
                    main = jnp.concatenate(
                        [band[0 : TILE - PAD], jnp.where(below, 0.0, edge)], axis=0
                    ).astype(BF16)
                    if k == 0:
                        spread_w[t, 0:TILE, block] = main
                        spread_w[t, TILE : 2 * TILE, block] = main
                    else:
                        spread_w[t, 2 * TILE :, block] = main
            blank = jnp.zeros((TILE - PAD, TILE), F32)
            high, low = (jnp.concatenate([blank, p], axis=0).astype(BF16) for p in packed)
            spread_w[t, 0:TILE, WIDE:] = high
            spread_w[t, TILE : 2 * TILE, WIDE:] = high
            spread_w[t, 2 * TILE :, WIDE:] = low

    def build_gather(reverse):
        for t in range(2):
            gather_w[t, 3 * TILE + 3 * PAD :, :] = jnp.zeros((TILE - 3 * PAD, WIDE), BF16)
            for u in range(KSIZE):
                block = slice(u * TILE, (u + 1) * TILE)
                line = taps_at(reverse[t : t + 1, :], KSIZE * (KSIZE - 1 - u), 1 - KSIZE)
                for k, band in enumerate(bands(line)):
                    edge = band[0:PAD]
                    past = edge_lane > edge_row
                    over = jnp.where(past, edge, 0.0).astype(BF16)
                    main = jnp.concatenate(
                        [jnp.where(past, 0.0, edge), band[PAD:]], axis=0
                    ).astype(BF16)
                    if k == 0:
                        gather_w[t, 0:TILE, block] = main
                        gather_w[t, TILE : 2 * TILE, block] = main
                        gather_w[t, 3 * TILE : 3 * TILE + PAD, block] = over
                        gather_w[t, 3 * TILE + PAD : 3 * TILE + 2 * PAD, block] = over
                    else:
                        gather_w[t, 2 * TILE : 3 * TILE, block] = main
                        gather_w[t, 3 * TILE + 2 * PAD : 3 * TILE + 3 * PAD, block] = over

    load_psf.wait()
    taps[...] = jnp.zeros_like(taps)
    taps[0:2, 0 : KSIZE * KSIZE] = psf_ref[0]
    kernels = orders(taps[...])
    build_spread()
    wide[:, 0:PAD, :] = jnp.zeros((2, PAD, WIDE + TILE), F32)
    wide[:, PAD + ROWS :, :] = jnp.zeros((2, PAD, WIDE + TILE), F32)

    def spread(source, out):
        tall_lane = lax.broadcasted_iota(jnp.int32, (EXT_ROWS, TILE), 1)
        over = None
        for t in range(2):
            high, low = halves(source[:, t * TILE : (t + 1) * TILE])
            left = jnp.concatenate([high, low, high], axis=1)
            for n in range(0, WIDE + TILE, 256):
                wide[t, PAD : PAD + ROWS, n : n + 256] = jnp.dot(
                    left, spread_w[t, :, n : n + 256], preferred_element_type=F32
                )
            total = over
            spare = None
            for u in range(KSIZE):
                rows = pl.ds(PAD - u, EXT_ROWS)
                piece = wide[t, rows, u * TILE : (u + 1) * TILE]
                total = piece if total is None else total + piece
                piece = wide[t, rows, WIDE:]
                if u:
                    piece = pltpu.roll(piece, TILE - RIM * u, 1)
                spare = piece if spare is None else spare + piece
            out[:, t * TILE : (t + 1) * TILE] = total
            over = jnp.where(tall_lane < RIM, spare, 0.0)
        out[:, 2 * TILE :] = over

    def gather(source, row, t):
        tall_lane = lax.broadcasted_iota(jnp.int32, (EXT_ROWS, TILE), 1)
        high, low = halves(source[row : row + EXT_ROWS, t * TILE : (t + 1) * TILE])
        edge = source[row : row + EXT_ROWS, (t + 1) * TILE : (t + 2) * TILE]
        edge = jnp.where(tall_lane < RIM, edge, 0.0)
        edge_high = edge.astype(BF16).astype(F32)
        edge_low = edge - edge_high
        edge = edge_high + pltpu.roll(edge_low, PAD, 1) + pltpu.roll(edge_high, 2 * PAD, 1)
        left = jnp.concatenate([high, low, high, edge.astype(BF16)], axis=1)
        total = None
        for n in range(0, WIDE, 256):
            width = min(256, WIDE - n)
            tall[t, :, n : n + width] = jnp.dot(
                left, gather_w[t, :, n : n + width], preferred_element_type=F32
            )
        for u in range(KSIZE):
            piece = tall[t, pl.ds(u, ROWS), u * TILE : (u + 1) * TILE]
            total = piece if total is None else total + piece
        return total

    def pack(strip, rows):
        out = None
        for k in range(strip.shape[0] // rows):
            part = strip[rows * k : rows * k + rows]
            part = jnp.where(lane[0:rows] < 2 * RIM, part, 0.0)
            part = pltpu.roll(part, 2 * RIM * k, 1) if k else part
            out = part if out is None else out + part
        return out

    def unpack(packed, groups):
        parts = []
        for k in range(groups):
            part = pltpu.roll(packed, TILE - 2 * RIM * k, 1) if k else packed
            parts.append(jnp.where(lane[0 : packed.shape[0]] < 2 * RIM, part, 0.0))
        return jnp.concatenate(parts, axis=0)

    def start_exchange():
        side = iota((EXT_ROWS, TILE), 1)
        right = jnp.where(side >= TILE - RIM, spill[:, TILE : 2 * TILE], spill[:, 2 * TILE :])
        strips[0] = spill[:, 0:TILE]
        strips[1] = pltpu.roll(right, RIM, 1)
        for i in range(2):
            send_side[i, 0:24] = pack(strips[i], 24)
            send_side[i, 24:] = kernels
            send_up_corner[i, 0:8] = pack(strips[i, 0:24], 8)
            send_up_corner[i, 8:] = kernels
            send_down_corner[i, 0:8] = pack(strips[i, 118:142], 8)
            send_down_corner[i, 8:] = kernels
        for send, at in ((send_up, 0), (send_down, 118)):
            for t in range(2):
                tile = slice(t * TILE, (t + 1) * TILE)
                send[16 * t : 16 * t + 16] = spill[at : at + 16, tile]
                send[32 + 4 * t : 36 + 4 * t] = spill[at + 16 : at + 20, tile]
            send[40:48] = pack(spill[at : at + 24, 2 * TILE :], 8)
            send[48:] = kernels
        plan = {
            (-1, 1): (send_up_corner.at[1], got_up_corner.at[1]),
            (1, -1): (send_down_corner.at[0], got_down_corner.at[0]),
            (-1, -1): (send_up_corner.at[0], got_up_corner.at[0]),
            (1, 1): (send_down_corner.at[1], got_down_corner.at[1]),
            (-1, 0): (send_up, got_up),
            (1, 0): (send_down, got_down),
            (0, -1): (send_side.at[0], got_side.at[0]),
            (0, 1): (send_side.at[1], got_side.at[1]),
        }
        return [
            pltpu.make_async_remote_copy(
                src_ref=source,
                dst_ref=target,
                send_sem=halo_send.at[i],
                recv_sem=halo_recv.at[i],
                device_id=neighbour(*d),
                device_id_type=MESH,
            )
            for i, (d, (source, target)) in enumerate(plan.items())
        ]

    above = jnp.where(rng > 0, 1.0, 0.0)
    below = jnp.where(rng < 15, 1.0, 0.0)
    left_of = jnp.where(azi > 0, 1.0, 0.0)
    right_of = jnp.where(azi < 31, 1.0, 0.0)

    def assemble():
        first, last = slice(0, TILE), slice(2 * TILE, EXT_COLS)
        tall_field[0:PAD] = jnp.zeros((PAD, EXT_COLS), F32)
        tall_field[PAD : PAD + EXT_ROWS] = spill[...]
        tall_field[PAD + EXT_ROWS :] = jnp.zeros((PAD, EXT_COLS), F32)
        for got, at, flag in ((got_down, 6, above), (got_up, 144, below)):
            for t in range(2):
                tile = slice(t * TILE, (t + 1) * TILE)
                tall_field[at : at + 16, tile] += got[16 * t : 16 * t + 16] * flag
                tall_field[at + 16 : at + 20, tile] += got[32 + 4 * t : 36 + 4 * t] * flag
            tall_field[at : at + 24, last] += unpack(got[40:48], 3) * flag

        def from_left(strip, rows, flag):
            strip = pltpu.roll(strip, TILE - RIM, 1) * flag
            near = iota(strip.shape, 1) < TILE // 2
            tall_field[rows, first] += jnp.where(near, strip, 0.0)
            tall_field[rows, last] += jnp.where(near, 0.0, strip)

        def from_right(strip, rows, flag):
            tall_field[rows, last] += strip * flag

        middle, top, bottom = slice(16, 160), slice(6, 30), slice(144, 168)
        from_right(unpack(got_side[0, 0:24], 6), middle, right_of)
        from_left(unpack(got_side[1, 0:24], 6), middle, left_of)
        from_right(unpack(got_down_corner[0, 0:8], 3), top, above * right_of)
        from_left(unpack(got_down_corner[1, 0:8], 3), top, above * left_of)
        from_right(unpack(got_up_corner[0, 0:8], 3), bottom, below * right_of)
        from_left(unpack(got_up_corner[1, 0:8], 3), bottom, below * left_of)
        r, c = iota((TALL_ROWS, EXT_COLS), 0), iota((TALL_ROWS, EXT_COLS), 1)
        inside = (
            (r >= jnp.where(rng == 0, PAD + RADIUS, 0))
            & (r < jnp.where(rng == 15, PAD + RADIUS + ROWS, TALL_ROWS))
            & (c >= jnp.where(azi == 0, RADIUS, 0))
            & (c < jnp.where(azi == 0, 320, EXT_COLS))
            & ((c < jnp.where(azi == 31, RADIUS + COLS, EXT_COLS)) | (c >= 320))
        )
        tall_field[...] = jnp.where(inside, tall_field[...], 0.0)

    def side_kernels(k):
        return tuple(
            (got[1, at + 1 + k : at + 2 + k] * (flag * left_of), got[0, at + k : at + 1 + k] * (flag * right_of))
            for got, at, flag in ((got_down_corner, 8, above), (got_side, 24, 1.0), (got_up_corner, 8, below))
        )

    def side_frames():
        fields = side_fields(tall_field[:, 0:TILE], tall_field[:, 2 * TILE :])
        parts = ((0, 32, 144, 16), (16, 144, 0, 128), (144, 32, 176, 16))
        group = band_group(iota((1, COLS), 1) & (TILE - 1))
        sums = []
        for (start, count, at, rows), (left, right) in zip(parts, side_kernels(2)):
            side_out[at : at + count] = jnp.dot(
                fields[start : start + count], side_gather_weights(left, right), preferred_element_type=F32
            )
            total = jnp.zeros((rows, COLS), F32)
            for u in range(KSIZE):
                total = jnp.where(group == KSIZE - 1 - u, side_out[at + u : at + u + rows], total)
            sums.append(total)
        frames = picked(jnp.concatenate(sums, axis=0), (0, RIM), TILE)
        r = iota(frames.shape, 0)
        return jnp.where((r >= 6) & (r < 154), frames, 0.0)

    def side_spread(frames):
        high, low = split_rows(frames)
        packed = (high + pltpu.roll(low, 24, 1) + pltpu.roll(high, 48, 1)).astype(BF16)
        for (start, stop), (left, right) in zip(((0, 16), (16, 144), (144, 160)), side_kernels(0)):
            side_back[start:stop] = jnp.dot(
                packed[start:stop], side_spread_weights(left, right), preferred_element_type=F32
            )
        group = band_group(iota((1, COLS), 1) & (TILE - 1))
        total = jnp.zeros((EXT_ROWS, COLS), F32)
        for u in range(KSIZE):
            total = jnp.where(group == u, side_back[PAD - u : PAD - u + EXT_ROWS], total)
        out = picked(total, (0, TILE), COLS)
        return out[:, 0:TILE], out[:, TILE:]

    def flat_frames(rows, kernels, low_row):
        high, low = halves(tall_field[rows, :])
        right = jnp.concatenate([high, low, high, jnp.zeros((32, EXT_COLS), BF16)], axis=0)
        tiles = []
        for t in range(2):
            out = jnp.dot(
                flat_gather_weights(kernels[t], low_row, low_row + RIM),
                right[:, t * TILE : t * TILE + COLS],
                preferred_element_type=F32,
            )
            total = out[0:PAD]
            for v in range(1, KSIZE):
                total = total + pltpu.roll(out[PAD * v : PAD * v + PAD], COLS - v, 1)
            tiles.append(total[:, 0:TILE])
        return tiles

    def flat_spread(tiles, kernels, shift):
        outs = []
        for t in range(2):
            high, low = halves(tiles[t])
            right = jnp.concatenate([high, low, high, jnp.zeros((80, TILE), BF16)], axis=0)
            out = jnp.dot(flat_spread_weights(kernels[t], shift), right, preferred_element_type=F32)
            out = jnp.concatenate([out, jnp.zeros((GROUPS, TILE), F32)], axis=1)
            total = out[0:PAD]
            for v in range(1, KSIZE):
                total = total + pltpu.roll(out[PAD * v : PAD * v + PAD], v, 1)
            outs.append(total)
        return outs

    def inner(x, y):
        z = x * y
        z = z[:, 0:TILE] + z[:, TILE:]
        while z.shape[0] > 8:
            half = z.shape[0] // 2
            z = z[0:half] + z[half:]
        return jnp.sum(jnp.sum(z, axis=0, keepdims=True), axis=1, keepdims=True)

    def own_block(source, row):
        shifted[...] = pltpu.roll(source[row : row + EXT_ROWS, :], EXT_COLS - RADIUS, 1)[:, 0:COLS]
        return shifted[pl.ds(RADIUS, ROWS), :]

    load_obs.wait()
    spread(obs_ref[...], spill)
    copies = start_exchange()
    pl.semaphore_wait(barrier, len(partners))
    for copy in copies:
        copy.start()
    build_gather(kernels[2:4])
    for copy in copies:
        copy.wait()
    assemble()
    for t in range(2):
        image[0, :, t * TILE : (t + 1) * TILE] = gather(tall_field, PAD, t)
    frames = side_frames()
    kernels_top = [got_down[52 + t : 53 + t] * above for t in range(2)]
    kernels_bottom = [got_up[52 + t : 53 + t] * below for t in range(2)]
    frames_top = flat_frames(slice(0, 32), kernels_top, 6)
    frames_bottom = flat_frames(slice(144, 176), kernels_bottom, 0)
    spread(image[0], field)
    grad[0] = own_block(tall_field, PAD)
    sums = [inner(grad[0], grad[0]), inner(image[0], image[0])]
    to_left, to_right = side_spread(frames)
    field[:, 0:TILE] += to_left
    field[:, 2 * TILE :] += to_right
    kernels_top = [got_down[54 + t : 55 + t] * above for t in range(2)]
    kernels_bottom = [got_up[54 + t : 55 + t] * below for t in range(2)]
    for t, out in enumerate(flat_spread(frames_top, kernels_top, 6)):
        field[0:PAD, t * TILE : t * TILE + COLS] += out
    for t, out in enumerate(flat_spread(frames_bottom, kernels_bottom, -RIM)):
        field[ROWS:, t * TILE : t * TILE + COLS] += out
    r, c = iota((EXT_ROWS, EXT_COLS), 0), iota((EXT_ROWS, EXT_COLS), 1)
    inside = (
        (r >= jnp.where(rng == 0, RADIUS, 0))
        & (r < jnp.where(rng == 15, ROWS + RADIUS, EXT_ROWS))
        & (c >= jnp.where(azi == 0, RADIUS, 0))
        & (c < jnp.where(azi == 31, COLS + RADIUS, EXT_COLS))
    )
    field[...] = jnp.where(inside, field[...], 0.0)
    for t in range(2):
        image[1, :, t * TILE : (t + 1) * TILE] = gather(field, 0, t)
    grad[1] = own_block(field, 0)
    store_grad = pltpu.make_async_copy(grad, grad_hbm, load.at[0])
    store_grad.start()
    sums += [inner(grad[1], grad[1]), inner(grad[0], grad[1])]
    sums += [inner(image[1], image[1]), inner(image[0], image[1])]
    store_image = pltpu.make_async_copy(image, image_hbm, load.at[1])
    store_image.start()
    line = lane[0:1]
    moments[0] = sum(jnp.where(line == i, x, 0.0) for i, x in enumerate(sums))
    for phase, got in enumerate((got_a, got_b)):
        for i, o in enumerate(OFFSETS[phase]):
            pltpu.make_async_remote_copy(
                src_ref=moments.at[phase],
                dst_ref=got.at[i],
                send_sem=sum_send.at[phase],
                recv_sem=sum_recv.at[phase],
                device_id=member(o),
                device_id_type=MESH,
            ).start()
        pltpu.make_async_copy(got, got, sum_recv.at[phase]).wait()
        moments[phase + 1] = moments[phase] + jnp.sum(got[...], axis=0)
    total = moments[2]
    gg, qq, ww, gw, pp, qp = (total[:, i : i + 1] for i in range(6))
    alpha = gg / qq
    gamma_1 = (gg - alpha * gw) - alpha * (gw - alpha * ww)
    rise = 1.0 + gamma_1 / gg
    delta_1 = rise * (rise * qq - alpha * qp) - alpha * (rise * qp - alpha * pp)
    alpha_1 = gamma_1 / delta_1
    near = alpha + alpha_1 * rise
    far = alpha * alpha_1
    factors[...] = jnp.where(line == 0, near, far)
    for phase, got in enumerate((got_a, got_b)):
        pltpu.make_async_copy(got, got, sum_send.at[phase]).wait()
    store_grad.wait()
    store_image.wait()


def finish(grad_hbm, image_hbm, obs_hbm, factors_hbm, est_hbm, res_hbm, grad, image, obs, factors, sems):
    ins = ((factors_hbm, factors), (grad_hbm, grad), (image_hbm, image), (obs_hbm, obs))
    loads = [pltpu.make_async_copy(a, b, sems.at[i]) for i, (a, b) in enumerate(ins)]
    for load in loads:
        load.start()
    loads[0].wait()
    loads[1].wait()
    near, far = factors[:, 0:1], factors[:, 1:2]
    grad[0] = near * grad[0] - far * grad[1]
    store_est = pltpu.make_async_copy(grad.at[0], est_hbm, sems.at[4])
    store_est.start()
    loads[2].wait()
    loads[3].wait()
    image[0] = obs[...] - near * image[0] + far * image[1]
    store_res = pltpu.make_async_copy(image.at[0], res_hbm, sems.at[5])
    store_res.start()
    store_est.wait()
    store_res.wait()


def body(observed, psf_tiles):
    pair = jax.ShapeDtypeStruct((2, ROWS, COLS), F32)
    hbm = pl.BlockSpec(memory_space=pltpu.HBM)
    grads, images, factors = pl.pallas_call(
        kernel,
        out_shape=(pair, pair, jax.ShapeDtypeStruct((1, TILE), F32)),
        in_specs=[hbm, hbm],
        out_specs=(hbm, hbm, pl.BlockSpec(memory_space=pltpu.VMEM)),
        scratch_shapes=[
            pltpu.VMEM((ROWS, COLS), F32),
            pltpu.VMEM((1, 2, KSIZE * KSIZE), F32),
            pltpu.VMEM((8, TILE), F32),
            pltpu.VMEM((2, 3 * TILE, WIDE + TILE), BF16),
            pltpu.VMEM((2, 4 * TILE, WIDE), BF16),
            pltpu.VMEM((2, ROWS + 2 * PAD, WIDE + TILE), F32),
            pltpu.VMEM((2, EXT_ROWS, WIDE), F32),
            pltpu.VMEM((EXT_ROWS, EXT_COLS), F32),
            pltpu.VMEM((TALL_ROWS, EXT_COLS), F32),
            pltpu.VMEM((EXT_ROWS, EXT_COLS), F32),
            pltpu.VMEM((2, ROWS, COLS), F32),
            pltpu.VMEM((2, ROWS, COLS), F32),
            pltpu.VMEM((EXT_ROWS, COLS), F32),
            pltpu.VMEM((2, EXT_ROWS, TILE), F32),
            pltpu.VMEM((2, 32, TILE), F32),
            pltpu.VMEM((56, TILE), F32),
            pltpu.VMEM((56, TILE), F32),
            pltpu.VMEM((2, 16, TILE), F32),
            pltpu.VMEM((2, 16, TILE), F32),
            pltpu.VMEM((2, 32, TILE), F32),
            pltpu.VMEM((56, TILE), F32),
            pltpu.VMEM((56, TILE), F32),
            pltpu.VMEM((2, 16, TILE), F32),
            pltpu.VMEM((2, 16, TILE), F32),
            pltpu.VMEM((208, COLS), F32),
            pltpu.VMEM((160, COLS), F32),
            pltpu.VMEM((3, 1, TILE), F32),
            pltpu.VMEM((len(OFFSETS[0]), 1, TILE), F32),
            pltpu.VMEM((len(OFFSETS[1]), 1, TILE), F32),
            pltpu.SemaphoreType.DMA((8,)),
            pltpu.SemaphoreType.DMA((8,)),
            pltpu.SemaphoreType.DMA((2,)),
            pltpu.SemaphoreType.DMA((2,)),
            pltpu.SemaphoreType.DMA((2,)),
        ],
        compiler_params=pltpu.CompilerParams(
            collective_id=0, has_side_effects=True, vmem_limit_bytes=61 << 20
        ),
    )(observed, psf_tiles)
    block = jax.ShapeDtypeStruct((ROWS, COLS), F32)
    return pl.pallas_call(
        finish,
        out_shape=(block, block),
        in_specs=[pl.BlockSpec(memory_space=pltpu.HBM)] * 4,
        out_specs=(pl.BlockSpec(memory_space=pltpu.HBM),) * 2,
        scratch_shapes=[
            pltpu.VMEM((2, ROWS, COLS), F32),
            pltpu.VMEM((2, ROWS, COLS), F32),
            pltpu.VMEM((ROWS, COLS), F32),
            pltpu.VMEM((1, TILE), F32),
            pltpu.SemaphoreType.DMA((6,)),
        ],
        compiler_params=pltpu.CompilerParams(vmem_limit_bytes=61 << 20),
    )(grads, images, observed, factors)


def solution(mesh):
    return jax.shard_map(
        body,
        mesh=mesh,
        in_specs=(P("rng", "azi"), P("rng", "azi", None)),
        out_specs=(P("rng", "azi"), P("rng", "azi")),
        check_vma=False,
    )
```

```python
import itertools

import jax
import jax.numpy as jnp
from jax import lax
from jax.experimental import pallas as pl
from jax.experimental.pallas import tpu as pltpu
from jax.sharding import PartitionSpec as P

TILE = 128
KSIZE = 11
RADIUS = 5
RIM = 2 * RADIUS
ROWS = 128
COLS = 256
EXT_ROWS = 144
EXT_COLS = 384
TALL_ROWS = 176
PAD = 16
GROUPS = KSIZE * PAD
WIDE = KSIZE * TILE
MESH = pl.DeviceIdType.MESH
F32 = jnp.float32
BF16 = jnp.bfloat16

PARTS = {"x": 4, "y": 4, "z": 16, "c": 2}
PHASES = (("x", "y", "c"), ("z",))
NEIGHBOURS = tuple(
    (dr, da) for dr in (-1, 0, 1) for da in (-1, 0, 1) if (dr, da) != (0, 0)
)


def group_offsets(axes):
    ranges = [range(PARTS[axis]) for axis in axes]
    offsets = [dict(zip(axes, o)) for o in itertools.product(*ranges) if any(o)]
    return sorted(
        offsets,
        key=lambda o: -sum(min(n, PARTS[a] - n) for a, n in o.items() if a != "c"),
    )


OFFSETS = tuple(group_offsets(axes) for axes in PHASES)


def band_group(n):
    return (n * 373) >> 12


def split_rows(x):
    high = x.astype(BF16).astype(F32)
    return high, x - high


def iota(shape, dim):
    return lax.broadcasted_iota(jnp.int32, shape, dim)


def orders(taps):
    a, b = iota((TILE, TILE), 0), iota((TILE, TILE), 1)
    last = KSIZE * KSIZE - 1

    def turned(n):
        return KSIZE * (n - KSIZE * band_group(n)) + band_group(n)

    back = last - b
    wanted = (back, turned(b), jnp.where(back >= 0, turned(jnp.maximum(back, 0)), -1))
    pick = [jnp.where((a == w) & (b <= last), 1.0, 0.0).astype(BF16) for w in wanted]
    first = taps.astype(BF16)
    rest = taps - first.astype(F32)
    second = rest.astype(BF16)
    third = (rest - second.astype(F32)).astype(BF16)
    parts = jnp.concatenate([first, second, third], axis=1)
    out = [taps]
    for p in pick:
        out.append(jnp.dot(parts, jnp.concatenate([p] * 3, axis=0), preferred_element_type=F32))
    row = iota((8, TILE), 0)
    total = out[0]
    for k in range(1, 4):
        total = jnp.where((row >= 2 * k) & (row < 2 * k + 2), pltpu.roll(out[k], 2 * k, 0), total)
    return total


def sloped(line, shift, rows):
    base = pltpu.roll(jnp.broadcast_to(line, (8, TILE)), shift, 1)
    return pltpu.roll(jnp.concatenate([base] * (rows // 8), axis=0), 0, 1, stride=1, stride_axis=0)


def side_gather_weights(left, right):
    i, n = iota((40, TILE), 0), iota((40, TILE), 1)
    j = n - KSIZE * band_group(n)
    halves_ = []
    for kernel_row, start in ((left, 0), (right, 20)):
        band = sloped(kernel_row, TILE - RIM - start, 40)
        c = i - start
        keep = (c >= 0) & (c < 20) & (j < RIM) & (n < 121) & (c - j >= 0) & (c - j < KSIZE)
        halves_.append(jnp.where(keep, band, 0.0))
    high, low = split_rows(jnp.concatenate(halves_, axis=1))
    return jnp.concatenate([high, high, low, jnp.zeros((8, COLS), F32)], axis=0).astype(BF16)


def side_spread_weights(left, right):
    i, n = iota((24, TILE), 0), iota((24, TILE), 1)
    c = n - KSIZE * band_group(n)
    valid = (c < RIM) & (n < 121)
    halves_ = []
    for kernel_row, keep in (
        (left, valid & (i < RIM) & (c <= i)),
        (right, valid & (i >= RIM) & (i < 2 * RIM) & (c >= i - RIM)),
    ):
        band = sloped(kernel_row, TILE - RIM, 24)
        halves_.append(jnp.where(keep, band, 0.0))
    high, low = split_rows(jnp.concatenate(halves_, axis=1))
    return jnp.concatenate([high, high, low, jnp.zeros((TILE - 72, COLS), F32)], axis=0).astype(BF16)


def flat_gather_weights(kernel_row, low_row, high_row):
    lane, row = iota((PAD, TILE), 1), iota((PAD, TILE), 0)
    blocks = []
    for v in range(KSIZE):
        line = jnp.broadcast_to(kernel_row, (PAD, TILE))
        line = pltpu.roll(line, TILE - KSIZE * v, 1) if v else line
        line = jnp.where(lane < KSIZE, line, 0.0)
        blocks.append(pltpu.roll(line, 0, 1, stride=1, stride_axis=0))
    band = jnp.concatenate(blocks, axis=0)
    r = jnp.concatenate([row] * KSIZE, axis=0)
    high, low = split_rows(jnp.where((r >= low_row) & (r < high_row), band, 0.0))
    return (high + pltpu.roll(high, 32, 1) + pltpu.roll(low, 64, 1)).astype(BF16)


def flat_spread_weights(kernel_row, shift):
    lane = iota((PAD, TILE), 1)
    blocks = []
    for v in range(KSIZE):
        line = jnp.broadcast_to(kernel_row, (PAD, TILE))
        line = pltpu.roll(line, (2 * TILE - (KSIZE * KSIZE - KSIZE) + KSIZE * v) % TILE, 1)
        line = pltpu.roll(jnp.where(lane < KSIZE, line, 0.0), shift % TILE, 1)
        line = pltpu.roll(line, 0, 1, stride=1, stride_axis=0)
        blocks.append(jnp.where(lane < PAD, line, 0.0))
    high, low = split_rows(jnp.concatenate(blocks, axis=0))
    return (high + pltpu.roll(high, PAD, 1) + pltpu.roll(low, 2 * PAD, 1)).astype(BF16)


def side_fields(near, far):
    lane = iota(near.shape, 1)
    left = jnp.where(lane >= TILE - RIM, far, jnp.where(lane < RIM, near, 0.0))
    right = jnp.where(lane < 20, far, 0.0)
    x = pltpu.roll(left, RIM, 1) + pltpu.roll(right, 20, 1)
    high, low = split_rows(x)
    return (high + pltpu.roll(low, 40, 1) + pltpu.roll(high, 80, 1)).astype(BF16)


def picked(x, places, width):
    n = iota((TILE, width), 0)
    j = n - KSIZE * band_group(n)
    lane = iota((TILE, width), 1)
    blocks = [
        jnp.where((j < RIM) & (n < 121) & (lane == j + place), 1.0, 0.0).astype(BF16)
        for place in places
    ]
    pick = jnp.concatenate(blocks, axis=0)
    high, low = halves(x)
    return jnp.dot(jnp.concatenate([high, low], axis=1), jnp.concatenate([pick, pick], axis=0), preferred_element_type=F32)


def halves(x):
    high = x.astype(BF16)
    low = (x - high.astype(F32)).astype(BF16)
    return high, low


def kernel(
    obs_hbm,
    psf_hbm,
    grad_hbm,
    image_hbm,
    factors,
    obs_ref,
    psf_ref,
    taps,
    spread_w,
    gather_w,
    wide,
    tall,
    spill,
    tall_field,
    field,
    image,
    grad,
    shifted,
    strips,
    send_side,
    send_up,
    send_down,
    send_up_corner,
    send_down_corner,
    got_side,
    got_up,
    got_down,
    got_up_corner,
    got_down_corner,
    side_out,
    side_back,
    moments,
    got_a,
    got_b,
    halo_send,
    halo_recv,
    sum_send,
    sum_recv,
    load,
):
    load_psf = pltpu.make_async_copy(psf_hbm, psf_ref, load.at[0])
    load_obs = pltpu.make_async_copy(obs_hbm, obs_ref, load.at[1])
    load_psf.start()
    load_obs.start()
    rng = lax.axis_index("rng")
    azi = lax.axis_index("azi")
    place = {
        "x": azi // 8,
        "y": rng // 4,
        "z": (rng % 4) * 4 + (azi // 2) % 4,
        "c": azi % 2,
    }

    def member(offset):
        at = {
            axis: lax.rem(place[axis] + offset[axis], PARTS[axis])
            if axis in offset
            else place[axis]
            for axis in PARTS
        }
        return (at["y"] * 4 + at["z"] // 4, at["x"] * 8 + (at["z"] % 4) * 2 + at["c"])

    def neighbour(dr, da):
        return (lax.rem(rng + dr + 16, 16), lax.rem(azi + da + 32, 32))

    barrier = pltpu.get_barrier_semaphore()
    partners = [neighbour(*d) for d in NEIGHBOURS]
    partners += [member(o) for offsets in OFFSETS for o in offsets]
    for partner in partners:
        pl.semaphore_signal(barrier, inc=1, device_id=partner, device_id_type=MESH)

    lane = lax.broadcasted_iota(jnp.int32, (TILE, TILE), 1)
    row = lax.broadcasted_iota(jnp.int32, (TILE, TILE), 0)

    edge_lane, edge_row = lane[0:PAD], row[0:PAD]

    def band(line, shift, back):
        line = pltpu.roll(jnp.broadcast_to(line, (8, TILE)), lax.rem(2 * TILE - shift, TILE), 1)
        line = jnp.where(lane[0:8] < KSIZE, line, 0.0)
        line = pltpu.roll(line, back, 1) if back else line
        line = pltpu.roll(line, 0, 1, stride=1, stride_axis=0)
        rows = [pltpu.roll(line, 8 * g, 1) if g else line for g in range(TILE // 8)]
        return jnp.concatenate(rows, axis=0)

    def build_spread():
        def one(u, packed):
            block = pl.ds(pl.multiple_of(u * TILE, TILE), TILE)
            out = []
            for t in range(2):
                rows = band(taps[t : t + 1, :], KSIZE * u, 0)
                edge = rows[TILE - PAD :]
                below = edge_lane < edge_row + (TILE - PAD)
                over = jnp.where(below, edge, 0.0)
                out.append(packed[t] + pltpu.roll(over, RIM * u, 1))
                main = jnp.concatenate([rows[0 : TILE - PAD], jnp.where(below, 0.0, edge)], axis=0)
                high, low = halves(main)
                spread_w[t, 0:TILE, block] = high
                spread_w[t, TILE : 2 * TILE, block] = high
                spread_w[t, 2 * TILE :, block] = low
            return tuple(out)

        packed = lax.fori_loop(0, KSIZE, one, (jnp.zeros((PAD, TILE), F32),) * 2)
        blank = jnp.zeros((TILE - PAD, TILE), BF16)
        for t in range(2):
            high, low = (jnp.concatenate([blank, p], axis=0) for p in halves(packed[t]))
            spread_w[t, 0:TILE, WIDE:] = high
            spread_w[t, TILE : 2 * TILE, WIDE:] = high
            spread_w[t, 2 * TILE :, WIDE:] = low

    def build_gather():
        gather_w[:, 3 * TILE + 3 * PAD :, :] = jnp.zeros((2, TILE - 3 * PAD, WIDE), BF16)

        def one(u, carry):
            block = pl.ds(pl.multiple_of(u * TILE, TILE), TILE)
            for t in range(2):
                rows = band(taps[2 + t : 3 + t, :], KSIZE * (KSIZE - 1) - KSIZE * u, TILE - RIM)
                edge = rows[0:PAD]
                past = edge_lane > edge_row
                high, low = halves(jnp.where(past, edge, 0.0))
                gather_w[t, 3 * TILE : 3 * TILE + PAD, block] = high
                gather_w[t, 3 * TILE + PAD : 3 * TILE + 2 * PAD, block] = high
                gather_w[t, 3 * TILE + 2 * PAD : 3 * TILE + 3 * PAD, block] = low
                main = jnp.concatenate([jnp.where(past, 0.0, edge), rows[PAD:]], axis=0)
                high, low = halves(main)
                gather_w[t, 0:TILE, block] = high
                gather_w[t, TILE : 2 * TILE, block] = high
                gather_w[t, 2 * TILE : 3 * TILE, block] = low
            return carry

        lax.fori_loop(0, KSIZE, one, 0)

    load_psf.wait()
    taps[...] = jnp.zeros_like(taps)
    taps[0:2, 0 : KSIZE * KSIZE] = psf_ref[0]
    kernels = orders(taps[...])
    taps[...] = kernels
    build_spread()
    wide[:, 0:PAD, :] = jnp.zeros((2, PAD, WIDE + TILE), F32)
    wide[:, PAD + ROWS :, :] = jnp.zeros((2, PAD, WIDE + TILE), F32)

    def spread(source, out):
        tall_lane = lax.broadcasted_iota(jnp.int32, (EXT_ROWS, TILE), 1)
        over = None
        for t in range(2):
            high, low = halves(source[:, t * TILE : (t + 1) * TILE])
            left = jnp.concatenate([high, low, high], axis=1)
            for n in range(0, WIDE + TILE, 256):
                wide[t, PAD : PAD + ROWS, n : n + 256] = jnp.dot(
                    left, spread_w[t, :, n : n + 256], preferred_element_type=F32
                )
            total = over
            spare = None
            for u in range(KSIZE):
                rows = pl.ds(PAD - u, EXT_ROWS)
                piece = wide[t, rows, u * TILE : (u + 1) * TILE]
                total = piece if total is None else total + piece
                piece = wide[t, rows, WIDE:]
                if u:
                    piece = pltpu.roll(piece, TILE - RIM * u, 1)
                spare = piece if spare is None else spare + piece
            out[:, t * TILE : (t + 1) * TILE] = total
            over = jnp.where(tall_lane < RIM, spare, 0.0)
        out[:, 2 * TILE :] = over

    def gather(source, row, t):
        tall_lane = lax.broadcasted_iota(jnp.int32, (EXT_ROWS, TILE), 1)
        high, low = halves(source[row : row + EXT_ROWS, t * TILE : (t + 1) * TILE])
        edge = source[row : row + EXT_ROWS, (t + 1) * TILE : (t + 2) * TILE]
        edge = jnp.where(tall_lane < RIM, edge, 0.0)
        edge_high = edge.astype(BF16).astype(F32)
        edge_low = edge - edge_high
        edge = edge_high + pltpu.roll(edge_low, PAD, 1) + pltpu.roll(edge_high, 2 * PAD, 1)
        left = jnp.concatenate([high, low, high, edge.astype(BF16)], axis=1)
        total = None
        for n in range(0, WIDE, 256):
            width = min(256, WIDE - n)
            tall[t, :, n : n + width] = jnp.dot(
                left, gather_w[t, :, n : n + width], preferred_element_type=F32
            )
        for u in range(KSIZE):
            piece = tall[t, pl.ds(u, ROWS), u * TILE : (u + 1) * TILE]
            total = piece if total is None else total + piece
        return total

    def pack(strip, rows):
        out = None
        for k in range(strip.shape[0] // rows):
            part = strip[rows * k : rows * k + rows]
            part = jnp.where(lane[0:rows] < 2 * RIM, part, 0.0)
            part = pltpu.roll(part, 2 * RIM * k, 1) if k else part
            out = part if out is None else out + part
        return out

    def unpack(packed, groups):
        parts = []
        for k in range(groups):
            part = pltpu.roll(packed, TILE - 2 * RIM * k, 1) if k else packed
            parts.append(jnp.where(lane[0 : packed.shape[0]] < 2 * RIM, part, 0.0))
        return jnp.concatenate(parts, axis=0)

    def start_exchange():
        side = iota((EXT_ROWS, TILE), 1)
        right = jnp.where(side >= TILE - RIM, spill[:, TILE : 2 * TILE], spill[:, 2 * TILE :])
        strips[0] = spill[:, 0:TILE]
        strips[1] = pltpu.roll(right, RIM, 1)
        for i in range(2):
            send_side[i, 0:24] = pack(strips[i], 24)
            send_side[i, 24:] = kernels
            send_up_corner[i, 0:8] = pack(strips[i, 0:24], 8)
            send_up_corner[i, 8:] = kernels
            send_down_corner[i, 0:8] = pack(strips[i, 118:142], 8)
            send_down_corner[i, 8:] = kernels
        for send, at in ((send_up, 0), (send_down, 118)):
            for t in range(2):
                tile = slice(t * TILE, (t + 1) * TILE)
                send[16 * t : 16 * t + 16] = spill[at : at + 16, tile]
                send[32 + 4 * t : 36 + 4 * t] = spill[at + 16 : at + 20, tile]
            send[40:48] = pack(spill[at : at + 24, 2 * TILE :], 8)
            send[48:] = kernels
        plan = {
            (-1, 1): (send_up_corner.at[1], got_up_corner.at[1]),
            (1, -1): (send_down_corner.at[0], got_down_corner.at[0]),
            (-1, -1): (send_up_corner.at[0], got_up_corner.at[0]),
            (1, 1): (send_down_corner.at[1], got_down_corner.at[1]),
            (-1, 0): (send_up, got_up),
            (1, 0): (send_down, got_down),
            (0, -1): (send_side.at[0], got_side.at[0]),
            (0, 1): (send_side.at[1], got_side.at[1]),
        }
        return [
            pltpu.make_async_remote_copy(
                src_ref=source,
                dst_ref=target,
                send_sem=halo_send.at[i],
                recv_sem=halo_recv.at[i],
                device_id=neighbour(*d),
                device_id_type=MESH,
            )
            for i, (d, (source, target)) in enumerate(plan.items())
        ]

    above = jnp.where(rng > 0, 1.0, 0.0)
    below = jnp.where(rng < 15, 1.0, 0.0)
    left_of = jnp.where(azi > 0, 1.0, 0.0)
    right_of = jnp.where(azi < 31, 1.0, 0.0)

    def assemble():
        first, last = slice(0, TILE), slice(2 * TILE, EXT_COLS)
        tall_field[0:PAD] = jnp.zeros((PAD, EXT_COLS), F32)
        tall_field[PAD : PAD + EXT_ROWS] = spill[...]
        tall_field[PAD + EXT_ROWS :] = jnp.zeros((PAD, EXT_COLS), F32)
        for got, at, flag in ((got_down, 6, above), (got_up, 144, below)):
            for t in range(2):
                tile = slice(t * TILE, (t + 1) * TILE)
                tall_field[at : at + 16, tile] += got[16 * t : 16 * t + 16] * flag
                tall_field[at + 16 : at + 20, tile] += got[32 + 4 * t : 36 + 4 * t] * flag
            tall_field[at : at + 24, last] += unpack(got[40:48], 3) * flag

        def from_left(strip, rows, flag):
            strip = pltpu.roll(strip, TILE - RIM, 1) * flag
            near = iota(strip.shape, 1) < TILE // 2
            tall_field[rows, first] += jnp.where(near, strip, 0.0)
            tall_field[rows, last] += jnp.where(near, 0.0, strip)

        def from_right(strip, rows, flag):
            tall_field[rows, last] += strip * flag

        middle, top, bottom = slice(16, 160), slice(6, 30), slice(144, 168)
        from_right(unpack(got_side[0, 0:24], 6), middle, right_of)
        from_left(unpack(got_side[1, 0:24], 6), middle, left_of)
        from_right(unpack(got_down_corner[0, 0:8], 3), top, above * right_of)
        from_left(unpack(got_down_corner[1, 0:8], 3), top, above * left_of)
        from_right(unpack(got_up_corner[0, 0:8], 3), bottom, below * right_of)
        from_left(unpack(got_up_corner[1, 0:8], 3), bottom, below * left_of)
        r, c = iota((TALL_ROWS, EXT_COLS), 0), iota((TALL_ROWS, EXT_COLS), 1)
        inside = (
            (r >= jnp.where(rng == 0, PAD + RADIUS, 0))
            & (r < jnp.where(rng == 15, PAD + RADIUS + ROWS, TALL_ROWS))
            & (c >= jnp.where(azi == 0, RADIUS, 0))
            & (c < jnp.where(azi == 0, 320, EXT_COLS))
            & ((c < jnp.where(azi == 31, RADIUS + COLS, EXT_COLS)) | (c >= 320))
        )
        tall_field[...] = jnp.where(inside, tall_field[...], 0.0)

    def side_kernels(k):
        return tuple(
            (got[1, at + 1 + k : at + 2 + k] * (flag * left_of), got[0, at + k : at + 1 + k] * (flag * right_of))
            for got, at, flag in ((got_down_corner, 8, above), (got_side, 24, 1.0), (got_up_corner, 8, below))
        )

    def side_frames():
        fields = side_fields(tall_field[:, 0:TILE], tall_field[:, 2 * TILE :])
        parts = ((0, 32, 144, 16), (16, 144, 0, 128), (144, 32, 176, 16))
        group = band_group(iota((1, COLS), 1) & (TILE - 1))
        sums = []
        for (start, count, at, rows), (left, right) in zip(parts, side_kernels(2)):
            side_out[at : at + count] = jnp.dot(
                fields[start : start + count], side_gather_weights(left, right), preferred_element_type=F32
            )
            total = jnp.zeros((rows, COLS), F32)
            for u in range(KSIZE):
                total = jnp.where(group == KSIZE - 1 - u, side_out[at + u : at + u + rows], total)
            sums.append(total)
        frames = picked(jnp.concatenate(sums, axis=0), (0, RIM), TILE)
        r = iota(frames.shape, 0)
        return jnp.where((r >= 6) & (r < 154), frames, 0.0)

    def side_spread(frames):
        high, low = split_rows(frames)
        packed = (high + pltpu.roll(low, 24, 1) + pltpu.roll(high, 48, 1)).astype(BF16)
        for (start, stop), (left, right) in zip(((0, 16), (16, 144), (144, 160)), side_kernels(0)):
            side_back[start:stop] = jnp.dot(
                packed[start:stop], side_spread_weights(left, right), preferred_element_type=F32
            )
        group = band_group(iota((1, COLS), 1) & (TILE - 1))
        total = jnp.zeros((EXT_ROWS, COLS), F32)
        for u in range(KSIZE):
            total = jnp.where(group == u, side_back[PAD - u : PAD - u + EXT_ROWS], total)
        out = picked(total, (0, TILE), COLS)
        return out[:, 0:TILE], out[:, TILE:]

    def flat_frames(rows, kernels, low_row):
        high, low = halves(tall_field[rows, :])
        right = jnp.concatenate([high, low, high, jnp.zeros((32, EXT_COLS), BF16)], axis=0)
        tiles = []
        for t in range(2):
            out = jnp.dot(
                flat_gather_weights(kernels[t], low_row, low_row + RIM),
                right[:, t * TILE : t * TILE + COLS],
                preferred_element_type=F32,
            )
            total = out[0:PAD]
            for v in range(1, KSIZE):
                total = total + pltpu.roll(out[PAD * v : PAD * v + PAD], COLS - v, 1)
            tiles.append(total[:, 0:TILE])
        return tiles

    def flat_spread(tiles, kernels, shift):
        outs = []
        for t in range(2):
            high, low = halves(tiles[t])
            right = jnp.concatenate([high, low, high, jnp.zeros((80, TILE), BF16)], axis=0)
            out = jnp.dot(flat_spread_weights(kernels[t], shift), right, preferred_element_type=F32)
            out = jnp.concatenate([out, jnp.zeros((GROUPS, TILE), F32)], axis=1)
            total = out[0:PAD]
            for v in range(1, KSIZE):
                total = total + pltpu.roll(out[PAD * v : PAD * v + PAD], v, 1)
            outs.append(total)
        return outs

    def inner(x, y):
        z = x * y
        z = z[:, 0:TILE] + z[:, TILE:]
        while z.shape[0] > 8:
            half = z.shape[0] // 2
            z = z[0:half] + z[half:]
        return jnp.sum(jnp.sum(z, axis=0, keepdims=True), axis=1, keepdims=True)

    def own_block(source, row):
        shifted[...] = pltpu.roll(source[row : row + EXT_ROWS, :], EXT_COLS - RADIUS, 1)[:, 0:COLS]
        return shifted[pl.ds(RADIUS, ROWS), :]

    load_obs.wait()
    spread(obs_ref[...], spill)
    copies = start_exchange()
    pl.semaphore_wait(barrier, len(partners))
    for copy in copies:
        copy.start()
    build_gather()
    for copy in copies:
        copy.wait()
    assemble()
    for t in range(2):
        image[0, :, t * TILE : (t + 1) * TILE] = gather(tall_field, PAD, t)
    frames = side_frames()
    kernels_top = [got_down[52 + t : 53 + t] * above for t in range(2)]
    kernels_bottom = [got_up[52 + t : 53 + t] * below for t in range(2)]
    frames_top = flat_frames(slice(0, 32), kernels_top, 6)
    frames_bottom = flat_frames(slice(144, 176), kernels_bottom, 0)
    spread(image[0], field)
    grad[0] = own_block(tall_field, PAD)
    sums = [inner(grad[0], grad[0]), inner(image[0], image[0])]
    to_left, to_right = side_spread(frames)
    field[:, 0:TILE] += to_left
    field[:, 2 * TILE :] += to_right
    kernels_top = [got_down[54 + t : 55 + t] * above for t in range(2)]
    kernels_bottom = [got_up[54 + t : 55 + t] * below for t in range(2)]
    for t, out in enumerate(flat_spread(frames_top, kernels_top, 6)):
        field[0:PAD, t * TILE : t * TILE + COLS] += out
    for t, out in enumerate(flat_spread(frames_bottom, kernels_bottom, -RIM)):
        field[ROWS:, t * TILE : t * TILE + COLS] += out
    r, c = iota((EXT_ROWS, EXT_COLS), 0), iota((EXT_ROWS, EXT_COLS), 1)
    inside = (
        (r >= jnp.where(rng == 0, RADIUS, 0))
        & (r < jnp.where(rng == 15, ROWS + RADIUS, EXT_ROWS))
        & (c >= jnp.where(azi == 0, RADIUS, 0))
        & (c < jnp.where(azi == 31, COLS + RADIUS, EXT_COLS))
    )
    field[...] = jnp.where(inside, field[...], 0.0)
    for t in range(2):
        image[1, :, t * TILE : (t + 1) * TILE] = gather(field, 0, t)
    grad[1] = own_block(field, 0)
    store_grad = pltpu.make_async_copy(grad, grad_hbm, load.at[0])
    store_grad.start()
    sums += [inner(grad[1], grad[1]), inner(grad[0], grad[1])]
    sums += [inner(image[1], image[1]), inner(image[0], image[1])]
    store_image = pltpu.make_async_copy(image, image_hbm, load.at[1])
    store_image.start()
    line = lane[0:1]
    moments[0] = sum(jnp.where(line == i, x, 0.0) for i, x in enumerate(sums))
    for phase, got in enumerate((got_a, got_b)):
        for i, o in enumerate(OFFSETS[phase]):
            pltpu.make_async_remote_copy(
                src_ref=moments.at[phase],
                dst_ref=got.at[i],
                send_sem=sum_send.at[phase],
                recv_sem=sum_recv.at[phase],
                device_id=member(o),
                device_id_type=MESH,
            ).start()
        pltpu.make_async_copy(got, got, sum_recv.at[phase]).wait()
        moments[phase + 1] = moments[phase] + jnp.sum(got[...], axis=0)
    total = moments[2]
    gg, qq, ww, gw, pp, qp = (total[:, i : i + 1] for i in range(6))
    alpha = gg / qq
    gamma_1 = (gg - alpha * gw) - alpha * (gw - alpha * ww)
    rise = 1.0 + gamma_1 / gg
    delta_1 = rise * (rise * qq - alpha * qp) - alpha * (rise * qp - alpha * pp)
    alpha_1 = gamma_1 / delta_1
    near = alpha + alpha_1 * rise
    far = alpha * alpha_1
    factors[...] = jnp.where(line == 0, near, far)
    for phase, got in enumerate((got_a, got_b)):
        pltpu.make_async_copy(got, got, sum_send.at[phase]).wait()
    store_grad.wait()
    store_image.wait()


def finish(grad_hbm, image_hbm, obs_hbm, factors_hbm, est_hbm, res_hbm, grad, image, obs, factors, sems):
    ins = ((factors_hbm, factors), (grad_hbm, grad), (image_hbm, image), (obs_hbm, obs))
    loads = [pltpu.make_async_copy(a, b, sems.at[i]) for i, (a, b) in enumerate(ins)]
    for load in loads:
        load.start()
    loads[0].wait()
    loads[1].wait()
    near, far = factors[:, 0:1], factors[:, 1:2]
    grad[0] = near * grad[0] - far * grad[1]
    store_est = pltpu.make_async_copy(grad.at[0], est_hbm, sems.at[4])
    store_est.start()
    loads[2].wait()
    loads[3].wait()
    image[0] = obs[...] - near * image[0] + far * image[1]
    store_res = pltpu.make_async_copy(image.at[0], res_hbm, sems.at[5])
    store_res.start()
    store_est.wait()
    store_res.wait()


def body(observed, psf_tiles):
    pair = jax.ShapeDtypeStruct((2, ROWS, COLS), F32)
    hbm = pl.BlockSpec(memory_space=pltpu.HBM)
    grads, images, factors = pl.pallas_call(
        kernel,
        out_shape=(pair, pair, jax.ShapeDtypeStruct((1, TILE), F32)),
        in_specs=[hbm, hbm],
        out_specs=(hbm, hbm, pl.BlockSpec(memory_space=pltpu.VMEM)),
        scratch_shapes=[
            pltpu.VMEM((ROWS, COLS), F32),
            pltpu.VMEM((1, 2, KSIZE * KSIZE), F32),
            pltpu.VMEM((8, TILE), F32),
            pltpu.VMEM((2, 3 * TILE, WIDE + TILE), BF16),
            pltpu.VMEM((2, 4 * TILE, WIDE), BF16),
            pltpu.VMEM((2, ROWS + 2 * PAD, WIDE + TILE), F32),
            pltpu.VMEM((2, EXT_ROWS, WIDE), F32),
            pltpu.VMEM((EXT_ROWS, EXT_COLS), F32),
            pltpu.VMEM((TALL_ROWS, EXT_COLS), F32),
            pltpu.VMEM((EXT_ROWS, EXT_COLS), F32),
            pltpu.VMEM((2, ROWS, COLS), F32),
            pltpu.VMEM((2, ROWS, COLS), F32),
            pltpu.VMEM((EXT_ROWS, COLS), F32),
            pltpu.VMEM((2, EXT_ROWS, TILE), F32),
            pltpu.VMEM((2, 32, TILE), F32),
            pltpu.VMEM((56, TILE), F32),
            pltpu.VMEM((56, TILE), F32),
            pltpu.VMEM((2, 16, TILE), F32),
            pltpu.VMEM((2, 16, TILE), F32),
            pltpu.VMEM((2, 32, TILE), F32),
            pltpu.VMEM((56, TILE), F32),
            pltpu.VMEM((56, TILE), F32),
            pltpu.VMEM((2, 16, TILE), F32),
            pltpu.VMEM((2, 16, TILE), F32),
            pltpu.VMEM((208, COLS), F32),
            pltpu.VMEM((160, COLS), F32),
            pltpu.VMEM((3, 1, TILE), F32),
            pltpu.VMEM((len(OFFSETS[0]), 1, TILE), F32),
            pltpu.VMEM((len(OFFSETS[1]), 1, TILE), F32),
            pltpu.SemaphoreType.DMA((8,)),
            pltpu.SemaphoreType.DMA((8,)),
            pltpu.SemaphoreType.DMA((2,)),
            pltpu.SemaphoreType.DMA((2,)),
            pltpu.SemaphoreType.DMA((2,)),
        ],
        compiler_params=pltpu.CompilerParams(
            collective_id=0, has_side_effects=True, vmem_limit_bytes=61 << 20
        ),
    )(observed, psf_tiles)
    block = jax.ShapeDtypeStruct((ROWS, COLS), F32)
    return pl.pallas_call(
        finish,
        out_shape=(block, block),
        in_specs=[pl.BlockSpec(memory_space=pltpu.HBM)] * 4,
        out_specs=(pl.BlockSpec(memory_space=pltpu.HBM),) * 2,
        scratch_shapes=[
            pltpu.VMEM((2, ROWS, COLS), F32),
            pltpu.VMEM((2, ROWS, COLS), F32),
            pltpu.VMEM((ROWS, COLS), F32),
            pltpu.VMEM((1, TILE), F32),
            pltpu.SemaphoreType.DMA((6,)),
        ],
        compiler_params=pltpu.CompilerParams(vmem_limit_bytes=61 << 20),
    )(grads, images, observed, factors)


def solution(mesh):
    return jax.shard_map(
        body,
        mesh=mesh,
        in_specs=(P("rng", "azi"), P("rng", "azi", None)),
        out_specs=(P("rng", "azi"), P("rng", "azi")),
        check_vma=False,
    )
```

```python
import itertools

import jax
import jax.numpy as jnp
from jax import lax
from jax.experimental import pallas as pl
from jax.experimental.pallas import tpu as pltpu
from jax.sharding import PartitionSpec as P

TILE = 128
KSIZE = 11
RADIUS = 5
RIM = 2 * RADIUS
ROWS = 128
COLS = 256
EXT_ROWS = 144
EXT_COLS = 384
TALL_ROWS = 176
PAD = 16
GROUPS = KSIZE * PAD
WIDE = KSIZE * TILE
MESH = pl.DeviceIdType.MESH
F32 = jnp.float32
BF16 = jnp.bfloat16

PARTS = {"x": 4, "y": 4, "z": 16, "c": 2}
PHASES = (("x", "y", "c"), ("z",))
NEIGHBOURS = tuple(
    (dr, da) for dr in (-1, 0, 1) for da in (-1, 0, 1) if (dr, da) != (0, 0)
)


def group_offsets(axes):
    ranges = [range(PARTS[axis]) for axis in axes]
    offsets = [dict(zip(axes, o)) for o in itertools.product(*ranges) if any(o)]
    return sorted(
        offsets,
        key=lambda o: -sum(min(n, PARTS[a] - n) for a, n in o.items() if a != "c"),
    )


OFFSETS = tuple(group_offsets(axes) for axes in PHASES)


def band_group(n):
    return (n * 373) >> 12


def split_rows(x):
    high = x.astype(BF16).astype(F32)
    return high, x - high


def iota(shape, dim):
    return lax.broadcasted_iota(jnp.int32, shape, dim)


def orders(taps):
    a, b = iota((TILE, TILE), 0), iota((TILE, TILE), 1)
    last = KSIZE * KSIZE - 1

    def turned(n):
        return KSIZE * (n - KSIZE * band_group(n)) + band_group(n)

    back = last - b
    wanted = (back, turned(b), jnp.where(back >= 0, turned(jnp.maximum(back, 0)), -1))
    pick = [jnp.where((a == w) & (b <= last), 1.0, 0.0).astype(BF16) for w in wanted]
    first = taps.astype(BF16)
    rest = taps - first.astype(F32)
    second = rest.astype(BF16)
    third = (rest - second.astype(F32)).astype(BF16)
    parts = jnp.concatenate([first, second, third], axis=1)
    out = [taps]
    for p in pick:
        out.append(jnp.dot(parts, jnp.concatenate([p] * 3, axis=0), preferred_element_type=F32))
    row = iota((8, TILE), 0)
    total = out[0]
    for k in range(1, 4):
        total = jnp.where((row >= 2 * k) & (row < 2 * k + 2), pltpu.roll(out[k], 2 * k, 0), total)
    return total


def sloped(line, shift, rows):
    base = pltpu.roll(jnp.broadcast_to(line, (8, TILE)), shift, 1)
    return pltpu.roll(jnp.concatenate([base] * (rows // 8), axis=0), 0, 1, stride=1, stride_axis=0)


def side_gather_weights(left, right):
    i, n = iota((40, TILE), 0), iota((40, TILE), 1)
    j = n - KSIZE * band_group(n)
    halves_ = []
    for kernel_row, start in ((left, 0), (right, 20)):
        band = sloped(kernel_row, TILE - RIM - start, 40)
        c = i - start
        keep = (c >= 0) & (c < 20) & (j < RIM) & (n < 121) & (c - j >= 0) & (c - j < KSIZE)
        halves_.append(jnp.where(keep, band, 0.0))
    high, low = split_rows(jnp.concatenate(halves_, axis=1))
    return jnp.concatenate([high, high, low, jnp.zeros((8, COLS), F32)], axis=0).astype(BF16)


def side_spread_weights(left, right):
    i, n = iota((24, TILE), 0), iota((24, TILE), 1)
    c = n - KSIZE * band_group(n)
    valid = (c < RIM) & (n < 121)
    halves_ = []
    for kernel_row, keep in (
        (left, valid & (i < RIM) & (c <= i)),
        (right, valid & (i >= RIM) & (i < 2 * RIM) & (c >= i - RIM)),
    ):
        band = sloped(kernel_row, TILE - RIM, 24)
        halves_.append(jnp.where(keep, band, 0.0))
    high, low = split_rows(jnp.concatenate(halves_, axis=1))
    return jnp.concatenate([high, high, low, jnp.zeros((TILE - 72, COLS), F32)], axis=0).astype(BF16)


def flat_bands(kernel_row, order, shift, lines):
    lane = iota((PAD, TILE), 1)
    last = KSIZE * (KSIZE - 1)
    base = pltpu.roll(jnp.broadcast_to(kernel_row, (8, TILE)), TILE - last, 1)
    taps = jnp.concatenate(
        [
            pltpu.roll(x, 0, 1, stride=KSIZE, stride_axis=0)
            for x in (base, pltpu.roll(base, 8 * KSIZE, 1))
        ],
        axis=0,
    )
    high, low = split_rows(jnp.where(lane < KSIZE, taps, 0.0))
    taps = high + pltpu.roll(high, 32, 1) + pltpu.roll(low, 64, 1)
    lines[...] = pltpu.roll(taps, shift % TILE, 1) if shift else taps
    blocks = []
    for v in order:
        line = jnp.broadcast_to(lines[v : v + 1, :], (8, TILE))
        line = pltpu.roll(line, 0, 1, stride=1, stride_axis=0)
        blocks += [line, pltpu.roll(line, 8, 1)]
    return jnp.concatenate(blocks, axis=0)


def flat_gather_weights(kernel_row, low_row, high_row, lines):
    band = flat_bands(kernel_row, range(KSIZE - 1, -1, -1), 0, lines)
    r = iota((GROUPS, TILE), 0) & (PAD - 1)
    return jnp.where((r >= low_row) & (r < high_row), band, 0.0).astype(BF16)


def flat_spread_weights(kernel_row, shift, lines):
    band = flat_bands(kernel_row, range(KSIZE), shift, lines)
    lane = iota((GROUPS, TILE), 1)
    keep = ((lane & 31) < PAD) & (lane < 96)
    return jnp.where(keep, band, 0.0).astype(BF16)


def side_fields(near, far):
    lane = iota(near.shape, 1)
    left = jnp.where(lane >= TILE - RIM, far, jnp.where(lane < RIM, near, 0.0))
    right = jnp.where(lane < 20, far, 0.0)
    x = pltpu.roll(left, RIM, 1) + pltpu.roll(right, 20, 1)
    high, low = split_rows(x)
    return (high + pltpu.roll(low, 40, 1) + pltpu.roll(high, 80, 1)).astype(BF16)


def picker(places, width):
    n = iota((TILE, width), 0)
    j = n - KSIZE * band_group(n)
    lane = iota((TILE, width), 1)
    blocks = [
        jnp.where((j < RIM) & (n < 121) & (lane == j + place), 1.0, 0.0).astype(BF16)
        for place in places
    ]
    return jnp.concatenate(blocks * 2, axis=0)


def picked(x, matrix):
    high, low = halves(x)
    return jnp.dot(jnp.concatenate([high, low], axis=1), matrix, preferred_element_type=F32)


def halves(x):
    high = x.astype(BF16)
    low = (x - high.astype(F32)).astype(BF16)
    return high, low


def kernel(
    obs_hbm,
    psf_hbm,
    grad_hbm,
    image_hbm,
    factors,
    obs_ref,
    psf_ref,
    taps,
    spread_w,
    gather_w,
    wide,
    tall,
    spill,
    tall_field,
    field,
    image,
    grad,
    shifted,
    strips,
    send_side,
    send_up,
    send_down,
    send_up_corner,
    send_down_corner,
    got_side,
    got_up,
    got_down,
    got_up_corner,
    got_down_corner,
    side_out,
    side_back,
    lines,
    pick_apart,
    pick_near,
    moments,
    got_a,
    got_b,
    halo_send,
    halo_recv,
    sum_send,
    sum_recv,
    load,
):
    rng = lax.axis_index("rng")
    azi = lax.axis_index("azi")
    place = {
        "x": azi // 8,
        "y": rng // 4,
        "z": (rng % 4) * 4 + (azi // 2) % 4,
        "c": azi % 2,
    }

    def member(offset):
        at = {
            axis: lax.rem(place[axis] + offset[axis], PARTS[axis])
            if axis in offset
            else place[axis]
            for axis in PARTS
        }
        return (at["y"] * 4 + at["z"] // 4, at["x"] * 8 + (at["z"] % 4) * 2 + at["c"])

    def neighbour(dr, da):
        return (lax.rem(rng + dr + 16, 16), lax.rem(azi + da + 32, 32))

    barrier = pltpu.get_barrier_semaphore()
    partners = [neighbour(*d) for d in NEIGHBOURS]
    partners += [member(o) for offsets in OFFSETS for o in offsets]
    for partner in partners:
        pl.semaphore_signal(barrier, inc=1, device_id=partner, device_id_type=MESH)
    load_psf = pltpu.make_async_copy(psf_hbm, psf_ref, load.at[0])
    load_obs = pltpu.make_async_copy(obs_hbm, obs_ref, load.at[1])
    load_psf.start()
    load_obs.start()

    lane = lax.broadcasted_iota(jnp.int32, (TILE, TILE), 1)
    row = lax.broadcasted_iota(jnp.int32, (TILE, TILE), 0)

    edge_lane, edge_row = lane[0:PAD], row[0:PAD]

    def band(line, shift, back):
        line = pltpu.roll(jnp.broadcast_to(line, (8, TILE)), lax.rem(2 * TILE - shift, TILE), 1)
        line = jnp.where(lane[0:8] < KSIZE, line, 0.0)
        line = pltpu.roll(line, back, 1) if back else line
        line = pltpu.roll(line, 0, 1, stride=1, stride_axis=0)
        rows = [pltpu.roll(line, 8 * g, 1) if g else line for g in range(TILE // 8)]
        return jnp.concatenate(rows, axis=0)

    def build_spread():
        def one(u, packed):
            block = pl.ds(pl.multiple_of(u * TILE, TILE), TILE)
            out = []
            for t in range(2):
                rows = band(taps[t : t + 1, :], KSIZE * u, 0)
                edge = rows[TILE - PAD :]
                below = edge_lane < edge_row + (TILE - PAD)
                over = jnp.where(below, edge, 0.0)
                out.append(packed[t] + pltpu.roll(over, KSIZE * u, 1))
                main = jnp.concatenate([rows[0 : TILE - PAD], jnp.where(below, 0.0, edge)], axis=0)
                high, low = halves(main)
                spread_w[t, 0:TILE, block] = high
                spread_w[t, TILE : 2 * TILE, block] = high
                spread_w[t, 2 * TILE :, block] = low
            return tuple(out)

        packed = lax.fori_loop(0, KSIZE, one, (jnp.zeros((PAD, TILE), F32),) * 2)
        blank = jnp.zeros((TILE - PAD, TILE), BF16)
        for t in range(2):
            high, low = (jnp.concatenate([blank, p], axis=0) for p in halves(packed[t]))
            spread_w[t, 0:TILE, WIDE:] = high
            spread_w[t, TILE : 2 * TILE, WIDE:] = high
            spread_w[t, 2 * TILE :, WIDE:] = low

    def build_gather():
        gather_w[:, 3 * TILE + 3 * PAD :, :] = jnp.zeros((2, TILE - 3 * PAD, WIDE), BF16)

        def one(u, carry):
            block = pl.ds(pl.multiple_of(u * TILE, TILE), TILE)
            for t in range(2):
                rows = band(taps[2 + t : 3 + t, :], KSIZE * (KSIZE - 1) - KSIZE * u, TILE - RIM)
                edge = rows[0:PAD]
                past = edge_lane > edge_row
                high, low = halves(jnp.where(past, edge, 0.0))
                gather_w[t, 3 * TILE : 3 * TILE + PAD, block] = high
                gather_w[t, 3 * TILE + PAD : 3 * TILE + 2 * PAD, block] = high
                gather_w[t, 3 * TILE + 2 * PAD : 3 * TILE + 3 * PAD, block] = low
                main = jnp.concatenate([jnp.where(past, 0.0, edge), rows[PAD:]], axis=0)
                high, low = halves(main)
                gather_w[t, 0:TILE, block] = high
                gather_w[t, TILE : 2 * TILE, block] = high
                gather_w[t, 2 * TILE : 3 * TILE, block] = low
            return carry

        lax.fori_loop(0, KSIZE, one, 0)

    pick_apart[...] = picker((0, TILE), COLS)
    pick_near[...] = picker((0, RIM), TILE)
    load_psf.wait()
    taps[...] = jnp.zeros_like(taps)
    taps[0:2, 0 : KSIZE * KSIZE] = psf_ref[0]
    kernels = orders(taps[...])
    taps[...] = kernels
    build_spread()
    wide[:, 0:PAD, :] = jnp.zeros((2, PAD, WIDE + TILE), F32)
    wide[:, PAD + ROWS :, :] = jnp.zeros((2, PAD, WIDE + TILE), F32)

    def spread(source, out):
        group = band_group(iota((1, TILE), 1))
        spares = []
        for t in range(2):
            high, low = halves(source[:, t * TILE : (t + 1) * TILE])
            left = jnp.concatenate([high, low, high], axis=1)
            for n in range(0, WIDE + TILE, 256):
                wide[t, PAD : PAD + ROWS, n : n + 256] = jnp.dot(
                    left, spread_w[t, :, n : n + 256], preferred_element_type=F32
                )
            total, spare = None, jnp.zeros((EXT_ROWS, TILE), F32)
            for u in range(KSIZE):
                rows = pl.ds(PAD - u, EXT_ROWS)
                piece = wide[t, rows, u * TILE : (u + 1) * TILE]
                total = piece if total is None else total + piece
                spare = jnp.where(group == u, wide[t, rows, WIDE:], spare)
            out[:, t * TILE : (t + 1) * TILE] = total
            spares.append(spare)
        over = picked(jnp.concatenate(spares, axis=1), pick_apart[...])
        out[:, TILE : 2 * TILE] += over[:, 0:TILE]
        out[:, 2 * TILE :] = over[:, TILE:]

    def gather(source, row, t):
        tall_lane = lax.broadcasted_iota(jnp.int32, (EXT_ROWS, TILE), 1)
        high, low = halves(source[row : row + EXT_ROWS, t * TILE : (t + 1) * TILE])
        edge = source[row : row + EXT_ROWS, (t + 1) * TILE : (t + 2) * TILE]
        edge = jnp.where(tall_lane < RIM, edge, 0.0)
        edge_high = edge.astype(BF16).astype(F32)
        edge_low = edge - edge_high
        edge = edge_high + pltpu.roll(edge_low, PAD, 1) + pltpu.roll(edge_high, 2 * PAD, 1)
        left = jnp.concatenate([high, low, high, edge.astype(BF16)], axis=1)
        total = None
        for n in range(0, WIDE, 256):
            width = min(256, WIDE - n)
            tall[t, :, n : n + width] = jnp.dot(
                left, gather_w[t, :, n : n + width], preferred_element_type=F32
            )
        for u in range(KSIZE):
            piece = tall[t, pl.ds(u, ROWS), u * TILE : (u + 1) * TILE]
            total = piece if total is None else total + piece
        return total

    def pack(strip, rows):
        out = None
        for k in range(strip.shape[0] // rows):
            part = strip[rows * k : rows * k + rows]
            part = jnp.where(lane[0:rows] < 2 * RIM, part, 0.0)
            part = pltpu.roll(part, 2 * RIM * k, 1) if k else part
            out = part if out is None else out + part
        return out

    def unpack(packed, groups):
        parts = []
        for k in range(groups):
            part = pltpu.roll(packed, TILE - 2 * RIM * k, 1) if k else packed
            parts.append(jnp.where(lane[0 : packed.shape[0]] < 2 * RIM, part, 0.0))
        return jnp.concatenate(parts, axis=0)

    def start_exchange():
        side = iota((EXT_ROWS, TILE), 1)
        right = jnp.where(side >= TILE - RIM, spill[:, TILE : 2 * TILE], spill[:, 2 * TILE :])
        strips[0] = spill[:, 0:TILE]
        strips[1] = pltpu.roll(right, RIM, 1)
        for i in range(2):
            send_side[i, 0:24] = pack(strips[i], 24)
            send_side[i, 24:] = kernels
            send_up_corner[i, 0:8] = pack(strips[i, 0:24], 8)
            send_up_corner[i, 8:] = kernels
            send_down_corner[i, 0:8] = pack(strips[i, 118:142], 8)
            send_down_corner[i, 8:] = kernels
        for send, at in ((send_up, 0), (send_down, 118)):
            for t in range(2):
                tile = slice(t * TILE, (t + 1) * TILE)
                send[16 * t : 16 * t + 16] = spill[at : at + 16, tile]
                send[32 + 4 * t : 36 + 4 * t] = spill[at + 16 : at + 20, tile]
            send[40:48] = pack(spill[at : at + 24, 2 * TILE :], 8)
            send[48:] = kernels
        plan = {
            (-1, 1): (send_up_corner.at[1], got_up_corner.at[1]),
            (1, -1): (send_down_corner.at[0], got_down_corner.at[0]),
            (-1, -1): (send_up_corner.at[0], got_up_corner.at[0]),
            (1, 1): (send_down_corner.at[1], got_down_corner.at[1]),
            (-1, 0): (send_up, got_up),
            (1, 0): (send_down, got_down),
            (0, -1): (send_side.at[0], got_side.at[0]),
            (0, 1): (send_side.at[1], got_side.at[1]),
        }
        return [
            pltpu.make_async_remote_copy(
                src_ref=source,
                dst_ref=target,
                send_sem=halo_send.at[i],
                recv_sem=halo_recv.at[i],
                device_id=neighbour(*d),
                device_id_type=MESH,
            )
            for i, (d, (source, target)) in enumerate(plan.items())
        ]

    above = jnp.where(rng > 0, 1.0, 0.0)
    below = jnp.where(rng < 15, 1.0, 0.0)
    left_of = jnp.where(azi > 0, 1.0, 0.0)
    right_of = jnp.where(azi < 31, 1.0, 0.0)

    def assemble():
        first, last = slice(0, TILE), slice(2 * TILE, EXT_COLS)
        tall_field[0:PAD] = jnp.zeros((PAD, EXT_COLS), F32)
        tall_field[PAD : PAD + EXT_ROWS] = spill[...]
        tall_field[PAD + EXT_ROWS :] = jnp.zeros((PAD, EXT_COLS), F32)
        for got, at, flag in ((got_down, 6, above), (got_up, 144, below)):
            for t in range(2):
                tile = slice(t * TILE, (t + 1) * TILE)
                tall_field[at : at + 16, tile] += got[16 * t : 16 * t + 16] * flag
                tall_field[at + 16 : at + 20, tile] += got[32 + 4 * t : 36 + 4 * t] * flag
            tall_field[at : at + 24, last] += unpack(got[40:48], 3) * flag

        def from_left(strip, rows, flag):
            strip = pltpu.roll(strip, TILE - RIM, 1) * flag
            near = iota(strip.shape, 1) < TILE // 2
            tall_field[rows, first] += jnp.where(near, strip, 0.0)
            tall_field[rows, last] += jnp.where(near, 0.0, strip)

        def from_right(strip, rows, flag):
            tall_field[rows, last] += strip * flag

        middle, top, bottom = slice(16, 160), slice(6, 30), slice(144, 168)
        from_right(unpack(got_side[0, 0:24], 6), middle, right_of)
        from_left(unpack(got_side[1, 0:24], 6), middle, left_of)
        from_right(unpack(got_down_corner[0, 0:8], 3), top, above * right_of)
        from_left(unpack(got_down_corner[1, 0:8], 3), top, above * left_of)
        from_right(unpack(got_up_corner[0, 0:8], 3), bottom, below * right_of)
        from_left(unpack(got_up_corner[1, 0:8], 3), bottom, below * left_of)
        r, c = iota((TALL_ROWS, EXT_COLS), 0), iota((TALL_ROWS, EXT_COLS), 1)
        inside = (
            (r >= jnp.where(rng == 0, PAD + RADIUS, 0))
            & (r < jnp.where(rng == 15, PAD + RADIUS + ROWS, TALL_ROWS))
            & (c >= jnp.where(azi == 0, RADIUS, 0))
            & (c < jnp.where(azi == 0, 320, EXT_COLS))
            & ((c < jnp.where(azi == 31, RADIUS + COLS, EXT_COLS)) | (c >= 320))
        )
        tall_field[...] = jnp.where(inside, tall_field[...], 0.0)

    def side_kernels(k):
        return tuple(
            (got[1, at + 1 + k : at + 2 + k] * (flag * left_of), got[0, at + k : at + 1 + k] * (flag * right_of))
            for got, at, flag in ((got_down_corner, 8, above), (got_side, 24, 1.0), (got_up_corner, 8, below))
        )

    def side_frames():
        fields = side_fields(tall_field[:, 0:TILE], tall_field[:, 2 * TILE :])
        parts = ((0, 32, 144, 16), (16, 144, 0, 128), (144, 32, 176, 16))
        group = band_group(iota((1, COLS), 1) & (TILE - 1))
        sums = []
        for (start, count, at, rows), (left, right) in zip(parts, side_kernels(2)):
            side_out[at : at + count] = jnp.dot(
                fields[start : start + count], side_gather_weights(left, right), preferred_element_type=F32
            )
            total = jnp.zeros((rows, COLS), F32)
            for u in range(KSIZE):
                total = jnp.where(group == KSIZE - 1 - u, side_out[at + u : at + u + rows], total)
            sums.append(total)
        frames = picked(jnp.concatenate(sums, axis=0), pick_near[...])
        r = iota(frames.shape, 0)
        return jnp.where((r >= 6) & (r < 154), frames, 0.0)

    def side_spread(frames):
        high, low = split_rows(frames)
        packed = (high + pltpu.roll(low, 24, 1) + pltpu.roll(high, 48, 1)).astype(BF16)
        for (start, stop), (left, right) in zip(((0, 16), (16, 144), (144, 160)), side_kernels(0)):
            side_back[start:stop] = jnp.dot(
                packed[start:stop], side_spread_weights(left, right), preferred_element_type=F32
            )
        group = band_group(iota((1, COLS), 1) & (TILE - 1))
        total = jnp.zeros((EXT_ROWS, COLS), F32)
        for u in range(KSIZE):
            total = jnp.where(group == u, side_back[PAD - u : PAD - u + EXT_ROWS], total)
        out = picked(total, pick_apart[...])
        return out[:, 0:TILE], out[:, TILE:]

    def flat_frames(rows, kernels, low_row, at):
        high, low = halves(tall_field[rows, :])
        right = jnp.concatenate([high, low, high, jnp.zeros((32, EXT_COLS), BF16)], axis=0)
        tiles = []
        for t in range(2):
            out = jnp.dot(
                flat_gather_weights(kernels[t], low_row, low_row + RIM, lines.at[at + t]),
                right[:, t * TILE : t * TILE + COLS],
                preferred_element_type=F32,
            )
            total = out[0:PAD]
            for v in range(1, KSIZE):
                total = total + pltpu.roll(out[PAD * v : PAD * v + PAD], COLS - v, 1)
            tiles.append(total[:, 0:TILE])
        return tiles

    def flat_spread(tiles, kernels, shift, at):
        outs = []
        for t in range(2):
            high, low = halves(tiles[t])
            gap = jnp.zeros((PAD, TILE), BF16)
            right = jnp.concatenate([high, gap, low, gap, high, gap, gap, gap], axis=0)
            out = jnp.dot(flat_spread_weights(kernels[t], shift, lines.at[at + t]), right, preferred_element_type=F32)
            out = jnp.concatenate([out, jnp.zeros((GROUPS, TILE), F32)], axis=1)
            total = out[0:PAD]
            for v in range(1, KSIZE):
                total = total + pltpu.roll(out[PAD * v : PAD * v + PAD], v, 1)
            outs.append(total)
        return outs

    def inner(x, y):
        z = x * y
        z = z[:, 0:TILE] + z[:, TILE:]
        while z.shape[0] > 8:
            half = z.shape[0] // 2
            z = z[0:half] + z[half:]
        return jnp.sum(jnp.sum(z, axis=0, keepdims=True), axis=1, keepdims=True)

    def inner_rimmed(x, y):
        r, c = iota((EXT_ROWS, EXT_COLS), 0), iota((EXT_ROWS, EXT_COLS), 1)
        own = (r >= RADIUS) & (r < ROWS + RADIUS) & (c >= RADIUS) & (c < COLS + RADIUS)
        z = jnp.where(own, x * y, 0.0)
        z = z[:, 0:TILE] + z[:, TILE : 2 * TILE] + z[:, 2 * TILE :]
        z = z[0:72] + z[72:]
        z = (z[0:24] + z[24:48]) + z[48:72]
        z = (z[0:8] + z[8:16]) + z[16:24]
        return jnp.sum(jnp.sum(z, axis=0, keepdims=True), axis=1, keepdims=True)

    def own_block(source, row):
        shifted[...] = pltpu.roll(source[row : row + EXT_ROWS, :], EXT_COLS - RADIUS, 1)[:, 0:COLS]
        return shifted[pl.ds(RADIUS, ROWS), :]

    load_obs.wait()
    spread(obs_ref[...], spill)
    copies = start_exchange()
    pl.semaphore_wait(barrier, len(partners))
    for copy in copies:
        copy.start()
    build_gather()
    for copy in copies:
        copy.wait()
    assemble()
    for t in range(2):
        image[0, :, t * TILE : (t + 1) * TILE] = gather(tall_field, PAD, t)
    frames = side_frames()
    kernels_top = [got_down[52 + t : 53 + t] * above for t in range(2)]
    kernels_bottom = [got_up[52 + t : 53 + t] * below for t in range(2)]
    frames_top = flat_frames(slice(0, 32), kernels_top, 6, 0)
    frames_bottom = flat_frames(slice(144, 176), kernels_bottom, 0, 2)
    spread(image[0], field)
    to_left, to_right = side_spread(frames)
    field[:, 0:TILE] += to_left
    field[:, 2 * TILE :] += to_right
    kernels_top = [got_down[54 + t : 55 + t] * above for t in range(2)]
    kernels_bottom = [got_up[54 + t : 55 + t] * below for t in range(2)]
    for t, out in enumerate(flat_spread(frames_top, kernels_top, 6, 4)):
        field[0:PAD, t * TILE : t * TILE + COLS] += out
    for t, out in enumerate(flat_spread(frames_bottom, kernels_bottom, -RIM, 6)):
        field[ROWS:, t * TILE : t * TILE + COLS] += out
    r, c = iota((EXT_ROWS, EXT_COLS), 0), iota((EXT_ROWS, EXT_COLS), 1)
    inside = (
        (r >= jnp.where(rng == 0, RADIUS, 0))
        & (r < jnp.where(rng == 15, ROWS + RADIUS, EXT_ROWS))
        & (c >= jnp.where(azi == 0, RADIUS, 0))
        & (c < jnp.where(azi == 31, COLS + RADIUS, EXT_COLS))
    )
    field[...] = jnp.where(inside, field[...], 0.0)
    for t in range(2):
        image[1, :, t * TILE : (t + 1) * TILE] = gather(field, 0, t)
    store_image = pltpu.make_async_copy(image, image_hbm, load.at[1])
    store_image.start()
    first = tall_field[PAD : PAD + EXT_ROWS, :]
    second = field[...]
    sums = [inner_rimmed(first, first), inner(image[0], image[0])]
    sums += [inner_rimmed(second, second), inner_rimmed(first, second)]
    sums += [inner(image[1], image[1]), inner(image[0], image[1])]
    line = lane[0:1]
    moments[0] = sum(jnp.where(line == i, x, 0.0) for i, x in enumerate(sums))
    for phase, got in enumerate((got_a, got_b)):
        for i, o in enumerate(OFFSETS[phase]):
            pltpu.make_async_remote_copy(
                src_ref=moments.at[phase],
                dst_ref=got.at[i],
                send_sem=sum_send.at[phase],
                recv_sem=sum_recv.at[phase],
                device_id=member(o),
                device_id_type=MESH,
            ).start()
        if phase == 0:
            grad[0] = own_block(tall_field, PAD)
            grad[1] = own_block(field, 0)
            store_grad = pltpu.make_async_copy(grad, grad_hbm, load.at[0])
            store_grad.start()
        pltpu.make_async_copy(got, got, sum_recv.at[phase]).wait()
        moments[phase + 1] = moments[phase] + jnp.sum(got[...], axis=0)
    total = moments[2]
    gg, qq, ww, gw, pp, qp = (total[:, i : i + 1] for i in range(6))
    alpha = gg / qq
    gamma_1 = (gg - alpha * gw) - alpha * (gw - alpha * ww)
    rise = 1.0 + gamma_1 / gg
    delta_1 = rise * (rise * qq - alpha * qp) - alpha * (rise * qp - alpha * pp)
    alpha_1 = gamma_1 / delta_1
    near = alpha + alpha_1 * rise
    far = alpha * alpha_1
    factors[...] = jnp.where(line == 0, near, far)
    for phase, got in enumerate((got_a, got_b)):
        pltpu.make_async_copy(got, got, sum_send.at[phase]).wait()
    store_grad.wait()
    store_image.wait()


def finish(grad_hbm, image_hbm, obs_hbm, factors_hbm, est_hbm, res_hbm, grad, image, obs, factors, sems):
    ins = ((factors_hbm, factors), (grad_hbm, grad), (image_hbm, image), (obs_hbm, obs))
    loads = [pltpu.make_async_copy(a, b, sems.at[i]) for i, (a, b) in enumerate(ins)]
    for load in loads:
        load.start()
    loads[0].wait()
    loads[1].wait()
    near, far = factors[:, 0:1], factors[:, 1:2]
    grad[0] = near * grad[0] - far * grad[1]
    store_est = pltpu.make_async_copy(grad.at[0], est_hbm, sems.at[4])
    store_est.start()
    loads[2].wait()
    loads[3].wait()
    image[0] = obs[...] - near * image[0] + far * image[1]
    store_res = pltpu.make_async_copy(image.at[0], res_hbm, sems.at[5])
    store_res.start()
    store_est.wait()
    store_res.wait()


def body(observed, psf_tiles):
    pair = jax.ShapeDtypeStruct((2, ROWS, COLS), F32)
    hbm = pl.BlockSpec(memory_space=pltpu.HBM)
    grads, images, factors = pl.pallas_call(
        kernel,
        out_shape=(pair, pair, jax.ShapeDtypeStruct((1, TILE), F32)),
        in_specs=[hbm, hbm],
        out_specs=(hbm, hbm, pl.BlockSpec(memory_space=pltpu.VMEM)),
        scratch_shapes=[
            pltpu.VMEM((ROWS, COLS), F32),
            pltpu.VMEM((1, 2, KSIZE * KSIZE), F32),
            pltpu.VMEM((8, TILE), F32),
            pltpu.VMEM((2, 3 * TILE, WIDE + TILE), BF16),
            pltpu.VMEM((2, 4 * TILE, WIDE), BF16),
            pltpu.VMEM((2, ROWS + 2 * PAD, WIDE + TILE), F32),
            pltpu.VMEM((2, EXT_ROWS, WIDE), F32),
            pltpu.VMEM((EXT_ROWS, EXT_COLS), F32),
            pltpu.VMEM((TALL_ROWS, EXT_COLS), F32),
            pltpu.VMEM((EXT_ROWS, EXT_COLS), F32),
            pltpu.VMEM((2, ROWS, COLS), F32),
            pltpu.VMEM((2, ROWS, COLS), F32),
            pltpu.VMEM((EXT_ROWS, COLS), F32),
            pltpu.VMEM((2, EXT_ROWS, TILE), F32),
            pltpu.VMEM((2, 32, TILE), F32),
            pltpu.VMEM((56, TILE), F32),
            pltpu.VMEM((56, TILE), F32),
            pltpu.VMEM((2, 16, TILE), F32),
            pltpu.VMEM((2, 16, TILE), F32),
            pltpu.VMEM((2, 32, TILE), F32),
            pltpu.VMEM((56, TILE), F32),
            pltpu.VMEM((56, TILE), F32),
            pltpu.VMEM((2, 16, TILE), F32),
            pltpu.VMEM((2, 16, TILE), F32),
            pltpu.VMEM((208, COLS), F32),
            pltpu.VMEM((160, COLS), F32),
            pltpu.VMEM((8, PAD, TILE), F32),
            pltpu.VMEM((4 * TILE, COLS), BF16),
            pltpu.VMEM((4 * TILE, TILE), BF16),
            pltpu.VMEM((3, 1, TILE), F32),
            pltpu.VMEM((len(OFFSETS[0]), 1, TILE), F32),
            pltpu.VMEM((len(OFFSETS[1]), 1, TILE), F32),
            pltpu.SemaphoreType.DMA((8,)),
            pltpu.SemaphoreType.DMA((8,)),
            pltpu.SemaphoreType.DMA((2,)),
            pltpu.SemaphoreType.DMA((2,)),
            pltpu.SemaphoreType.DMA((2,)),
        ],
        compiler_params=pltpu.CompilerParams(
            collective_id=0, has_side_effects=True, vmem_limit_bytes=61 << 20
        ),
    )(observed, psf_tiles)
    block = jax.ShapeDtypeStruct((ROWS, COLS), F32)
    return pl.pallas_call(
        finish,
        out_shape=(block, block),
        in_specs=[pl.BlockSpec(memory_space=pltpu.HBM)] * 4,
        out_specs=(pl.BlockSpec(memory_space=pltpu.HBM),) * 2,
        scratch_shapes=[
            pltpu.VMEM((2, ROWS, COLS), F32),
            pltpu.VMEM((2, ROWS, COLS), F32),
            pltpu.VMEM((ROWS, COLS), F32),
            pltpu.VMEM((1, TILE), F32),
            pltpu.SemaphoreType.DMA((6,)),
        ],
        compiler_params=pltpu.CompilerParams(vmem_limit_bytes=61 << 20),
    )(grads, images, observed, factors)


def solution(mesh):
    return jax.shard_map(
        body,
        mesh=mesh,
        in_specs=(P("rng", "azi"), P("rng", "azi", None)),
        out_specs=(P("rng", "azi"), P("rng", "azi")),
        check_vma=False,
    )
```

```python
import itertools

import jax
import jax.numpy as jnp
from jax import lax
from jax.experimental import pallas as pl
from jax.experimental.pallas import tpu as pltpu
from jax.sharding import PartitionSpec as P

TILE = 128
KSIZE = 11
RADIUS = 5
RIM = 2 * RADIUS
ROWS = 128
COLS = 256
EXT_ROWS = 144
EXT_COLS = 384
TALL_ROWS = 176
PAD = 16
GROUPS = KSIZE * PAD
WIDE = KSIZE * TILE
MESH = pl.DeviceIdType.MESH
F32 = jnp.float32
BF16 = jnp.bfloat16

PARTS = {"x": 4, "y": 4, "z": 16, "c": 2}
PHASES = (("x", "y", "c"), ("z",))
NEIGHBOURS = tuple(
    (dr, da) for dr in (-1, 0, 1) for da in (-1, 0, 1) if (dr, da) != (0, 0)
)


def group_offsets(axes):
    ranges = [range(PARTS[axis]) for axis in axes]
    offsets = [dict(zip(axes, o)) for o in itertools.product(*ranges) if any(o)]
    return sorted(
        offsets,
        key=lambda o: -sum(min(n, PARTS[a] - n) for a, n in o.items() if a != "c"),
    )


OFFSETS = tuple(group_offsets(axes) for axes in PHASES)


def band_group(n):
    return (n * 373) >> 12


def split_rows(x):
    high = x.astype(BF16).astype(F32)
    return high, x - high


def iota(shape, dim):
    return lax.broadcasted_iota(jnp.int32, shape, dim)


def orders(taps):
    a, b = iota((TILE, TILE), 0), iota((TILE, TILE), 1)
    last = KSIZE * KSIZE - 1

    def turned(n):
        return KSIZE * (n - KSIZE * band_group(n)) + band_group(n)

    back = last - b
    wanted = (back, turned(b), jnp.where(back >= 0, turned(jnp.maximum(back, 0)), -1))
    pick = [jnp.where((a == w) & (b <= last), 1.0, 0.0).astype(BF16) for w in wanted]
    first = taps.astype(BF16)
    rest = taps - first.astype(F32)
    second = rest.astype(BF16)
    third = (rest - second.astype(F32)).astype(BF16)
    parts = jnp.concatenate([first, second, third], axis=1)
    out = [taps]
    for p in pick:
        out.append(jnp.dot(parts, jnp.concatenate([p] * 3, axis=0), preferred_element_type=F32))
    row = iota((8, TILE), 0)
    total = out[0]
    for k in range(1, 4):
        total = jnp.where((row >= 2 * k) & (row < 2 * k + 2), pltpu.roll(out[k], 2 * k, 0), total)
    return total


def sloped(line, shift, rows):
    base = pltpu.roll(jnp.broadcast_to(line, (8, TILE)), shift, 1)
    return pltpu.roll(jnp.concatenate([base] * (rows // 8), axis=0), 0, 1, stride=1, stride_axis=0)


def side_gather_weights(left, right):
    i, n = iota((40, TILE), 0), iota((40, TILE), 1)
    j = n - KSIZE * band_group(n)
    halves_ = []
    for kernel_row, start in ((left, 0), (right, 20)):
        band = sloped(kernel_row, TILE - RIM - start, 40)
        c = i - start
        keep = (c >= 0) & (c < 20) & (j < RIM) & (n < 121) & (c - j >= 0) & (c - j < KSIZE)
        halves_.append(jnp.where(keep, band, 0.0))
    high, low = split_rows(jnp.concatenate(halves_, axis=1))
    return jnp.concatenate([high, high, low, jnp.zeros((8, COLS), F32)], axis=0).astype(BF16)


def side_spread_weights(left, right):
    i, n = iota((24, TILE), 0), iota((24, TILE), 1)
    c = n - KSIZE * band_group(n)
    valid = (c < RIM) & (n < 121)
    halves_ = []
    for kernel_row, keep in (
        (left, valid & (i < RIM) & (c <= i)),
        (right, valid & (i >= RIM) & (i < 2 * RIM) & (c >= i - RIM)),
    ):
        band = sloped(kernel_row, TILE - RIM, 24)
        halves_.append(jnp.where(keep, band, 0.0))
    high, low = split_rows(jnp.concatenate(halves_, axis=1))
    return jnp.concatenate([high, high, low, jnp.zeros((TILE - 72, COLS), F32)], axis=0).astype(BF16)


def flat_bands(kernel_row, order, shift, lines):
    lane = iota((PAD, TILE), 1)
    last = KSIZE * (KSIZE - 1)
    base = pltpu.roll(jnp.broadcast_to(kernel_row, (8, TILE)), TILE - last, 1)
    taps = jnp.concatenate(
        [
            pltpu.roll(x, 0, 1, stride=KSIZE, stride_axis=0)
            for x in (base, pltpu.roll(base, 8 * KSIZE, 1))
        ],
        axis=0,
    )
    high, low = split_rows(jnp.where(lane < KSIZE, taps, 0.0))
    taps = high + pltpu.roll(high, 32, 1) + pltpu.roll(low, 64, 1)
    lines[...] = pltpu.roll(taps, shift % TILE, 1) if shift else taps
    blocks = []
    for v in order:
        line = jnp.broadcast_to(lines[v : v + 1, :], (8, TILE))
        line = pltpu.roll(line, 0, 1, stride=1, stride_axis=0)
        blocks += [line, pltpu.roll(line, 8, 1)]
    return jnp.concatenate(blocks, axis=0)


def flat_gather_weights(kernel_row, low_row, high_row, lines):
    band = flat_bands(kernel_row, range(KSIZE - 1, -1, -1), 0, lines)
    r = iota((GROUPS, TILE), 0) & (PAD - 1)
    return jnp.where((r >= low_row) & (r < high_row), band, 0.0).astype(BF16)


def flat_spread_weights(kernel_row, shift, lines):
    band = flat_bands(kernel_row, range(KSIZE), shift, lines)
    lane = iota((GROUPS, TILE), 1)
    keep = ((lane & 31) < PAD) & (lane < 96)
    return jnp.where(keep, band, 0.0).astype(BF16)


def side_fields(near, far):
    lane = iota(near.shape, 1)
    left = jnp.where(lane >= TILE - RIM, far, jnp.where(lane < RIM, near, 0.0))
    right = jnp.where(lane < 20, far, 0.0)
    x = pltpu.roll(left, RIM, 1) + pltpu.roll(right, 20, 1)
    high, low = split_rows(x)
    return (high + pltpu.roll(low, 40, 1) + pltpu.roll(high, 80, 1)).astype(BF16)


def picker(places, width):
    n = iota((TILE, width), 0)
    j = n - KSIZE * band_group(n)
    lane = iota((TILE, width), 1)
    blocks = [
        jnp.where((j < RIM) & (n < 121) & (lane == j + place), 1.0, 0.0).astype(BF16)
        for place in places
    ]
    return jnp.concatenate(blocks * 2, axis=0)


def picked(x, matrix):
    high, low = halves(x)
    return jnp.dot(jnp.concatenate([high, low], axis=1), matrix, preferred_element_type=F32)


def halves(x):
    high = x.astype(BF16)
    low = (x - high.astype(F32)).astype(BF16)
    return high, low


def kernel(
    obs_hbm,
    psf_hbm,
    grad_hbm,
    image_hbm,
    factors,
    obs_ref,
    psf_ref,
    taps,
    spread_w,
    gather_w,
    wide,
    tall,
    spill,
    tall_field,
    field,
    image,
    grad,
    shifted,
    strips,
    send_side,
    send_up,
    send_down,
    send_up_corner,
    send_down_corner,
    got_side,
    got_up,
    got_down,
    got_up_corner,
    got_down_corner,
    side_out,
    side_back,
    lines,
    pick_apart,
    pick_near,
    moments,
    got_a,
    got_b,
    halo_send,
    halo_recv,
    sum_send,
    sum_recv,
    load,
):
    rng = lax.axis_index("rng")
    azi = lax.axis_index("azi")
    place = {
        "x": azi // 8,
        "y": rng // 4,
        "z": (rng % 4) * 4 + (azi // 2) % 4,
        "c": azi % 2,
    }

    def member(offset):
        at = {
            axis: lax.rem(place[axis] + offset[axis], PARTS[axis])
            if axis in offset
            else place[axis]
            for axis in PARTS
        }
        return (at["y"] * 4 + at["z"] // 4, at["x"] * 8 + (at["z"] % 4) * 2 + at["c"])

    def neighbour(dr, da):
        return (lax.rem(rng + dr + 16, 16), lax.rem(azi + da + 32, 32))

    barrier = pltpu.get_barrier_semaphore()
    partners = [neighbour(*d) for d in NEIGHBOURS]
    partners += [member(o) for offsets in OFFSETS for o in offsets]
    for partner in partners:
        pl.semaphore_signal(barrier, inc=1, device_id=partner, device_id_type=MESH)
    load_psf = pltpu.make_async_copy(psf_hbm, psf_ref, load.at[0])
    load_obs = pltpu.make_async_copy(obs_hbm, obs_ref, load.at[1])
    load_psf.start()
    load_obs.start()

    lane = lax.broadcasted_iota(jnp.int32, (TILE, TILE), 1)
    row = lax.broadcasted_iota(jnp.int32, (TILE, TILE), 0)

    edge_lane, edge_row = lane[0:PAD], row[0:PAD]

    def band(line, shift, back):
        line = pltpu.roll(jnp.broadcast_to(line, (8, TILE)), lax.rem(3 * TILE - shift, TILE), 1)
        line = jnp.where(lane[0:8] < KSIZE, line, 0.0)
        line = pltpu.roll(line, back, 1) if back else line
        line = pltpu.roll(line, 0, 1, stride=1, stride_axis=0)
        rows = [pltpu.roll(line, 8 * g, 1) if g else line for g in range(TILE // 8)]
        return jnp.concatenate(rows, axis=0)

    def build_spread():
        def one(u, packed):
            block = pl.ds(pl.multiple_of(u * TILE, TILE), TILE)
            used = jnp.where(u < KSIZE, 1.0, 0.0)
            out = []
            for t in range(2):
                rows = band(taps[t : t + 1, :], KSIZE * u, 0)
                edge = rows[TILE - PAD :]
                below = edge_lane < edge_row + (TILE - PAD)
                over = jnp.where(below, edge, 0.0) * used
                out.append(packed[t] + pltpu.roll(over, lax.rem(KSIZE * u, TILE), 1))
                main = jnp.concatenate([rows[0 : TILE - PAD], jnp.where(below, 0.0, edge)], axis=0)
                high, low = halves(main)
                spread_w[t, 0:TILE, block] = high
                spread_w[t, TILE : 2 * TILE, block] = high
                spread_w[t, 2 * TILE :, block] = low
            return tuple(out)

        def three(i, packed):
            for k in range(3):
                packed = one(3 * i + k, packed)
            return packed

        packed = lax.fori_loop(0, 4, three, (jnp.zeros((PAD, TILE), F32),) * 2)
        blank = jnp.zeros((TILE - PAD, TILE), BF16)
        for t in range(2):
            high, low = (jnp.concatenate([blank, p], axis=0) for p in halves(packed[t]))
            spread_w[t, 0:TILE, WIDE:] = high
            spread_w[t, TILE : 2 * TILE, WIDE:] = high
            spread_w[t, 2 * TILE :, WIDE:] = low

    def build_gather():
        gather_w[:, 3 * TILE + 3 * PAD :, :] = jnp.zeros((2, TILE - 3 * PAD, WIDE + TILE), BF16)

        def one(u, carry):
            block = pl.ds(pl.multiple_of(u * TILE, TILE), TILE)
            for t in range(2):
                rows = band(taps[2 + t : 3 + t, :], KSIZE * (KSIZE - 1) - KSIZE * u, TILE - RIM)
                edge = rows[0:PAD]
                past = edge_lane > edge_row
                high, low = halves(jnp.where(past, edge, 0.0))
                gather_w[t, 3 * TILE : 3 * TILE + PAD, block] = high
                gather_w[t, 3 * TILE + PAD : 3 * TILE + 2 * PAD, block] = high
                gather_w[t, 3 * TILE + 2 * PAD : 3 * TILE + 3 * PAD, block] = low
                main = jnp.concatenate([jnp.where(past, 0.0, edge), rows[PAD:]], axis=0)
                high, low = halves(main)
                gather_w[t, 0:TILE, block] = high
                gather_w[t, TILE : 2 * TILE, block] = high
                gather_w[t, 2 * TILE : 3 * TILE, block] = low
            return carry

        def three(i, carry):
            for k in range(3):
                one(3 * i + k, carry)
            return carry

        lax.fori_loop(0, 4, three, 0)

    pick_apart[...] = picker((0, TILE), COLS)
    pick_near[...] = picker((0, RIM), TILE)
    load_psf.wait()
    taps[...] = jnp.zeros_like(taps)
    taps[0:2, 0 : KSIZE * KSIZE] = psf_ref[0]
    kernels = orders(taps[...])
    taps[...] = kernels
    build_spread()
    wide[:, 0:PAD, :] = jnp.zeros((2, PAD, WIDE + TILE), F32)
    wide[:, PAD + ROWS :, :] = jnp.zeros((2, PAD, WIDE + TILE), F32)

    def spread(source, out):
        group = band_group(iota((1, TILE), 1))
        spares = []
        for t in range(2):
            high, low = halves(source[:, t * TILE : (t + 1) * TILE])
            left = jnp.concatenate([high, low, high], axis=1)
            for n in range(0, WIDE + TILE, 256):
                wide[t, PAD : PAD + ROWS, n : n + 256] = jnp.dot(
                    left, spread_w[t, :, n : n + 256], preferred_element_type=F32
                )
            total, spare = None, jnp.zeros((EXT_ROWS, TILE), F32)
            for u in range(KSIZE):
                rows = pl.ds(PAD - u, EXT_ROWS)
                piece = wide[t, rows, u * TILE : (u + 1) * TILE]
                total = piece if total is None else total + piece
                spare = jnp.where(group == u, wide[t, rows, WIDE:], spare)
            out[:, t * TILE : (t + 1) * TILE] = total
            spares.append(spare)
        over = picked(jnp.concatenate(spares, axis=1), pick_apart[...])
        out[:, TILE : 2 * TILE] += over[:, 0:TILE]
        out[:, 2 * TILE :] = over[:, TILE:]

    def gather(source, row, t):
        tall_lane = lax.broadcasted_iota(jnp.int32, (EXT_ROWS, TILE), 1)
        high, low = halves(source[row : row + EXT_ROWS, t * TILE : (t + 1) * TILE])
        edge = source[row : row + EXT_ROWS, (t + 1) * TILE : (t + 2) * TILE]
        edge = jnp.where(tall_lane < RIM, edge, 0.0)
        edge_high = edge.astype(BF16).astype(F32)
        edge_low = edge - edge_high
        edge = edge_high + pltpu.roll(edge_low, PAD, 1) + pltpu.roll(edge_high, 2 * PAD, 1)
        left = jnp.concatenate([high, low, high, edge.astype(BF16)], axis=1)
        total = None
        for n in range(0, WIDE, 256):
            width = min(256, WIDE - n)
            tall[t, :, n : n + width] = jnp.dot(
                left, gather_w[t, :, n : n + width], preferred_element_type=F32
            )
        for u in range(KSIZE):
            piece = tall[t, pl.ds(u, ROWS), u * TILE : (u + 1) * TILE]
            total = piece if total is None else total + piece
        return total

    def pack(strip, rows):
        out = None
        for k in range(strip.shape[0] // rows):
            part = strip[rows * k : rows * k + rows]
            part = jnp.where(lane[0:rows] < 2 * RIM, part, 0.0)
            part = pltpu.roll(part, 2 * RIM * k, 1) if k else part
            out = part if out is None else out + part
        return out

    def unpack(packed, groups):
        parts = []
        for k in range(groups):
            part = pltpu.roll(packed, TILE - 2 * RIM * k, 1) if k else packed
            parts.append(jnp.where(lane[0 : packed.shape[0]] < 2 * RIM, part, 0.0))
        return jnp.concatenate(parts, axis=0)

    def start_exchange():
        side = iota((EXT_ROWS, TILE), 1)
        right = jnp.where(side >= TILE - RIM, spill[:, TILE : 2 * TILE], spill[:, 2 * TILE :])
        strips[0] = spill[:, 0:TILE]
        strips[1] = pltpu.roll(right, RIM, 1)
        for i in range(2):
            send_side[i, 0:24] = pack(strips[i], 24)
            send_side[i, 24:] = kernels
            send_up_corner[i, 0:8] = pack(strips[i, 0:24], 8)
            send_up_corner[i, 8:] = kernels
            send_down_corner[i, 0:8] = pack(strips[i, 118:142], 8)
            send_down_corner[i, 8:] = kernels
        for send, at in ((send_up, 0), (send_down, 118)):
            for t in range(2):
                tile = slice(t * TILE, (t + 1) * TILE)
                send[16 * t : 16 * t + 16] = spill[at : at + 16, tile]
                send[32 + 4 * t : 36 + 4 * t] = spill[at + 16 : at + 20, tile]
            send[40:48] = pack(spill[at : at + 24, 2 * TILE :], 8)
            send[48:] = kernels
        plan = {
            (-1, 1): (send_up_corner.at[1], got_up_corner.at[1]),
            (1, -1): (send_down_corner.at[0], got_down_corner.at[0]),
            (-1, -1): (send_up_corner.at[0], got_up_corner.at[0]),
            (1, 1): (send_down_corner.at[1], got_down_corner.at[1]),
            (-1, 0): (send_up, got_up),
            (1, 0): (send_down, got_down),
            (0, -1): (send_side.at[0], got_side.at[0]),
            (0, 1): (send_side.at[1], got_side.at[1]),
        }
        return [
            pltpu.make_async_remote_copy(
                src_ref=source,
                dst_ref=target,
                send_sem=halo_send.at[i],
                recv_sem=halo_recv.at[i],
                device_id=neighbour(*d),
                device_id_type=MESH,
            )
            for i, (d, (source, target)) in enumerate(plan.items())
        ]

    above = jnp.where(rng > 0, 1.0, 0.0)
    below = jnp.where(rng < 15, 1.0, 0.0)
    left_of = jnp.where(azi > 0, 1.0, 0.0)
    right_of = jnp.where(azi < 31, 1.0, 0.0)

    def assemble():
        first, last = slice(0, TILE), slice(2 * TILE, EXT_COLS)
        tall_field[0:PAD] = jnp.zeros((PAD, EXT_COLS), F32)
        tall_field[PAD : PAD + EXT_ROWS] = spill[...]
        tall_field[PAD + EXT_ROWS :] = jnp.zeros((PAD, EXT_COLS), F32)
        for got, at, flag in ((got_down, 6, above), (got_up, 144, below)):
            for t in range(2):
                tile = slice(t * TILE, (t + 1) * TILE)
                tall_field[at : at + 16, tile] += got[16 * t : 16 * t + 16] * flag
                tall_field[at + 16 : at + 20, tile] += got[32 + 4 * t : 36 + 4 * t] * flag
            tall_field[at : at + 24, last] += unpack(got[40:48], 3) * flag

        def from_left(strip, rows, flag):
            strip = pltpu.roll(strip, TILE - RIM, 1) * flag
            near = iota(strip.shape, 1) < TILE // 2
            tall_field[rows, first] += jnp.where(near, strip, 0.0)
            tall_field[rows, last] += jnp.where(near, 0.0, strip)

        def from_right(strip, rows, flag):
            tall_field[rows, last] += strip * flag

        middle, top, bottom = slice(16, 160), slice(6, 30), slice(144, 168)
        from_right(unpack(got_side[0, 0:24], 6), middle, right_of)
        from_left(unpack(got_side[1, 0:24], 6), middle, left_of)
        from_right(unpack(got_down_corner[0, 0:8], 3), top, above * right_of)
        from_left(unpack(got_down_corner[1, 0:8], 3), top, above * left_of)
        from_right(unpack(got_up_corner[0, 0:8], 3), bottom, below * right_of)
        from_left(unpack(got_up_corner[1, 0:8], 3), bottom, below * left_of)
        r, c = iota((TALL_ROWS, EXT_COLS), 0), iota((TALL_ROWS, EXT_COLS), 1)
        inside = (
            (r >= jnp.where(rng == 0, PAD + RADIUS, 0))
            & (r < jnp.where(rng == 15, PAD + RADIUS + ROWS, TALL_ROWS))
            & (c >= jnp.where(azi == 0, RADIUS, 0))
            & (c < jnp.where(azi == 0, 320, EXT_COLS))
            & ((c < jnp.where(azi == 31, RADIUS + COLS, EXT_COLS)) | (c >= 320))
        )
        tall_field[...] = jnp.where(inside, tall_field[...], 0.0)

    def side_kernels(k):
        return tuple(
            (got[1, at + 1 + k : at + 2 + k] * (flag * left_of), got[0, at + k : at + 1 + k] * (flag * right_of))
            for got, at, flag in ((got_down_corner, 8, above), (got_side, 24, 1.0), (got_up_corner, 8, below))
        )

    def side_frames():
        fields = side_fields(tall_field[:, 0:TILE], tall_field[:, 2 * TILE :])
        parts = ((0, 32, 144, 16), (16, 144, 0, 128), (144, 32, 176, 16))
        group = band_group(iota((1, COLS), 1) & (TILE - 1))
        sums = []
        for (start, count, at, rows), (left, right) in zip(parts, side_kernels(2)):
            side_out[at : at + count] = jnp.dot(
                fields[start : start + count], side_gather_weights(left, right), preferred_element_type=F32
            )
            total = jnp.zeros((rows, COLS), F32)
            for u in range(KSIZE):
                total = jnp.where(group == KSIZE - 1 - u, side_out[at + u : at + u + rows], total)
            sums.append(total)
        frames = picked(jnp.concatenate(sums, axis=0), pick_near[...])
        r = iota(frames.shape, 0)
        return jnp.where((r >= 6) & (r < 154), frames, 0.0)

    def side_spread(frames):
        high, low = split_rows(frames)
        packed = (high + pltpu.roll(low, 24, 1) + pltpu.roll(high, 48, 1)).astype(BF16)
        for (start, stop), (left, right) in zip(((0, 16), (16, 144), (144, 160)), side_kernels(0)):
            side_back[start:stop] = jnp.dot(
                packed[start:stop], side_spread_weights(left, right), preferred_element_type=F32
            )
        group = band_group(iota((1, COLS), 1) & (TILE - 1))
        total = jnp.zeros((EXT_ROWS, COLS), F32)
        for u in range(KSIZE):
            total = jnp.where(group == u, side_back[PAD - u : PAD - u + EXT_ROWS], total)
        out = picked(total, pick_apart[...])
        return out[:, 0:TILE], out[:, TILE:]

    def flat_frames(rows, kernels, low_row, at):
        high, low = halves(tall_field[rows, :])
        right = jnp.concatenate([high, low, high, jnp.zeros((32, EXT_COLS), BF16)], axis=0)
        tiles = []
        for t in range(2):
            out = jnp.dot(
                flat_gather_weights(kernels[t], low_row, low_row + RIM, lines.at[at + t]),
                right[:, t * TILE : t * TILE + COLS],
                preferred_element_type=F32,
            )
            total = out[0:PAD]
            for v in range(1, KSIZE):
                total = total + pltpu.roll(out[PAD * v : PAD * v + PAD], COLS - v, 1)
            tiles.append(total[:, 0:TILE])
        return tiles

    def flat_spread(tiles, kernels, shift, at):
        outs = []
        for t in range(2):
            high, low = halves(tiles[t])
            gap = jnp.zeros((PAD, TILE), BF16)
            right = jnp.concatenate([high, gap, low, gap, high, gap, gap, gap], axis=0)
            out = jnp.dot(flat_spread_weights(kernels[t], shift, lines.at[at + t]), right, preferred_element_type=F32)
            near, far = out[0:PAD], None
            for v in range(1, KSIZE):
                piece = pltpu.roll(out[PAD * v : PAD * v + PAD], v, 1)
                past = edge_lane < v
                near = near + jnp.where(past, 0.0, piece)
                piece = jnp.where(past, piece, 0.0)
                far = piece if far is None else far + piece
            total = jnp.concatenate([near, far], axis=1)
            outs.append(total)
        return outs

    def inner(x, y):
        z = x * y
        z = z[:, 0:TILE] + z[:, TILE:]
        while z.shape[0] > 8:
            half = z.shape[0] // 2
            z = z[0:half] + z[half:]
        return jnp.sum(jnp.sum(z, axis=0, keepdims=True), axis=1, keepdims=True)

    def inner_rimmed(x, y):
        r, c = iota((EXT_ROWS, EXT_COLS), 0), iota((EXT_ROWS, EXT_COLS), 1)
        own = (r >= RADIUS) & (r < ROWS + RADIUS) & (c >= RADIUS) & (c < COLS + RADIUS)
        z = jnp.where(own, x * y, 0.0)
        z = z[:, 0:TILE] + z[:, TILE : 2 * TILE] + z[:, 2 * TILE :]
        z = z[0:72] + z[72:]
        z = (z[0:24] + z[24:48]) + z[48:72]
        z = (z[0:8] + z[8:16]) + z[16:24]
        return jnp.sum(jnp.sum(z, axis=0, keepdims=True), axis=1, keepdims=True)

    def own_block(source, row):
        shifted[...] = pltpu.roll(source[row : row + EXT_ROWS, :], EXT_COLS - RADIUS, 1)[:, 0:COLS]
        return shifted[pl.ds(RADIUS, ROWS), :]

    load_obs.wait()
    spread(obs_ref[...], spill)
    copies = start_exchange()
    pl.semaphore_wait(barrier, len(partners))
    for copy in copies:
        copy.start()
    build_gather()
    for copy in copies:
        copy.wait()
    assemble()
    for t in range(2):
        image[0, :, t * TILE : (t + 1) * TILE] = gather(tall_field, PAD, t)
    frames = side_frames()
    kernels_top = [got_down[52 + t : 53 + t] * above for t in range(2)]
    kernels_bottom = [got_up[52 + t : 53 + t] * below for t in range(2)]
    frames_top = flat_frames(slice(0, 32), kernels_top, 6, 0)
    frames_bottom = flat_frames(slice(144, 176), kernels_bottom, 0, 2)
    spread(image[0], field)
    to_left, to_right = side_spread(frames)
    field[:, 0:TILE] += to_left
    field[:, 2 * TILE :] += to_right
    kernels_top = [got_down[54 + t : 55 + t] * above for t in range(2)]
    kernels_bottom = [got_up[54 + t : 55 + t] * below for t in range(2)]
    for t, out in enumerate(flat_spread(frames_top, kernels_top, 6, 4)):
        field[0:PAD, t * TILE : t * TILE + COLS] += out
    for t, out in enumerate(flat_spread(frames_bottom, kernels_bottom, -RIM, 6)):
        field[ROWS:, t * TILE : t * TILE + COLS] += out
    r, c = iota((EXT_ROWS, EXT_COLS), 0), iota((EXT_ROWS, EXT_COLS), 1)
    inside = (
        (r >= jnp.where(rng == 0, RADIUS, 0))
        & (r < jnp.where(rng == 15, ROWS + RADIUS, EXT_ROWS))
        & (c >= jnp.where(azi == 0, RADIUS, 0))
        & (c < jnp.where(azi == 31, COLS + RADIUS, EXT_COLS))
    )
    field[...] = jnp.where(inside, field[...], 0.0)
    for t in range(2):
        image[1, :, t * TILE : (t + 1) * TILE] = gather(field, 0, t)
    store_image = pltpu.make_async_copy(image, image_hbm, load.at[1])
    store_image.start()
    first = tall_field[PAD : PAD + EXT_ROWS, :]
    second = field[...]
    sums = [inner_rimmed(first, first), inner(image[0], image[0])]
    sums += [inner_rimmed(second, second), inner_rimmed(first, second)]
    sums += [inner(image[1], image[1]), inner(image[0], image[1])]
    line = lane[0:1]
    moments[0] = sum(jnp.where(line == i, x, 0.0) for i, x in enumerate(sums))
    for phase, got in enumerate((got_a, got_b)):
        for i, o in enumerate(OFFSETS[phase]):
            pltpu.make_async_remote_copy(
                src_ref=moments.at[phase],
                dst_ref=got.at[i],
                send_sem=sum_send.at[phase],
                recv_sem=sum_recv.at[phase],
                device_id=member(o),
                device_id_type=MESH,
            ).start()
        if phase == 0:
            grad[0] = own_block(tall_field, PAD)
            grad[1] = own_block(field, 0)
            store_grad = pltpu.make_async_copy(grad, grad_hbm, load.at[0])
            store_grad.start()
        pltpu.make_async_copy(got, got, sum_recv.at[phase]).wait()
        moments[phase + 1] = moments[phase] + jnp.sum(got[...], axis=0)
    total = moments[2]
    gg, qq, ww, gw, pp, qp = (total[:, i : i + 1] for i in range(6))
    alpha = gg / qq
    gamma_1 = (gg - alpha * gw) - alpha * (gw - alpha * ww)
    rise = 1.0 + gamma_1 / gg
    delta_1 = rise * (rise * qq - alpha * qp) - alpha * (rise * qp - alpha * pp)
    alpha_1 = gamma_1 / delta_1
    near = alpha + alpha_1 * rise
    far = alpha * alpha_1
    factors[...] = jnp.where(line == 0, near, far)
    for phase, got in enumerate((got_a, got_b)):
        pltpu.make_async_copy(got, got, sum_send.at[phase]).wait()
    store_grad.wait()
    store_image.wait()


def finish(grad_hbm, image_hbm, obs_hbm, factors_hbm, est_hbm, res_hbm, grad, image, obs, factors, sems):
    ins = ((factors_hbm, factors), (grad_hbm, grad), (image_hbm, image), (obs_hbm, obs))
    loads = [pltpu.make_async_copy(a, b, sems.at[i]) for i, (a, b) in enumerate(ins)]
    for load in loads:
        load.start()
    loads[0].wait()
    loads[1].wait()
    near, far = factors[:, 0:1], factors[:, 1:2]
    grad[0] = near * grad[0] - far * grad[1]
    store_est = pltpu.make_async_copy(grad.at[0], est_hbm, sems.at[4])
    store_est.start()
    loads[2].wait()
    loads[3].wait()
    image[0] = obs[...] - near * image[0] + far * image[1]
    store_res = pltpu.make_async_copy(image.at[0], res_hbm, sems.at[5])
    store_res.start()
    store_est.wait()
    store_res.wait()


def body(observed, psf_tiles):
    pair = jax.ShapeDtypeStruct((2, ROWS, COLS), F32)
    hbm = pl.BlockSpec(memory_space=pltpu.HBM)
    grads, images, factors = pl.pallas_call(
        kernel,
        out_shape=(pair, pair, jax.ShapeDtypeStruct((1, TILE), F32)),
        in_specs=[hbm, hbm],
        out_specs=(hbm, hbm, pl.BlockSpec(memory_space=pltpu.VMEM)),
        scratch_shapes=[
            pltpu.VMEM((ROWS, COLS), F32),
            pltpu.VMEM((1, 2, KSIZE * KSIZE), F32),
            pltpu.VMEM((8, TILE), F32),
            pltpu.VMEM((2, 3 * TILE, WIDE + TILE), BF16),
            pltpu.VMEM((2, 4 * TILE, WIDE + TILE), BF16),
            pltpu.VMEM((2, ROWS + 2 * PAD, WIDE + TILE), F32),
            pltpu.VMEM((2, EXT_ROWS, WIDE), F32),
            pltpu.VMEM((EXT_ROWS, EXT_COLS), F32),
            pltpu.VMEM((TALL_ROWS, EXT_COLS), F32),
            pltpu.VMEM((EXT_ROWS, EXT_COLS), F32),
            pltpu.VMEM((2, ROWS, COLS), F32),
            pltpu.VMEM((2, ROWS, COLS), F32),
            pltpu.VMEM((EXT_ROWS, COLS), F32),
            pltpu.VMEM((2, EXT_ROWS, TILE), F32),
            pltpu.VMEM((2, 32, TILE), F32),
            pltpu.VMEM((56, TILE), F32),
            pltpu.VMEM((56, TILE), F32),
            pltpu.VMEM((2, 16, TILE), F32),
            pltpu.VMEM((2, 16, TILE), F32),
            pltpu.VMEM((2, 32, TILE), F32),
            pltpu.VMEM((56, TILE), F32),
            pltpu.VMEM((56, TILE), F32),
            pltpu.VMEM((2, 16, TILE), F32),
            pltpu.VMEM((2, 16, TILE), F32),
            pltpu.VMEM((208, COLS), F32),
            pltpu.VMEM((160, COLS), F32),
            pltpu.VMEM((8, PAD, TILE), F32),
            pltpu.VMEM((4 * TILE, COLS), BF16),
            pltpu.VMEM((4 * TILE, TILE), BF16),
            pltpu.VMEM((3, 1, TILE), F32),
            pltpu.VMEM((len(OFFSETS[0]), 1, TILE), F32),
            pltpu.VMEM((len(OFFSETS[1]), 1, TILE), F32),
            pltpu.SemaphoreType.DMA((8,)),
            pltpu.SemaphoreType.DMA((8,)),
            pltpu.SemaphoreType.DMA((2,)),
            pltpu.SemaphoreType.DMA((2,)),
            pltpu.SemaphoreType.DMA((2,)),
        ],
        compiler_params=pltpu.CompilerParams(
            collective_id=0, has_side_effects=True, vmem_limit_bytes=61 << 20
        ),
    )(observed, psf_tiles)
    block = jax.ShapeDtypeStruct((ROWS, COLS), F32)
    return pl.pallas_call(
        finish,
        out_shape=(block, block),
        in_specs=[pl.BlockSpec(memory_space=pltpu.HBM)] * 4,
        out_specs=(pl.BlockSpec(memory_space=pltpu.HBM),) * 2,
        scratch_shapes=[
            pltpu.VMEM((2, ROWS, COLS), F32),
            pltpu.VMEM((2, ROWS, COLS), F32),
            pltpu.VMEM((ROWS, COLS), F32),
            pltpu.VMEM((1, TILE), F32),
            pltpu.SemaphoreType.DMA((6,)),
        ],
        compiler_params=pltpu.CompilerParams(vmem_limit_bytes=61 << 20),
    )(grads, images, observed, factors)


def solution(mesh):
    return jax.shard_map(
        body,
        mesh=mesh,
        in_specs=(P("rng", "azi"), P("rng", "azi", None)),
        out_specs=(P("rng", "azi"), P("rng", "azi")),
        check_vma=False,
    )
```

```python
import itertools

import jax
import jax.numpy as jnp
from jax import lax
from jax.experimental import pallas as pl
from jax.experimental.pallas import tpu as pltpu
from jax.sharding import PartitionSpec as P

TILE = 128
KSIZE = 11
RADIUS = 5
RIM = 2 * RADIUS
ROWS = 128
COLS = 256
EXT_ROWS = 144
EXT_COLS = 384
TALL_ROWS = 176
PAD = 16
GROUPS = KSIZE * PAD
WIDE = KSIZE * TILE
MESH = pl.DeviceIdType.MESH
F32 = jnp.float32
BF16 = jnp.bfloat16

PARTS = {"x": 4, "y": 4, "z": 16, "c": 2}
PHASES = (("x", "y", "c"), ("z",))
NEIGHBOURS = tuple(
    (dr, da) for dr in (-1, 0, 1) for da in (-1, 0, 1) if (dr, da) != (0, 0)
)


def group_offsets(axes):
    ranges = [range(PARTS[axis]) for axis in axes]
    offsets = [dict(zip(axes, o)) for o in itertools.product(*ranges) if any(o)]
    return sorted(
        offsets,
        key=lambda o: -sum(min(n, PARTS[a] - n) for a, n in o.items() if a != "c"),
    )


OFFSETS = tuple(group_offsets(axes) for axes in PHASES)


def band_group(n):
    return (n * 373) >> 12


def split_rows(x):
    high = x.astype(BF16).astype(F32)
    return high, x - high


def iota(shape, dim):
    return lax.broadcasted_iota(jnp.int32, shape, dim)


def orders(taps):
    a, b = iota((TILE, TILE), 0), iota((TILE, TILE), 1)
    last = KSIZE * KSIZE - 1

    def turned(n):
        return KSIZE * (n - KSIZE * band_group(n)) + band_group(n)

    back = last - b
    wanted = (back, turned(b), jnp.where(back >= 0, turned(jnp.maximum(back, 0)), -1))
    pick = [jnp.where((a == w) & (b <= last), 1.0, 0.0).astype(BF16) for w in wanted]
    first = taps.astype(BF16)
    rest = taps - first.astype(F32)
    second = rest.astype(BF16)
    third = (rest - second.astype(F32)).astype(BF16)
    parts = jnp.concatenate([first, second, third], axis=1)
    out = [taps]
    for p in pick:
        out.append(jnp.dot(parts, jnp.concatenate([p] * 3, axis=0), preferred_element_type=F32))
    row = iota((8, TILE), 0)
    total = out[0]
    for k in range(1, 4):
        total = jnp.where((row >= 2 * k) & (row < 2 * k + 2), pltpu.roll(out[k], 2 * k, 0), total)
    return total


def sloped(line, shift, rows):
    base = pltpu.roll(jnp.broadcast_to(line, (8, TILE)), shift, 1)
    return pltpu.roll(jnp.concatenate([base] * (rows // 8), axis=0), 0, 1, stride=1, stride_axis=0)


def side_gather_weights(left, right):
    i, n = iota((40, TILE), 0), iota((40, TILE), 1)
    j = n - KSIZE * band_group(n)
    halves_ = []
    for kernel_row, start in ((left, 0), (right, 20)):
        band = sloped(kernel_row, TILE - RIM - start, 40)
        c = i - start
        keep = (c >= 0) & (c < 20) & (j < RIM) & (n < 121) & (c - j >= 0) & (c - j < KSIZE)
        halves_.append(jnp.where(keep, band, 0.0))
    high, low = split_rows(jnp.concatenate(halves_, axis=1))
    return jnp.concatenate([high, high, low, jnp.zeros((8, COLS), F32)], axis=0).astype(BF16)


def side_spread_weights(left, right):
    i, n = iota((24, TILE), 0), iota((24, TILE), 1)
    c = n - KSIZE * band_group(n)
    valid = (c < RIM) & (n < 121)
    halves_ = []
    for kernel_row, keep in (
        (left, valid & (i < RIM) & (c <= i)),
        (right, valid & (i >= RIM) & (i < 2 * RIM) & (c >= i - RIM)),
    ):
        band = sloped(kernel_row, TILE - RIM, 24)
        halves_.append(jnp.where(keep, band, 0.0))
    high, low = split_rows(jnp.concatenate(halves_, axis=1))
    return jnp.concatenate([high, high, low, jnp.zeros((TILE - 72, COLS), F32)], axis=0).astype(BF16)


def flat_bands(kernel_row, order, shift, lines):
    lane = iota((PAD, TILE), 1)
    last = KSIZE * (KSIZE - 1)
    base = pltpu.roll(jnp.broadcast_to(kernel_row, (8, TILE)), TILE - last, 1)
    taps = jnp.concatenate(
        [
            pltpu.roll(x, 0, 1, stride=KSIZE, stride_axis=0)
            for x in (base, pltpu.roll(base, 8 * KSIZE, 1))
        ],
        axis=0,
    )
    high, low = split_rows(jnp.where(lane < KSIZE, taps, 0.0))
    taps = high + pltpu.roll(high, 32, 1) + pltpu.roll(low, 64, 1)
    lines[...] = pltpu.roll(taps, shift % TILE, 1) if shift else taps
    blocks = []
    for v in order:
        line = jnp.broadcast_to(lines[v : v + 1, :], (8, TILE))
        line = pltpu.roll(line, 0, 1, stride=1, stride_axis=0)
        blocks += [line, pltpu.roll(line, 8, 1)]
    return jnp.concatenate(blocks, axis=0)


def flat_gather_weights(kernel_row, low_row, high_row, lines):
    band = flat_bands(kernel_row, range(KSIZE - 1, -1, -1), 0, lines)
    r = iota((GROUPS, TILE), 0) & (PAD - 1)
    return jnp.where((r >= low_row) & (r < high_row), band, 0.0).astype(BF16)


def flat_spread_weights(kernel_row, shift, lines):
    band = flat_bands(kernel_row, range(KSIZE), shift, lines)
    lane = iota((GROUPS, TILE), 1)
    keep = ((lane & 31) < PAD) & (lane < 96)
    return jnp.where(keep, band, 0.0).astype(BF16)


def side_fields(near, far):
    lane = iota(near.shape, 1)
    left = jnp.where(lane >= TILE - RIM, far, jnp.where(lane < RIM, near, 0.0))
    right = jnp.where(lane < 20, far, 0.0)
    x = pltpu.roll(left, RIM, 1) + pltpu.roll(right, 20, 1)
    high, low = split_rows(x)
    return (high + pltpu.roll(low, 40, 1) + pltpu.roll(high, 80, 1)).astype(BF16)


def picker(places, width):
    n = iota((TILE, width), 0)
    j = n - KSIZE * band_group(n)
    lane = iota((TILE, width), 1)
    blocks = [
        jnp.where((j < RIM) & (n < 121) & (lane == j + place), 1.0, 0.0).astype(BF16)
        for place in places
    ]
    return jnp.concatenate(blocks * 2, axis=0)


def picked(x, matrix):
    high, low = halves(x)
    return jnp.dot(jnp.concatenate([high, low], axis=1), matrix, preferred_element_type=F32)


def halves(x):
    high = x.astype(BF16)
    low = (x - high.astype(F32)).astype(BF16)
    return high, low


def kernel(
    obs_hbm,
    psf_hbm,
    grad_hbm,
    image_hbm,
    factors,
    obs_ref,
    psf_ref,
    taps,
    spread_w,
    gather_w,
    wide,
    tall,
    spill,
    tall_field,
    field,
    image,
    grad,
    shifted,
    strips,
    send_side,
    send_up,
    send_down,
    send_up_corner,
    send_down_corner,
    got_side,
    got_up,
    got_down,
    got_up_corner,
    got_down_corner,
    side_out,
    side_back,
    lines,
    flat_w,
    side_w,
    pick_apart,
    pick_near,
    moments,
    got_a,
    got_b,
    halo_send,
    halo_recv,
    sum_send,
    sum_recv,
    load,
):
    rng = lax.axis_index("rng")
    azi = lax.axis_index("azi")
    place = {
        "x": azi // 8,
        "y": rng // 4,
        "z": (rng % 4) * 4 + (azi // 2) % 4,
        "c": azi % 2,
    }

    def member(offset):
        at = {
            axis: lax.rem(place[axis] + offset[axis], PARTS[axis])
            if axis in offset
            else place[axis]
            for axis in PARTS
        }
        return (at["y"] * 4 + at["z"] // 4, at["x"] * 8 + (at["z"] % 4) * 2 + at["c"])

    def neighbour(dr, da):
        return (lax.rem(rng + dr + 16, 16), lax.rem(azi + da + 32, 32))

    barrier = pltpu.get_barrier_semaphore()
    partners = [neighbour(*d) for d in NEIGHBOURS]
    partners += [member(o) for offsets in OFFSETS for o in offsets]
    for partner in partners:
        pl.semaphore_signal(barrier, inc=1, device_id=partner, device_id_type=MESH)
    load_psf = pltpu.make_async_copy(psf_hbm, psf_ref, load.at[0])
    load_obs = pltpu.make_async_copy(obs_hbm, obs_ref, load.at[1])
    load_psf.start()
    load_obs.start()

    lane = lax.broadcasted_iota(jnp.int32, (TILE, TILE), 1)
    row = lax.broadcasted_iota(jnp.int32, (TILE, TILE), 0)

    edge_lane, edge_row = lane[0:PAD], row[0:PAD]

    def band(line, shift, back):
        line = pltpu.roll(jnp.broadcast_to(line, (8, TILE)), lax.rem(3 * TILE - shift, TILE), 1)
        line = jnp.where(lane[0:8] < KSIZE, line, 0.0)
        line = pltpu.roll(line, back, 1) if back else line
        line = pltpu.roll(line, 0, 1, stride=1, stride_axis=0)
        rows = [pltpu.roll(line, 8 * g, 1) if g else line for g in range(TILE // 8)]
        return jnp.concatenate(rows, axis=0)

    def build_spread():
        def one(u, packed):
            block = pl.ds(pl.multiple_of(u * TILE, TILE), TILE)
            used = jnp.where(u < KSIZE, 1.0, 0.0)
            out = []
            for t in range(2):
                rows = band(taps[t : t + 1, :], KSIZE * u, 0)
                edge = rows[TILE - PAD :]
                below = edge_lane < edge_row + (TILE - PAD)
                over = jnp.where(below, edge, 0.0) * used
                out.append(packed[t] + pltpu.roll(over, lax.rem(KSIZE * u, TILE), 1))
                main = jnp.concatenate([rows[0 : TILE - PAD], jnp.where(below, 0.0, edge)], axis=0)
                high, low = halves(main)
                spread_w[t, 0:TILE, block] = high
                spread_w[t, TILE : 2 * TILE, block] = high
                spread_w[t, 2 * TILE :, block] = low
            return tuple(out)

        def six(i, packed):
            for k in range(6):
                packed = one(6 * i + k, packed)
            return packed

        packed = lax.fori_loop(0, 2, six, (jnp.zeros((PAD, TILE), F32),) * 2)
        blank = jnp.zeros((TILE - PAD, TILE), BF16)
        for t in range(2):
            high, low = (jnp.concatenate([blank, p], axis=0) for p in halves(packed[t]))
            spread_w[t, 0:TILE, WIDE:] = high
            spread_w[t, TILE : 2 * TILE, WIDE:] = high
            spread_w[t, 2 * TILE :, WIDE:] = low

    def build_gather():
        gather_w[:, 3 * TILE + 3 * PAD :, :] = jnp.zeros((2, TILE - 3 * PAD, WIDE + TILE), BF16)

        def one(u, carry):
            block = pl.ds(pl.multiple_of(u * TILE, TILE), TILE)
            for t in range(2):
                rows = band(taps[2 + t : 3 + t, :], KSIZE * (KSIZE - 1) - KSIZE * u, TILE - RIM)
                edge = rows[0:PAD]
                past = edge_lane > edge_row
                high, low = halves(jnp.where(past, edge, 0.0))
                gather_w[t, 3 * TILE : 3 * TILE + PAD, block] = high
                gather_w[t, 3 * TILE + PAD : 3 * TILE + 2 * PAD, block] = high
                gather_w[t, 3 * TILE + 2 * PAD : 3 * TILE + 3 * PAD, block] = low
                main = jnp.concatenate([jnp.where(past, 0.0, edge), rows[PAD:]], axis=0)
                high, low = halves(main)
                gather_w[t, 0:TILE, block] = high
                gather_w[t, TILE : 2 * TILE, block] = high
                gather_w[t, 2 * TILE : 3 * TILE, block] = low
            return carry

        def six(i, carry):
            for k in range(6):
                one(6 * i + k, carry)
            return carry

        lax.fori_loop(0, 2, six, 0)

    pick_apart[...] = picker((0, TILE), COLS)
    pick_near[...] = picker((0, RIM), TILE)
    load_psf.wait()
    taps[...] = jnp.zeros_like(taps)
    taps[0:2, 0 : KSIZE * KSIZE] = psf_ref[0]
    kernels = orders(taps[...])
    taps[...] = kernels
    build_spread()
    wide[:, 0:PAD, :] = jnp.zeros((2, PAD, WIDE + TILE), F32)
    wide[:, PAD + ROWS :, :] = jnp.zeros((2, PAD, WIDE + TILE), F32)

    def spread(source, out):
        group = band_group(iota((1, TILE), 1))
        spares = []
        for t in range(2):
            high, low = halves(source[:, t * TILE : (t + 1) * TILE])
            left = jnp.concatenate([high, low, high], axis=1)
            for n in range(0, WIDE + TILE, 256):
                wide[t, PAD : PAD + ROWS, n : n + 256] = jnp.dot(
                    left, spread_w[t, :, n : n + 256], preferred_element_type=F32
                )
            total, spare = None, jnp.zeros((EXT_ROWS, TILE), F32)
            for u in range(KSIZE):
                rows = pl.ds(PAD - u, EXT_ROWS)
                piece = wide[t, rows, u * TILE : (u + 1) * TILE]
                total = piece if total is None else total + piece
                spare = jnp.where(group == u, wide[t, rows, WIDE:], spare)
            out[:, t * TILE : (t + 1) * TILE] = total
            spares.append(spare)
        over = picked(jnp.concatenate(spares, axis=1), pick_apart[...])
        out[:, TILE : 2 * TILE] += over[:, 0:TILE]
        out[:, 2 * TILE :] = over[:, TILE:]

    def gather(source, row, t):
        tall_lane = lax.broadcasted_iota(jnp.int32, (EXT_ROWS, TILE), 1)
        high, low = halves(source[row : row + EXT_ROWS, t * TILE : (t + 1) * TILE])
        edge = source[row : row + EXT_ROWS, (t + 1) * TILE : (t + 2) * TILE]
        edge = jnp.where(tall_lane < RIM, edge, 0.0)
        edge_high = edge.astype(BF16).astype(F32)
        edge_low = edge - edge_high
        edge = edge_high + pltpu.roll(edge_low, PAD, 1) + pltpu.roll(edge_high, 2 * PAD, 1)
        left = jnp.concatenate([high, low, high, edge.astype(BF16)], axis=1)
        total = None
        for n in range(0, WIDE, 256):
            width = min(256, WIDE - n)
            tall[t, :, n : n + width] = jnp.dot(
                left, gather_w[t, :, n : n + width], preferred_element_type=F32
            )
        for u in range(KSIZE):
            piece = tall[t, pl.ds(u, ROWS), u * TILE : (u + 1) * TILE]
            total = piece if total is None else total + piece
        return total

    def pack(strip, rows):
        out = None
        for k in range(strip.shape[0] // rows):
            part = strip[rows * k : rows * k + rows]
            part = jnp.where(lane[0:rows] < 2 * RIM, part, 0.0)
            part = pltpu.roll(part, 2 * RIM * k, 1) if k else part
            out = part if out is None else out + part
        return out

    def unpack(packed, groups):
        parts = []
        for k in range(groups):
            part = pltpu.roll(packed, TILE - 2 * RIM * k, 1) if k else packed
            parts.append(jnp.where(lane[0 : packed.shape[0]] < 2 * RIM, part, 0.0))
        return jnp.concatenate(parts, axis=0)

    def start_exchange():
        side = iota((EXT_ROWS, TILE), 1)
        right = jnp.where(side >= TILE - RIM, spill[:, TILE : 2 * TILE], spill[:, 2 * TILE :])
        strips[0] = spill[:, 0:TILE]
        strips[1] = pltpu.roll(right, RIM, 1)
        for i in range(2):
            send_side[i, 0:24] = pack(strips[i], 24)
            send_side[i, 24:] = kernels
            send_up_corner[i, 0:8] = pack(strips[i, 0:24], 8)
            send_up_corner[i, 8:] = kernels
            send_down_corner[i, 0:8] = pack(strips[i, 118:142], 8)
            send_down_corner[i, 8:] = kernels
        for send, at in ((send_up, 0), (send_down, 118)):
            for t in range(2):
                tile = slice(t * TILE, (t + 1) * TILE)
                send[16 * t : 16 * t + 16] = spill[at : at + 16, tile]
                send[32 + 4 * t : 36 + 4 * t] = spill[at + 16 : at + 20, tile]
            send[40:48] = pack(spill[at : at + 24, 2 * TILE :], 8)
            send[48:] = kernels
        plan = {
            (-1, 1): (send_up_corner.at[1], got_up_corner.at[1]),
            (1, -1): (send_down_corner.at[0], got_down_corner.at[0]),
            (-1, -1): (send_up_corner.at[0], got_up_corner.at[0]),
            (1, 1): (send_down_corner.at[1], got_down_corner.at[1]),
            (-1, 0): (send_up, got_up),
            (1, 0): (send_down, got_down),
            (0, -1): (send_side.at[0], got_side.at[0]),
            (0, 1): (send_side.at[1], got_side.at[1]),
        }
        return [
            pltpu.make_async_remote_copy(
                src_ref=source,
                dst_ref=target,
                send_sem=halo_send.at[i],
                recv_sem=halo_recv.at[i],
                device_id=neighbour(*d),
                device_id_type=MESH,
            )
            for i, (d, (source, target)) in enumerate(plan.items())
        ]

    above = jnp.where(rng > 0, 1.0, 0.0)
    below = jnp.where(rng < 15, 1.0, 0.0)
    left_of = jnp.where(azi > 0, 1.0, 0.0)
    right_of = jnp.where(azi < 31, 1.0, 0.0)

    def prepare_frames():
        for t in range(2):
            for at, got, flag, low_row, shift in ((0, got_down, above, 6, 6), (2, got_up, below, 0, -RIM)):
                flat_w[at + t] = flat_gather_weights(
                    got[52 + t : 53 + t] * flag, low_row, low_row + RIM, lines.at[at + t]
                )
                flat_w[4 + at + t] = flat_spread_weights(
                    got[54 + t : 55 + t] * flag, shift, lines.at[4 + at + t]
                )
        side_w[0] = side_gather_weights(*side_kernels(2)[1])
        side_w[1] = side_spread_weights(*side_kernels(0)[1])

    def assemble(corners):
        first, last = slice(0, TILE), slice(2 * TILE, EXT_COLS)
        tall_field[0:PAD] = jnp.zeros((PAD, EXT_COLS), F32)
        tall_field[PAD : PAD + EXT_ROWS] = spill[...]
        tall_field[PAD + EXT_ROWS :] = jnp.zeros((PAD, EXT_COLS), F32)
        for got, at, flag in ((got_down, 6, above), (got_up, 144, below)):
            for t in range(2):
                tile = slice(t * TILE, (t + 1) * TILE)
                tall_field[at : at + 16, tile] += got[16 * t : 16 * t + 16] * flag
                tall_field[at + 16 : at + 20, tile] += got[32 + 4 * t : 36 + 4 * t] * flag
            tall_field[at : at + 24, last] += unpack(got[40:48], 3) * flag

        def from_left(strip, rows, flag):
            strip = pltpu.roll(strip, TILE - RIM, 1) * flag
            near = iota(strip.shape, 1) < TILE // 2
            tall_field[rows, first] += jnp.where(near, strip, 0.0)
            tall_field[rows, last] += jnp.where(near, 0.0, strip)

        def from_right(strip, rows, flag):
            tall_field[rows, last] += strip * flag

        middle, top, bottom = slice(16, 160), slice(6, 30), slice(144, 168)
        from_right(unpack(got_side[0, 0:24], 6), middle, right_of)
        from_left(unpack(got_side[1, 0:24], 6), middle, left_of)
        for copy in corners:
            copy.wait()
        from_right(unpack(got_down_corner[0, 0:8], 3), top, above * right_of)
        from_left(unpack(got_down_corner[1, 0:8], 3), top, above * left_of)
        from_right(unpack(got_up_corner[0, 0:8], 3), bottom, below * right_of)
        from_left(unpack(got_up_corner[1, 0:8], 3), bottom, below * left_of)
        r, c = iota((TALL_ROWS, EXT_COLS), 0), iota((TALL_ROWS, EXT_COLS), 1)
        inside = (
            (r >= jnp.where(rng == 0, PAD + RADIUS, 0))
            & (r < jnp.where(rng == 15, PAD + RADIUS + ROWS, TALL_ROWS))
            & (c >= jnp.where(azi == 0, RADIUS, 0))
            & (c < jnp.where(azi == 0, 320, EXT_COLS))
            & ((c < jnp.where(azi == 31, RADIUS + COLS, EXT_COLS)) | (c >= 320))
        )
        tall_field[...] = jnp.where(inside, tall_field[...], 0.0)

    def side_kernels(k):
        return tuple(
            (got[1, at + 1 + k : at + 2 + k] * (flag * left_of), got[0, at + k : at + 1 + k] * (flag * right_of))
            for got, at, flag in ((got_down_corner, 8, above), (got_side, 24, 1.0), (got_up_corner, 8, below))
        )

    def side_frames():
        fields = side_fields(tall_field[:, 0:TILE], tall_field[:, 2 * TILE :])
        parts = ((0, 32, 144, 16), (16, 144, 0, 128), (144, 32, 176, 16))
        group = band_group(iota((1, COLS), 1) & (TILE - 1))
        sums = []
        for (start, count, at, rows), (left, right) in zip(parts, side_kernels(2)):
            side_out[at : at + count] = jnp.dot(
                fields[start : start + count],
                side_w[0] if start == PAD else side_gather_weights(left, right),
                preferred_element_type=F32,
            )
            total = jnp.zeros((rows, COLS), F32)
            for u in range(KSIZE):
                total = jnp.where(group == KSIZE - 1 - u, side_out[at + u : at + u + rows], total)
            sums.append(total)
        frames = picked(jnp.concatenate(sums, axis=0), pick_near[...])
        r = iota(frames.shape, 0)
        return jnp.where((r >= 6) & (r < 154), frames, 0.0)

    def side_spread(frames):
        high, low = split_rows(frames)
        packed = (high + pltpu.roll(low, 24, 1) + pltpu.roll(high, 48, 1)).astype(BF16)
        for (start, stop), (left, right) in zip(((0, 16), (16, 144), (144, 160)), side_kernels(0)):
            side_back[start:stop] = jnp.dot(
                packed[start:stop],
                side_w[1] if start == PAD else side_spread_weights(left, right),
                preferred_element_type=F32,
            )
        group = band_group(iota((1, COLS), 1) & (TILE - 1))
        total = jnp.zeros((EXT_ROWS, COLS), F32)
        for u in range(KSIZE):
            total = jnp.where(group == u, side_back[PAD - u : PAD - u + EXT_ROWS], total)
        out = picked(total, pick_apart[...])
        return out[:, 0:TILE], out[:, TILE:]

    def flat_frames(rows, at):
        high, low = halves(tall_field[rows, :])
        right = jnp.concatenate([high, low, high, jnp.zeros((32, EXT_COLS), BF16)], axis=0)
        tiles = []
        for t in range(2):
            out = jnp.dot(
                flat_w[at + t],
                right[:, t * TILE : t * TILE + COLS],
                preferred_element_type=F32,
            )
            total = out[0:PAD]
            for v in range(1, KSIZE):
                total = total + pltpu.roll(out[PAD * v : PAD * v + PAD], COLS - v, 1)
            tiles.append(total[:, 0:TILE])
        return tiles

    def flat_spread(tiles, at):
        outs = []
        for t in range(2):
            high, low = halves(tiles[t])
            gap = jnp.zeros((PAD, TILE), BF16)
            right = jnp.concatenate([high, gap, low, gap, high, gap, gap, gap], axis=0)
            out = jnp.dot(flat_w[at + t], right, preferred_element_type=F32)
            near, far = out[0:PAD], None
            for v in range(1, KSIZE):
                piece = pltpu.roll(out[PAD * v : PAD * v + PAD], v, 1)
                past = edge_lane < v
                near = near + jnp.where(past, 0.0, piece)
                piece = jnp.where(past, piece, 0.0)
                far = piece if far is None else far + piece
            total = jnp.concatenate([near, far], axis=1)
            outs.append(total)
        return outs

    def inner(x, y):
        z = x * y
        z = z[:, 0:TILE] + z[:, TILE:]
        while z.shape[0] > 8:
            half = z.shape[0] // 2
            z = z[0:half] + z[half:]
        return jnp.sum(jnp.sum(z, axis=0, keepdims=True), axis=1, keepdims=True)

    def inner_rimmed(x, y):
        r, c = iota((EXT_ROWS, EXT_COLS), 0), iota((EXT_ROWS, EXT_COLS), 1)
        own = (r >= RADIUS) & (r < ROWS + RADIUS) & (c >= RADIUS) & (c < COLS + RADIUS)
        z = jnp.where(own, x * y, 0.0)
        z = z[:, 0:TILE] + z[:, TILE : 2 * TILE] + z[:, 2 * TILE :]
        z = z[0:72] + z[72:]
        z = (z[0:24] + z[24:48]) + z[48:72]
        z = (z[0:8] + z[8:16]) + z[16:24]
        return jnp.sum(jnp.sum(z, axis=0, keepdims=True), axis=1, keepdims=True)

    def own_block(source, row):
        shifted[...] = pltpu.roll(source[row : row + EXT_ROWS, :], EXT_COLS - RADIUS, 1)[:, 0:COLS]
        return shifted[pl.ds(RADIUS, ROWS), :]

    load_obs.wait()
    spread(obs_ref[...], spill)
    copies = start_exchange()
    pl.semaphore_wait(barrier, len(partners))
    for copy in copies:
        copy.start()
    build_gather()
    for copy in copies[4:]:
        copy.wait()
    prepare_frames()
    assemble(copies[:4])
    for t in range(2):
        image[0, :, t * TILE : (t + 1) * TILE] = gather(tall_field, PAD, t)
    frames = side_frames()
    frames_top = flat_frames(slice(0, 32), 0)
    frames_bottom = flat_frames(slice(144, 176), 2)
    spread(image[0], field)
    to_left, to_right = side_spread(frames)
    field[:, 0:TILE] += to_left
    field[:, 2 * TILE :] += to_right
    for t, out in enumerate(flat_spread(frames_top, 4)):
        field[0:PAD, t * TILE : t * TILE + COLS] += out
    for t, out in enumerate(flat_spread(frames_bottom, 6)):
        field[ROWS:, t * TILE : t * TILE + COLS] += out
    r, c = iota((EXT_ROWS, EXT_COLS), 0), iota((EXT_ROWS, EXT_COLS), 1)
    inside = (
        (r >= jnp.where(rng == 0, RADIUS, 0))
        & (r < jnp.where(rng == 15, ROWS + RADIUS, EXT_ROWS))
        & (c >= jnp.where(azi == 0, RADIUS, 0))
        & (c < jnp.where(azi == 31, COLS + RADIUS, EXT_COLS))
    )
    field[...] = jnp.where(inside, field[...], 0.0)
    for t in range(2):
        image[1, :, t * TILE : (t + 1) * TILE] = gather(field, 0, t)
    store_image = pltpu.make_async_copy(image, image_hbm, load.at[1])
    store_image.start()
    first = tall_field[PAD : PAD + EXT_ROWS, :]
    second = field[...]
    sums = [inner_rimmed(first, first), inner(image[0], image[0])]
    sums += [inner_rimmed(second, second), inner_rimmed(first, second)]
    sums += [inner(image[1], image[1]), inner(image[0], image[1])]
    line = lane[0:1]
    moments[0] = sum(jnp.where(line == i, x, 0.0) for i, x in enumerate(sums))
    for phase, got in enumerate((got_a, got_b)):
        for i, o in enumerate(OFFSETS[phase]):
            pltpu.make_async_remote_copy(
                src_ref=moments.at[phase],
                dst_ref=got.at[i],
                send_sem=sum_send.at[phase],
                recv_sem=sum_recv.at[phase],
                device_id=member(o),
                device_id_type=MESH,
            ).start()
        if phase == 0:
            grad[0] = own_block(tall_field, PAD)
            grad[1] = own_block(field, 0)
            store_grad = pltpu.make_async_copy(grad, grad_hbm, load.at[0])
            store_grad.start()
        pltpu.make_async_copy(got, got, sum_recv.at[phase]).wait()
        moments[phase + 1] = moments[phase] + jnp.sum(got[...], axis=0)
    total = moments[2]
    gg, qq, ww, gw, pp, qp = (total[:, i : i + 1] for i in range(6))
    alpha = gg / qq
    gamma_1 = (gg - alpha * gw) - alpha * (gw - alpha * ww)
    rise = 1.0 + gamma_1 / gg
    delta_1 = rise * (rise * qq - alpha * qp) - alpha * (rise * qp - alpha * pp)
    alpha_1 = gamma_1 / delta_1
    near = alpha + alpha_1 * rise
    far = alpha * alpha_1
    factors[...] = jnp.where(line == 0, near, far)
    for phase, got in enumerate((got_a, got_b)):
        pltpu.make_async_copy(got, got, sum_send.at[phase]).wait()
    store_grad.wait()
    store_image.wait()


def finish(grad_hbm, image_hbm, obs_hbm, factors_hbm, est_hbm, res_hbm, grad, image, obs, factors, sems):
    ins = ((factors_hbm, factors), (grad_hbm, grad), (image_hbm, image), (obs_hbm, obs))
    loads = [pltpu.make_async_copy(a, b, sems.at[i]) for i, (a, b) in enumerate(ins)]
    for load in loads:
        load.start()
    loads[0].wait()
    loads[1].wait()
    near, far = factors[:, 0:1], factors[:, 1:2]
    grad[0] = near * grad[0] - far * grad[1]
    store_est = pltpu.make_async_copy(grad.at[0], est_hbm, sems.at[4])
    store_est.start()
    loads[2].wait()
    loads[3].wait()
    image[0] = obs[...] - near * image[0] + far * image[1]
    store_res = pltpu.make_async_copy(image.at[0], res_hbm, sems.at[5])
    store_res.start()
    store_est.wait()
    store_res.wait()


def body(observed, psf_tiles):
    pair = jax.ShapeDtypeStruct((2, ROWS, COLS), F32)
    hbm = pl.BlockSpec(memory_space=pltpu.HBM)
    grads, images, factors = pl.pallas_call(
        kernel,
        out_shape=(pair, pair, jax.ShapeDtypeStruct((1, TILE), F32)),
        in_specs=[hbm, hbm],
        out_specs=(hbm, hbm, pl.BlockSpec(memory_space=pltpu.VMEM)),
        scratch_shapes=[
            pltpu.VMEM((ROWS, COLS), F32),
            pltpu.VMEM((1, 2, KSIZE * KSIZE), F32),
            pltpu.VMEM((8, TILE), F32),
            pltpu.VMEM((2, 3 * TILE, WIDE + TILE), BF16),
            pltpu.VMEM((2, 4 * TILE, WIDE + TILE), BF16),
            pltpu.VMEM((2, ROWS + 2 * PAD, WIDE + TILE), F32),
            pltpu.VMEM((2, EXT_ROWS, WIDE), F32),
            pltpu.VMEM((EXT_ROWS, EXT_COLS), F32),
            pltpu.VMEM((TALL_ROWS, EXT_COLS), F32),
            pltpu.VMEM((EXT_ROWS, EXT_COLS), F32),
            pltpu.VMEM((2, ROWS, COLS), F32),
            pltpu.VMEM((2, ROWS, COLS), F32),
            pltpu.VMEM((EXT_ROWS, COLS), F32),
            pltpu.VMEM((2, EXT_ROWS, TILE), F32),
            pltpu.VMEM((2, 32, TILE), F32),
            pltpu.VMEM((56, TILE), F32),
            pltpu.VMEM((56, TILE), F32),
            pltpu.VMEM((2, 16, TILE), F32),
            pltpu.VMEM((2, 16, TILE), F32),
            pltpu.VMEM((2, 32, TILE), F32),
            pltpu.VMEM((56, TILE), F32),
            pltpu.VMEM((56, TILE), F32),
            pltpu.VMEM((2, 16, TILE), F32),
            pltpu.VMEM((2, 16, TILE), F32),
            pltpu.VMEM((208, COLS), F32),
            pltpu.VMEM((160, COLS), F32),
            pltpu.VMEM((8, PAD, TILE), F32),
            pltpu.VMEM((8, GROUPS, TILE), BF16),
            pltpu.VMEM((2, TILE, COLS), BF16),
            pltpu.VMEM((4 * TILE, COLS), BF16),
            pltpu.VMEM((4 * TILE, TILE), BF16),
            pltpu.VMEM((3, 1, TILE), F32),
            pltpu.VMEM((len(OFFSETS[0]), 1, TILE), F32),
            pltpu.VMEM((len(OFFSETS[1]), 1, TILE), F32),
            pltpu.SemaphoreType.DMA((8,)),
            pltpu.SemaphoreType.DMA((8,)),
            pltpu.SemaphoreType.DMA((2,)),
            pltpu.SemaphoreType.DMA((2,)),
            pltpu.SemaphoreType.DMA((2,)),
        ],
        compiler_params=pltpu.CompilerParams(
            collective_id=0, has_side_effects=True, vmem_limit_bytes=61 << 20
        ),
    )(observed, psf_tiles)
    block = jax.ShapeDtypeStruct((ROWS, COLS), F32)
    return pl.pallas_call(
        finish,
        out_shape=(block, block),
        in_specs=[pl.BlockSpec(memory_space=pltpu.HBM)] * 4,
        out_specs=(pl.BlockSpec(memory_space=pltpu.HBM),) * 2,
        scratch_shapes=[
            pltpu.VMEM((2, ROWS, COLS), F32),
            pltpu.VMEM((2, ROWS, COLS), F32),
            pltpu.VMEM((ROWS, COLS), F32),
            pltpu.VMEM((1, TILE), F32),
            pltpu.SemaphoreType.DMA((6,)),
        ],
        compiler_params=pltpu.CompilerParams(vmem_limit_bytes=61 << 20),
    )(grads, images, observed, factors)


def solution(mesh):
    return jax.shard_map(
        body,
        mesh=mesh,
        in_specs=(P("rng", "azi"), P("rng", "azi", None)),
        out_specs=(P("rng", "azi"), P("rng", "azi")),
        check_vma=False,
    )
```

```python
import itertools

import jax
import jax.numpy as jnp
from jax import lax
from jax.experimental import pallas as pl
from jax.experimental.pallas import tpu as pltpu
from jax.sharding import PartitionSpec as P

TILE = 128
KSIZE = 11
RADIUS = 5
RIM = 2 * RADIUS
ROWS = 128
COLS = 256
EXT_ROWS = 144
EXT_COLS = 384
TALL_ROWS = 176
PAD = 16
GROUPS = KSIZE * PAD
WIDE = KSIZE * TILE
MESH = pl.DeviceIdType.MESH
F32 = jnp.float32
BF16 = jnp.bfloat16

PARTS = {"x": 4, "y": 4, "z": 16, "c": 2}
PHASES = (("x", "y", "c"), ("z",))
NEIGHBOURS = tuple(
    (dr, da) for dr in (-1, 0, 1) for da in (-1, 0, 1) if (dr, da) != (0, 0)
)


def group_offsets(axes):
    ranges = [range(PARTS[axis]) for axis in axes]
    offsets = [dict(zip(axes, o)) for o in itertools.product(*ranges) if any(o)]
    return sorted(
        offsets,
        key=lambda o: -sum(min(n, PARTS[a] - n) for a, n in o.items() if a != "c"),
    )


OFFSETS = tuple(group_offsets(axes) for axes in PHASES)


def band_group(n):
    return (n * 373) >> 12


def split_rows(x):
    high = x.astype(BF16).astype(F32)
    return high, x - high


def iota(shape, dim):
    return lax.broadcasted_iota(jnp.int32, shape, dim)


def orders(taps):
    a, b = iota((TILE, TILE), 0), iota((TILE, TILE), 1)
    last = KSIZE * KSIZE - 1

    def turned(n):
        return KSIZE * (n - KSIZE * band_group(n)) + band_group(n)

    back = last - b
    wanted = (back, turned(b), jnp.where(back >= 0, turned(jnp.maximum(back, 0)), -1))
    pick = [jnp.where((a == w) & (b <= last), 1.0, 0.0).astype(BF16) for w in wanted]
    first = taps.astype(BF16)
    rest = taps - first.astype(F32)
    second = rest.astype(BF16)
    third = (rest - second.astype(F32)).astype(BF16)
    parts = jnp.concatenate([first, second, third], axis=1)
    out = [taps]
    for p in pick:
        out.append(jnp.dot(parts, jnp.concatenate([p] * 3, axis=0), preferred_element_type=F32))
    row = iota((8, TILE), 0)
    total = out[0]
    for k in range(1, 4):
        total = jnp.where((row >= 2 * k) & (row < 2 * k + 2), pltpu.roll(out[k], 2 * k, 0), total)
    return total


def sloped(line, shift, rows):
    base = pltpu.roll(jnp.broadcast_to(line, (8, TILE)), shift, 1)
    return pltpu.roll(jnp.concatenate([base] * (rows // 8), axis=0), 0, 1, stride=1, stride_axis=0)


def side_gather_weights(left, right):
    i, n = iota((40, TILE), 0), iota((40, TILE), 1)
    j = n - KSIZE * band_group(n)
    halves_ = []
    for kernel_row, start in ((left, 0), (right, 20)):
        band = sloped(kernel_row, TILE - RIM - start, 40)
        c = i - start
        keep = (c >= 0) & (c < 20) & (j < RIM) & (n < 121) & (c - j >= 0) & (c - j < KSIZE)
        halves_.append(jnp.where(keep, band, 0.0))
    high, low = split_rows(jnp.concatenate(halves_, axis=1))
    return jnp.concatenate([high, high, low, jnp.zeros((8, COLS), F32)], axis=0).astype(BF16)


def side_spread_weights(left, right):
    i, n = iota((24, TILE), 0), iota((24, TILE), 1)
    c = n - KSIZE * band_group(n)
    valid = (c < RIM) & (n < 121)
    halves_ = []
    for kernel_row, keep in (
        (left, valid & (i < RIM) & (c <= i)),
        (right, valid & (i >= RIM) & (i < 2 * RIM) & (c >= i - RIM)),
    ):
        band = sloped(kernel_row, TILE - RIM, 24)
        halves_.append(jnp.where(keep, band, 0.0))
    high, low = split_rows(jnp.concatenate(halves_, axis=1))
    return jnp.concatenate([high, high, low, jnp.zeros((TILE - 72, COLS), F32)], axis=0).astype(BF16)


def flat_bands(kernel_row, order, shift, lines):
    lane = iota((PAD, TILE), 1)
    last = KSIZE * (KSIZE - 1)
    base = pltpu.roll(jnp.broadcast_to(kernel_row, (8, TILE)), TILE - last, 1)
    taps = jnp.concatenate(
        [
            pltpu.roll(x, 0, 1, stride=KSIZE, stride_axis=0)
            for x in (base, pltpu.roll(base, 8 * KSIZE, 1))
        ],
        axis=0,
    )
    high, low = split_rows(jnp.where(lane < KSIZE, taps, 0.0))
    taps = high + pltpu.roll(high, 32, 1) + pltpu.roll(low, 64, 1)
    lines[...] = pltpu.roll(taps, shift % TILE, 1) if shift else taps
    blocks = []
    for v in order:
        line = jnp.broadcast_to(lines[v : v + 1, :], (8, TILE))
        line = pltpu.roll(line, 0, 1, stride=1, stride_axis=0)
        blocks += [line, pltpu.roll(line, 8, 1)]
    return jnp.concatenate(blocks, axis=0)


def flat_gather_weights(kernel_row, low_row, high_row, lines):
    band = flat_bands(kernel_row, range(KSIZE - 1, -1, -1), 0, lines)
    r = iota((GROUPS, TILE), 0) & (PAD - 1)
    return jnp.where((r >= low_row) & (r < high_row), band, 0.0).astype(BF16)


def flat_spread_weights(kernel_row, shift, lines):
    band = flat_bands(kernel_row, range(KSIZE), shift, lines)
    lane = iota((GROUPS, TILE), 1)
    keep = ((lane & 31) < PAD) & (lane < 96)
    return jnp.where(keep, band, 0.0).astype(BF16)


def side_fields(near, far):
    lane = iota(near.shape, 1)
    left = jnp.where(lane >= TILE - RIM, far, jnp.where(lane < RIM, near, 0.0))
    right = jnp.where(lane < 20, far, 0.0)
    x = pltpu.roll(left, RIM, 1) + pltpu.roll(right, 20, 1)
    high, low = split_rows(x)
    return (high + pltpu.roll(low, 40, 1) + pltpu.roll(high, 80, 1)).astype(BF16)


def picker(places, width):
    n = iota((TILE, width), 0)
    j = n - KSIZE * band_group(n)
    lane = iota((TILE, width), 1)
    blocks = [
        jnp.where((j < RIM) & (n < 121) & (lane == j + place), 1.0, 0.0).astype(BF16)
        for place in places
    ]
    return jnp.concatenate(blocks * 2, axis=0)


def picked(x, matrix):
    high, low = halves(x)
    return jnp.dot(jnp.concatenate([high, low], axis=1), matrix, preferred_element_type=F32)


def halves(x):
    high = x.astype(BF16)
    low = (x - high.astype(F32)).astype(BF16)
    return high, low


def kernel(
    obs_hbm,
    psf_hbm,
    grad_hbm,
    image_hbm,
    factors,
    obs_ref,
    psf_ref,
    taps,
    spread_w,
    gather_w,
    wide,
    tall,
    spill,
    tall_field,
    field,
    image,
    grad,
    shifted,
    strips,
    send_side,
    send_up,
    send_down,
    send_up_corner,
    send_down_corner,
    got_side,
    got_up,
    got_down,
    got_up_corner,
    got_down_corner,
    side_out,
    side_back,
    lines,
    flat_w,
    side_w,
    pick_apart,
    pick_near,
    moments,
    got_a,
    got_b,
    halo_send,
    halo_recv,
    sum_send,
    sum_recv,
    load,
):
    rng = lax.axis_index("rng")
    azi = lax.axis_index("azi")
    place = {
        "x": azi // 8,
        "y": rng // 4,
        "z": (rng % 4) * 4 + (azi // 2) % 4,
        "c": azi % 2,
    }

    def member(offset):
        at = {
            axis: lax.rem(place[axis] + offset[axis], PARTS[axis])
            if axis in offset
            else place[axis]
            for axis in PARTS
        }
        return (at["y"] * 4 + at["z"] // 4, at["x"] * 8 + (at["z"] % 4) * 2 + at["c"])

    def neighbour(dr, da):
        return (lax.rem(rng + dr + 16, 16), lax.rem(azi + da + 32, 32))

    barrier = pltpu.get_barrier_semaphore()
    partners = [neighbour(*d) for d in NEIGHBOURS]
    partners += [member(o) for offsets in OFFSETS for o in offsets]
    for partner in partners:
        pl.semaphore_signal(barrier, inc=1, device_id=partner, device_id_type=MESH)
    load_psf = pltpu.make_async_copy(psf_hbm, psf_ref, load.at[0])
    load_obs = pltpu.make_async_copy(obs_hbm, obs_ref, load.at[1])
    load_psf.start()
    load_obs.start()

    lane = lax.broadcasted_iota(jnp.int32, (TILE, TILE), 1)
    row = lax.broadcasted_iota(jnp.int32, (TILE, TILE), 0)

    edge_lane, edge_row = lane[0:PAD], row[0:PAD]

    def band(line, shift, back):
        line = pltpu.roll(jnp.broadcast_to(line, (8, TILE)), lax.rem(3 * TILE - shift, TILE), 1)
        line = jnp.where(lane[0:8] < KSIZE, line, 0.0)
        line = pltpu.roll(line, back, 1) if back else line
        line = pltpu.roll(line, 0, 1, stride=1, stride_axis=0)
        rows = [pltpu.roll(line, 8 * g, 1) if g else line for g in range(TILE // 8)]
        return jnp.concatenate(rows, axis=0)

    def build_spread():
        def one(u, packed):
            block = pl.ds(pl.multiple_of(u * TILE, TILE), TILE)
            used = jnp.where(u < KSIZE, 1.0, 0.0)
            out = []
            for t in range(2):
                rows = band(taps[t : t + 1, :], KSIZE * u, 0)
                edge = rows[TILE - PAD :]
                below = edge_lane < edge_row + (TILE - PAD)
                over = jnp.where(below, edge, 0.0) * used
                out.append(packed[t] + pltpu.roll(over, lax.rem(KSIZE * u, TILE), 1))
                main = jnp.concatenate([rows[0 : TILE - PAD], jnp.where(below, 0.0, edge)], axis=0)
                high, low = halves(main)
                spread_w[t, 0:TILE, block] = high
                spread_w[t, TILE : 2 * TILE, block] = high
                spread_w[t, 2 * TILE :, block] = low
            return tuple(out)

        def six(i, packed):
            for k in range(6):
                packed = one(6 * i + k, packed)
            return packed

        packed = lax.fori_loop(0, 2, six, (jnp.zeros((PAD, TILE), F32),) * 2)
        blank = jnp.zeros((TILE - PAD, TILE), BF16)
        for t in range(2):
            high, low = (jnp.concatenate([blank, p], axis=0) for p in halves(packed[t]))
            spread_w[t, 0:TILE, WIDE:] = high
            spread_w[t, TILE : 2 * TILE, WIDE:] = high
            spread_w[t, 2 * TILE :, WIDE:] = low

    def build_gather():
        gather_w[:, 3 * TILE + 3 * PAD :, :] = jnp.zeros((2, TILE - 3 * PAD, WIDE + TILE), BF16)

        def one(u, carry):
            block = pl.ds(pl.multiple_of(u * TILE, TILE), TILE)
            for t in range(2):
                rows = band(taps[2 + t : 3 + t, :], KSIZE * (KSIZE - 1) - KSIZE * u, TILE - RIM)
                edge = rows[0:PAD]
                past = edge_lane > edge_row
                high, low = halves(jnp.where(past, edge, 0.0))
                gather_w[t, 3 * TILE : 3 * TILE + PAD, block] = high
                gather_w[t, 3 * TILE + PAD : 3 * TILE + 2 * PAD, block] = high
                gather_w[t, 3 * TILE + 2 * PAD : 3 * TILE + 3 * PAD, block] = low
                main = jnp.concatenate([jnp.where(past, 0.0, edge), rows[PAD:]], axis=0)
                high, low = halves(main)
                gather_w[t, 0:TILE, block] = high
                gather_w[t, TILE : 2 * TILE, block] = high
                gather_w[t, 2 * TILE : 3 * TILE, block] = low
            return carry

        def six(i, carry):
            for k in range(6):
                one(6 * i + k, carry)
            return carry

        lax.fori_loop(0, 2, six, 0)

    pick_apart[...] = picker((0, TILE), COLS)
    pick_near[...] = picker((0, RIM), TILE)
    load_psf.wait()
    taps[...] = jnp.zeros_like(taps)
    taps[0:2, 0 : KSIZE * KSIZE] = psf_ref[0]
    kernels = orders(taps[...])
    taps[...] = kernels
    build_spread()
    wide[:, 0:PAD, :] = jnp.zeros((2, PAD, WIDE + TILE), F32)
    wide[:, PAD + ROWS :, :] = jnp.zeros((2, PAD, WIDE + TILE), F32)

    def spread(source, out):
        group = band_group(iota((1, TILE), 1))
        spares = []
        for t in range(2):
            high, low = halves(source[:, t * TILE : (t + 1) * TILE])
            left = jnp.concatenate([high, low, high], axis=1)
            for n in range(0, WIDE + TILE, 256):
                wide[t, PAD : PAD + ROWS, n : n + 256] = jnp.dot(
                    left, spread_w[t, :, n : n + 256], preferred_element_type=F32
                )
            total, spare = None, jnp.zeros((EXT_ROWS, TILE), F32)
            for u in range(KSIZE):
                rows = pl.ds(PAD - u, EXT_ROWS)
                piece = wide[t, rows, u * TILE : (u + 1) * TILE]
                total = piece if total is None else total + piece
                spare = jnp.where(group == u, wide[t, rows, WIDE:], spare)
            out[:, t * TILE : (t + 1) * TILE] = total
            spares.append(spare)
        over = picked(jnp.concatenate(spares, axis=1), pick_apart[...])
        out[:, TILE : 2 * TILE] += over[:, 0:TILE]
        out[:, 2 * TILE :] = over[:, TILE:]

    def gather(source, row, t):
        tall_lane = lax.broadcasted_iota(jnp.int32, (EXT_ROWS, TILE), 1)
        high, low = halves(source[row : row + EXT_ROWS, t * TILE : (t + 1) * TILE])
        edge = source[row : row + EXT_ROWS, (t + 1) * TILE : (t + 2) * TILE]
        edge = jnp.where(tall_lane < RIM, edge, 0.0)
        edge_high = edge.astype(BF16).astype(F32)
        edge_low = edge - edge_high
        edge = edge_high + pltpu.roll(edge_low, PAD, 1) + pltpu.roll(edge_high, 2 * PAD, 1)
        left = jnp.concatenate([high, low, high, edge.astype(BF16)], axis=1)
        total = None
        for n in range(0, WIDE, 256):
            width = min(256, WIDE - n)
            tall[t, :, n : n + width] = jnp.dot(
                left, gather_w[t, :, n : n + width], preferred_element_type=F32
            )
        for u in range(KSIZE):
            piece = tall[t, pl.ds(u, ROWS), u * TILE : (u + 1) * TILE]
            total = piece if total is None else total + piece
        return total

    def pack(strip, rows):
        out = None
        for k in range(strip.shape[0] // rows):
            part = strip[rows * k : rows * k + rows]
            part = jnp.where(lane[0:rows] < 2 * RIM, part, 0.0)
            part = pltpu.roll(part, 2 * RIM * k, 1) if k else part
            out = part if out is None else out + part
        return out

    def unpack(packed, groups):
        parts = []
        for k in range(groups):
            part = pltpu.roll(packed, TILE - 2 * RIM * k, 1) if k else packed
            parts.append(jnp.where(lane[0 : packed.shape[0]] < 2 * RIM, part, 0.0))
        return jnp.concatenate(parts, axis=0)

    def start_exchange():
        side = iota((EXT_ROWS, TILE), 1)
        right = jnp.where(side >= TILE - RIM, spill[:, TILE : 2 * TILE], spill[:, 2 * TILE :])
        strips[0] = spill[:, 0:TILE]
        strips[1] = pltpu.roll(right, RIM, 1)
        for i in range(2):
            send_side[i, 0:24] = pack(strips[i], 24)
            send_side[i, 24:] = kernels
            send_up_corner[i, 0:8] = pack(strips[i, 0:24], 8)
            send_up_corner[i, 8:] = kernels
            send_down_corner[i, 0:8] = pack(strips[i, 118:142], 8)
            send_down_corner[i, 8:] = kernels
        for send, at in ((send_up, 0), (send_down, 118)):
            for t in range(2):
                tile = slice(t * TILE, (t + 1) * TILE)
                send[16 * t : 16 * t + 16] = spill[at : at + 16, tile]
                send[32 + 4 * t : 36 + 4 * t] = spill[at + 16 : at + 20, tile]
            send[40:48] = pack(spill[at : at + 24, 2 * TILE :], 8)
            send[48:] = kernels
        plan = {
            (-1, 1): (send_up_corner.at[1], got_up_corner.at[1]),
            (1, -1): (send_down_corner.at[0], got_down_corner.at[0]),
            (-1, -1): (send_up_corner.at[0], got_up_corner.at[0]),
            (1, 1): (send_down_corner.at[1], got_down_corner.at[1]),
            (-1, 0): (send_up, got_up),
            (1, 0): (send_down, got_down),
            (0, -1): (send_side.at[0], got_side.at[0]),
            (0, 1): (send_side.at[1], got_side.at[1]),
        }
        return [
            pltpu.make_async_remote_copy(
                src_ref=source,
                dst_ref=target,
                send_sem=halo_send.at[i],
                recv_sem=halo_recv.at[i],
                device_id=neighbour(*d),
                device_id_type=MESH,
            )
            for i, (d, (source, target)) in enumerate(plan.items())
        ]

    above = jnp.where(rng > 0, 1.0, 0.0)
    below = jnp.where(rng < 15, 1.0, 0.0)
    left_of = jnp.where(azi > 0, 1.0, 0.0)
    right_of = jnp.where(azi < 31, 1.0, 0.0)

    def prepare_frames():
        for t in range(2):
            for at, got, flag, low_row, shift in ((0, got_down, above, 6, 6), (2, got_up, below, 0, -RIM)):
                flat_w[at + t] = flat_gather_weights(
                    got[52 + t : 53 + t] * flag, low_row, low_row + RIM, lines.at[at + t]
                )
                flat_w[4 + at + t] = flat_spread_weights(
                    got[54 + t : 55 + t] * flag, shift, lines.at[4 + at + t]
                )
        side_w[0] = side_gather_weights(*side_kernels(2)[1])
        side_w[1] = side_spread_weights(*side_kernels(0)[1])

    def assemble(corners):
        first, last = slice(0, TILE), slice(2 * TILE, EXT_COLS)
        tall_field[0:PAD] = jnp.zeros((PAD, EXT_COLS), F32)
        tall_field[PAD : PAD + EXT_ROWS] = spill[...]
        tall_field[PAD + EXT_ROWS :] = jnp.zeros((PAD, EXT_COLS), F32)
        for got, at, flag in ((got_down, 6, above), (got_up, 144, below)):
            for t in range(2):
                tile = slice(t * TILE, (t + 1) * TILE)
                tall_field[at : at + 16, tile] += got[16 * t : 16 * t + 16] * flag
                tall_field[at + 16 : at + 20, tile] += got[32 + 4 * t : 36 + 4 * t] * flag
            tall_field[at : at + 24, last] += unpack(got[40:48], 3) * flag

        def from_left(strip, rows, flag):
            strip = pltpu.roll(strip, TILE - RIM, 1) * flag
            near = iota(strip.shape, 1) < TILE // 2
            tall_field[rows, first] += jnp.where(near, strip, 0.0)
            tall_field[rows, last] += jnp.where(near, 0.0, strip)

        def from_right(strip, rows, flag):
            tall_field[rows, last] += strip * flag

        middle, top, bottom = slice(16, 160), slice(6, 30), slice(144, 168)
        from_right(unpack(got_side[0, 0:24], 6), middle, right_of)
        from_left(unpack(got_side[1, 0:24], 6), middle, left_of)
        for copy in corners:
            copy.wait_recv()
        from_right(unpack(got_down_corner[0, 0:8], 3), top, above * right_of)
        from_left(unpack(got_down_corner[1, 0:8], 3), top, above * left_of)
        from_right(unpack(got_up_corner[0, 0:8], 3), bottom, below * right_of)
        from_left(unpack(got_up_corner[1, 0:8], 3), bottom, below * left_of)
        r, c = iota((TALL_ROWS, EXT_COLS), 0), iota((TALL_ROWS, EXT_COLS), 1)
        inside = (
            (r >= jnp.where(rng == 0, PAD + RADIUS, 0))
            & (r < jnp.where(rng == 15, PAD + RADIUS + ROWS, TALL_ROWS))
            & (c >= jnp.where(azi == 0, RADIUS, 0))
            & (c < jnp.where(azi == 0, 320, EXT_COLS))
            & ((c < jnp.where(azi == 31, RADIUS + COLS, EXT_COLS)) | (c >= 320))
        )
        tall_field[...] = jnp.where(inside, tall_field[...], 0.0)

    def side_kernels(k):
        return tuple(
            (got[1, at + 1 + k : at + 2 + k] * (flag * left_of), got[0, at + k : at + 1 + k] * (flag * right_of))
            for got, at, flag in ((got_down_corner, 8, above), (got_side, 24, 1.0), (got_up_corner, 8, below))
        )

    def side_frames():
        fields = side_fields(tall_field[:, 0:TILE], tall_field[:, 2 * TILE :])
        parts = ((0, 32, 144, 16), (16, 144, 0, 128), (144, 32, 176, 16))
        group = band_group(iota((1, COLS), 1) & (TILE - 1))
        sums = []
        for (start, count, at, rows), (left, right) in zip(parts, side_kernels(2)):
            side_out[at : at + count] = jnp.dot(
                fields[start : start + count],
                side_w[0] if start == PAD else side_gather_weights(left, right),
                preferred_element_type=F32,
            )
            total = jnp.zeros((rows, COLS), F32)
            for u in range(KSIZE):
                total = jnp.where(group == KSIZE - 1 - u, side_out[at + u : at + u + rows], total)
            sums.append(total)
        frames = picked(jnp.concatenate(sums, axis=0), pick_near[...])
        r = iota(frames.shape, 0)
        return jnp.where((r >= 6) & (r < 154), frames, 0.0)

    def side_spread(frames):
        high, low = split_rows(frames)
        packed = (high + pltpu.roll(low, 24, 1) + pltpu.roll(high, 48, 1)).astype(BF16)
        for (start, stop), (left, right) in zip(((0, 16), (16, 144), (144, 160)), side_kernels(0)):
            side_back[start:stop] = jnp.dot(
                packed[start:stop],
                side_w[1] if start == PAD else side_spread_weights(left, right),
                preferred_element_type=F32,
            )
        group = band_group(iota((1, COLS), 1) & (TILE - 1))
        total = jnp.zeros((EXT_ROWS, COLS), F32)
        for u in range(KSIZE):
            total = jnp.where(group == u, side_back[PAD - u : PAD - u + EXT_ROWS], total)
        out = picked(total, pick_apart[...])
        return out[:, 0:TILE], out[:, TILE:]

    def flat_frames(rows, at):
        high, low = halves(tall_field[rows, :])
        right = jnp.concatenate([high, low, high, jnp.zeros((32, EXT_COLS), BF16)], axis=0)
        tiles = []
        for t in range(2):
            out = jnp.dot(
                flat_w[at + t],
                right[:, t * TILE : t * TILE + COLS],
                preferred_element_type=F32,
            )
            total = out[0:PAD]
            for v in range(1, KSIZE):
                total = total + pltpu.roll(out[PAD * v : PAD * v + PAD], COLS - v, 1)
            tiles.append(total[:, 0:TILE])
        return tiles

    def flat_spread(tiles, at):
        outs = []
        for t in range(2):
            high, low = halves(tiles[t])
            gap = jnp.zeros((PAD, TILE), BF16)
            right = jnp.concatenate([high, gap, low, gap, high, gap, gap, gap], axis=0)
            out = jnp.dot(flat_w[at + t], right, preferred_element_type=F32)
            near, far = out[0:PAD], None
            for v in range(1, KSIZE):
                piece = pltpu.roll(out[PAD * v : PAD * v + PAD], v, 1)
                past = edge_lane < v
                near = near + jnp.where(past, 0.0, piece)
                piece = jnp.where(past, piece, 0.0)
                far = piece if far is None else far + piece
            total = jnp.concatenate([near, far], axis=1)
            outs.append(total)
        return outs

    def inner(x, y):
        z = x * y
        z = z[:, 0:TILE] + z[:, TILE:]
        while z.shape[0] > 8:
            half = z.shape[0] // 2
            z = z[0:half] + z[half:]
        return jnp.sum(jnp.sum(z, axis=0, keepdims=True), axis=1, keepdims=True)

    def inner_rimmed(x, y):
        r, c = iota((EXT_ROWS, EXT_COLS), 0), iota((EXT_ROWS, EXT_COLS), 1)
        own = (r >= RADIUS) & (r < ROWS + RADIUS) & (c >= RADIUS) & (c < COLS + RADIUS)
        z = jnp.where(own, x * y, 0.0)
        z = z[:, 0:TILE] + z[:, TILE : 2 * TILE] + z[:, 2 * TILE :]
        z = z[0:72] + z[72:]
        z = (z[0:24] + z[24:48]) + z[48:72]
        z = (z[0:8] + z[8:16]) + z[16:24]
        return jnp.sum(jnp.sum(z, axis=0, keepdims=True), axis=1, keepdims=True)

    def own_block(source, row):
        shifted[...] = pltpu.roll(source[row : row + EXT_ROWS, :], EXT_COLS - RADIUS, 1)[:, 0:COLS]
        return shifted[pl.ds(RADIUS, ROWS), :]

    load_obs.wait()
    spread(obs_ref[...], spill)
    copies = start_exchange()
    pl.semaphore_wait(barrier, len(partners))
    for copy in copies:
        copy.start()
    build_gather()
    for copy in copies[4:]:
        copy.wait_recv()
    prepare_frames()
    assemble(copies[:4])
    for t in range(2):
        image[0, :, t * TILE : (t + 1) * TILE] = gather(tall_field, PAD, t)
    frames = side_frames()
    frames_top = flat_frames(slice(0, 32), 0)
    frames_bottom = flat_frames(slice(144, 176), 2)
    spread(image[0], field)
    to_left, to_right = side_spread(frames)
    field[:, 0:TILE] += to_left
    field[:, 2 * TILE :] += to_right
    for t, out in enumerate(flat_spread(frames_top, 4)):
        field[0:PAD, t * TILE : t * TILE + COLS] += out
    for t, out in enumerate(flat_spread(frames_bottom, 6)):
        field[ROWS:, t * TILE : t * TILE + COLS] += out
    r, c = iota((EXT_ROWS, EXT_COLS), 0), iota((EXT_ROWS, EXT_COLS), 1)
    inside = (
        (r >= jnp.where(rng == 0, RADIUS, 0))
        & (r < jnp.where(rng == 15, ROWS + RADIUS, EXT_ROWS))
        & (c >= jnp.where(azi == 0, RADIUS, 0))
        & (c < jnp.where(azi == 31, COLS + RADIUS, EXT_COLS))
    )
    field[...] = jnp.where(inside, field[...], 0.0)
    for t in range(2):
        image[1, :, t * TILE : (t + 1) * TILE] = gather(field, 0, t)
    store_image = pltpu.make_async_copy(image, image_hbm, load.at[1])
    store_image.start()
    first = tall_field[PAD : PAD + EXT_ROWS, :]
    second = field[...]
    sums = [inner_rimmed(first, first), inner(image[0], image[0])]
    sums += [inner_rimmed(second, second), inner_rimmed(first, second)]
    sums += [inner(image[1], image[1]), inner(image[0], image[1])]
    line = lane[0:1]
    moments[0] = sum(jnp.where(line == i, x, 0.0) for i, x in enumerate(sums))
    for phase, got in enumerate((got_a, got_b)):
        for i, o in enumerate(OFFSETS[phase]):
            pltpu.make_async_remote_copy(
                src_ref=moments.at[phase],
                dst_ref=got.at[i],
                send_sem=sum_send.at[phase],
                recv_sem=sum_recv.at[phase],
                device_id=member(o),
                device_id_type=MESH,
            ).start()
        if phase == 0:
            grad[0] = own_block(tall_field, PAD)
            grad[1] = own_block(field, 0)
            store_grad = pltpu.make_async_copy(grad, grad_hbm, load.at[0])
            store_grad.start()
        pltpu.make_async_copy(got, got, sum_recv.at[phase]).wait()
        moments[phase + 1] = moments[phase] + jnp.sum(got[...], axis=0)
    total = moments[2]
    gg, qq, ww, gw, pp, qp = (total[:, i : i + 1] for i in range(6))
    alpha = gg / qq
    gamma_1 = (gg - alpha * gw) - alpha * (gw - alpha * ww)
    rise = 1.0 + gamma_1 / gg
    delta_1 = rise * (rise * qq - alpha * qp) - alpha * (rise * qp - alpha * pp)
    alpha_1 = gamma_1 / delta_1
    near = alpha + alpha_1 * rise
    far = alpha * alpha_1
    factors[...] = jnp.where(line == 0, near, far)
    for phase, got in enumerate((got_a, got_b)):
        pltpu.make_async_copy(got, got, sum_send.at[phase]).wait()
    for copy in copies:
        copy.wait_send()
    store_grad.wait()
    store_image.wait()


def finish(grad_hbm, image_hbm, obs_hbm, factors_hbm, est_hbm, res_hbm, grad, image, obs, factors, sems):
    ins = [(factors_hbm, factors), (grad_hbm.at[0], grad.at[0]), (grad_hbm.at[1], grad.at[1])]
    ins += [(image_hbm.at[0], image.at[0]), (image_hbm.at[1], image.at[1]), (obs_hbm, obs)]
    loads = [pltpu.make_async_copy(a, b, sems.at[i]) for i, (a, b) in enumerate(ins)]
    for load in loads:
        load.start()
    for load in loads[:3]:
        load.wait()
    near, far = factors[:, 0:1], factors[:, 1:2]
    grad[0] = near * grad[0] - far * grad[1]
    store_est = pltpu.make_async_copy(grad.at[0], est_hbm, sems.at[6])
    store_est.start()
    for load in loads[3:]:
        load.wait()
    image[0] = obs[...] - near * image[0] + far * image[1]
    store_res = pltpu.make_async_copy(image.at[0], res_hbm, sems.at[7])
    store_res.start()
    store_est.wait()
    store_res.wait()


def body(observed, psf_tiles):
    pair = jax.ShapeDtypeStruct((2, ROWS, COLS), F32)
    hbm = pl.BlockSpec(memory_space=pltpu.HBM)
    grads, images, factors = pl.pallas_call(
        kernel,
        out_shape=(pair, pair, jax.ShapeDtypeStruct((1, TILE), F32)),
        in_specs=[hbm, hbm],
        out_specs=(hbm, hbm, pl.BlockSpec(memory_space=pltpu.VMEM)),
        scratch_shapes=[
            pltpu.VMEM((ROWS, COLS), F32),
            pltpu.VMEM((1, 2, KSIZE * KSIZE), F32),
            pltpu.VMEM((8, TILE), F32),
            pltpu.VMEM((2, 3 * TILE, WIDE + TILE), BF16),
            pltpu.VMEM((2, 4 * TILE, WIDE + TILE), BF16),
            pltpu.VMEM((2, ROWS + 2 * PAD, WIDE + TILE), F32),
            pltpu.VMEM((2, EXT_ROWS, WIDE), F32),
            pltpu.VMEM((EXT_ROWS, EXT_COLS), F32),
            pltpu.VMEM((TALL_ROWS, EXT_COLS), F32),
            pltpu.VMEM((EXT_ROWS, EXT_COLS), F32),
            pltpu.VMEM((2, ROWS, COLS), F32),
            pltpu.VMEM((2, ROWS, COLS), F32),
            pltpu.VMEM((EXT_ROWS, COLS), F32),
            pltpu.VMEM((2, EXT_ROWS, TILE), F32),
            pltpu.VMEM((2, 32, TILE), F32),
            pltpu.VMEM((56, TILE), F32),
            pltpu.VMEM((56, TILE), F32),
            pltpu.VMEM((2, 16, TILE), F32),
            pltpu.VMEM((2, 16, TILE), F32),
            pltpu.VMEM((2, 32, TILE), F32),
            pltpu.VMEM((56, TILE), F32),
            pltpu.VMEM((56, TILE), F32),
            pltpu.VMEM((2, 16, TILE), F32),
            pltpu.VMEM((2, 16, TILE), F32),
            pltpu.VMEM((208, COLS), F32),
            pltpu.VMEM((160, COLS), F32),
            pltpu.VMEM((8, PAD, TILE), F32),
            pltpu.VMEM((8, GROUPS, TILE), BF16),
            pltpu.VMEM((2, TILE, COLS), BF16),
            pltpu.VMEM((4 * TILE, COLS), BF16),
            pltpu.VMEM((4 * TILE, TILE), BF16),
            pltpu.VMEM((3, 1, TILE), F32),
            pltpu.VMEM((len(OFFSETS[0]), 1, TILE), F32),
            pltpu.VMEM((len(OFFSETS[1]), 1, TILE), F32),
            pltpu.SemaphoreType.DMA((8,)),
            pltpu.SemaphoreType.DMA((8,)),
            pltpu.SemaphoreType.DMA((2,)),
            pltpu.SemaphoreType.DMA((2,)),
            pltpu.SemaphoreType.DMA((2,)),
        ],
        compiler_params=pltpu.CompilerParams(
            collective_id=0, has_side_effects=True, vmem_limit_bytes=61 << 20
        ),
    )(observed, psf_tiles)
    block = jax.ShapeDtypeStruct((ROWS, COLS), F32)
    return pl.pallas_call(
        finish,
        out_shape=(block, block),
        in_specs=[pl.BlockSpec(memory_space=pltpu.HBM)] * 4,
        out_specs=(pl.BlockSpec(memory_space=pltpu.HBM),) * 2,
        scratch_shapes=[
            pltpu.VMEM((2, ROWS, COLS), F32),
            pltpu.VMEM((2, ROWS, COLS), F32),
            pltpu.VMEM((ROWS, COLS), F32),
            pltpu.VMEM((1, TILE), F32),
            pltpu.SemaphoreType.DMA((8,)),
        ],
        compiler_params=pltpu.CompilerParams(vmem_limit_bytes=61 << 20),
    )(grads, images, observed, factors)


def solution(mesh):
    return jax.shard_map(
        body,
        mesh=mesh,
        in_specs=(P("rng", "azi"), P("rng", "azi", None)),
        out_specs=(P("rng", "azi"), P("rng", "azi")),
        check_vma=False,
    )
```

```python
import itertools

import jax
import jax.numpy as jnp
from jax import lax
from jax.experimental import pallas as pl
from jax.experimental.pallas import tpu as pltpu
from jax.sharding import PartitionSpec as P

TILE = 128
KSIZE = 11
RADIUS = 5
RIM = 2 * RADIUS
ROWS = 128
COLS = 256
EXT_ROWS = 144
EXT_COLS = 384
TALL_ROWS = 176
PAD = 16
GROUPS = KSIZE * PAD
WIDE = KSIZE * TILE
MESH = pl.DeviceIdType.MESH
F32 = jnp.float32
BF16 = jnp.bfloat16

PARTS = {"x": 4, "y": 4, "z": 16, "c": 2}
PHASES = (("x", "y", "c"), ("z",))
NEIGHBOURS = tuple(
    (dr, da) for dr in (-1, 0, 1) for da in (-1, 0, 1) if (dr, da) != (0, 0)
)


def group_offsets(axes):
    ranges = [range(PARTS[axis]) for axis in axes]
    offsets = [dict(zip(axes, o)) for o in itertools.product(*ranges) if any(o)]
    return sorted(
        offsets,
        key=lambda o: -sum(min(n, PARTS[a] - n) for a, n in o.items() if a != "c"),
    )


OFFSETS = tuple(group_offsets(axes) for axes in PHASES)


def band_group(n):
    return (n * 373) >> 12


def split_rows(x):
    high = x.astype(BF16).astype(F32)
    return high, x - high


def iota(shape, dim):
    return lax.broadcasted_iota(jnp.int32, shape, dim)


def orders(taps):
    a, b = iota((TILE, TILE), 0), iota((TILE, TILE), 1)
    last = KSIZE * KSIZE - 1

    def turned(n):
        return KSIZE * (n - KSIZE * band_group(n)) + band_group(n)

    back = last - b
    wanted = (back, turned(b), jnp.where(back >= 0, turned(jnp.maximum(back, 0)), -1))
    pick = [jnp.where((a == w) & (b <= last), 1.0, 0.0).astype(BF16) for w in wanted]
    first = taps.astype(BF16)
    rest = taps - first.astype(F32)
    second = rest.astype(BF16)
    third = (rest - second.astype(F32)).astype(BF16)
    parts = jnp.concatenate([first, second, third], axis=1)
    out = [taps]
    for p in pick:
        out.append(jnp.dot(parts, jnp.concatenate([p] * 3, axis=0), preferred_element_type=F32))
    row = iota((8, TILE), 0)
    total = out[0]
    for k in range(1, 4):
        total = jnp.where((row >= 2 * k) & (row < 2 * k + 2), pltpu.roll(out[k], 2 * k, 0), total)
    return total


def sloped(line, shift, rows):
    base = pltpu.roll(jnp.broadcast_to(line, (8, TILE)), shift, 1)
    return pltpu.roll(jnp.concatenate([base] * (rows // 8), axis=0), 0, 1, stride=1, stride_axis=0)


def side_gather_weights(left, right):
    i, n = iota((40, TILE), 0), iota((40, TILE), 1)
    j = n - KSIZE * band_group(n)
    halves_ = []
    for kernel_row, start in ((left, 0), (right, 20)):
        band = sloped(kernel_row, TILE - RIM - start, 40)
        c = i - start
        keep = (c >= 0) & (c < 20) & (j < RIM) & (n < 121) & (c - j >= 0) & (c - j < KSIZE)
        halves_.append(jnp.where(keep, band, 0.0))
    high, low = split_rows(jnp.concatenate(halves_, axis=1))
    return jnp.concatenate([high, high, low, jnp.zeros((8, COLS), F32)], axis=0).astype(BF16)


def side_spread_weights(left, right):
    i, n = iota((24, TILE), 0), iota((24, TILE), 1)
    c = n - KSIZE * band_group(n)
    valid = (c < RIM) & (n < 121)
    halves_ = []
    for kernel_row, keep in (
        (left, valid & (i < RIM) & (c <= i)),
        (right, valid & (i >= RIM) & (i < 2 * RIM) & (c >= i - RIM)),
    ):
        band = sloped(kernel_row, TILE - RIM, 24)
        halves_.append(jnp.where(keep, band, 0.0))
    high, low = split_rows(jnp.concatenate(halves_, axis=1))
    return jnp.concatenate([high, high, low, jnp.zeros((TILE - 72, COLS), F32)], axis=0).astype(BF16)


def flat_bands(kernel_row, order, shift, lines):
    lane = iota((PAD, TILE), 1)
    last = KSIZE * (KSIZE - 1)
    base = pltpu.roll(jnp.broadcast_to(kernel_row, (8, TILE)), TILE - last, 1)
    taps = jnp.concatenate(
        [
            pltpu.roll(x, 0, 1, stride=KSIZE, stride_axis=0)
            for x in (base, pltpu.roll(base, 8 * KSIZE, 1))
        ],
        axis=0,
    )
    high, low = split_rows(jnp.where(lane < KSIZE, taps, 0.0))
    taps = high + pltpu.roll(high, 32, 1) + pltpu.roll(low, 64, 1)
    lines[...] = pltpu.roll(taps, shift % TILE, 1) if shift else taps
    blocks = []
    for v in order:
        line = jnp.broadcast_to(lines[v : v + 1, :], (8, TILE))
        line = pltpu.roll(line, 0, 1, stride=1, stride_axis=0)
        blocks += [line, pltpu.roll(line, 8, 1)]
    return jnp.concatenate(blocks, axis=0)


def flat_gather_weights(kernel_row, low_row, high_row, lines):
    band = flat_bands(kernel_row, range(KSIZE - 1, -1, -1), 0, lines)
    r = iota((GROUPS, TILE), 0) & (PAD - 1)
    return jnp.where((r >= low_row) & (r < high_row), band, 0.0).astype(BF16)


def flat_spread_weights(kernel_row, shift, lines):
    band = flat_bands(kernel_row, range(KSIZE), shift, lines)
    lane = iota((GROUPS, TILE), 1)
    keep = ((lane & 31) < PAD) & (lane < 96)
    return jnp.where(keep, band, 0.0).astype(BF16)


def side_fields(near, far):
    lane = iota(near.shape, 1)
    left = jnp.where(lane >= TILE - RIM, far, jnp.where(lane < RIM, near, 0.0))
    right = jnp.where(lane < 20, far, 0.0)
    x = pltpu.roll(left, RIM, 1) + pltpu.roll(right, 20, 1)
    high, low = split_rows(x)
    return (high + pltpu.roll(low, 40, 1) + pltpu.roll(high, 80, 1)).astype(BF16)


def picker(places, width):
    n = iota((TILE, width), 0)
    j = n - KSIZE * band_group(n)
    lane = iota((TILE, width), 1)
    blocks = [
        jnp.where((j < RIM) & (n < 121) & (lane == j + place), 1.0, 0.0).astype(BF16)
        for place in places
    ]
    return jnp.concatenate(blocks * 2, axis=0)


def picked(x, matrix):
    high, low = halves(x)
    return jnp.dot(jnp.concatenate([high, low], axis=1), matrix, preferred_element_type=F32)


def halves(x):
    high = x.astype(BF16)
    low = (x - high.astype(F32)).astype(BF16)
    return high, low


def kernel(
    obs_hbm,
    psf_hbm,
    grad_hbm,
    image_hbm,
    factors,
    obs_ref,
    psf_ref,
    taps,
    spread_w,
    gather_w,
    wide,
    tall,
    spill,
    tall_field,
    field,
    image,
    grad,
    shifted,
    strips,
    send_side,
    send_up,
    send_down,
    send_up_corner,
    send_down_corner,
    got_side,
    got_up,
    got_down,
    got_up_corner,
    got_down_corner,
    side_out,
    side_back,
    lines,
    pick_apart,
    pick_near,
    moments,
    got_a,
    got_b,
    halo_send,
    halo_recv,
    sum_send,
    sum_recv,
    load,
):
    rng = lax.axis_index("rng")
    azi = lax.axis_index("azi")
    place = {
        "x": azi // 8,
        "y": rng // 4,
        "z": (rng % 4) * 4 + (azi // 2) % 4,
        "c": azi % 2,
    }

    def member(offset):
        at = {
            axis: lax.rem(place[axis] + offset[axis], PARTS[axis])
            if axis in offset
            else place[axis]
            for axis in PARTS
        }
        return (at["y"] * 4 + at["z"] // 4, at["x"] * 8 + (at["z"] % 4) * 2 + at["c"])

    def neighbour(dr, da):
        return (lax.rem(rng + dr + 16, 16), lax.rem(azi + da + 32, 32))

    barrier = pltpu.get_barrier_semaphore()
    near_by = [neighbour(*d) for d in NEIGHBOURS]
    partners = near_by + [member(o) for offsets in OFFSETS for o in offsets]
    for partner in near_by:
        pl.semaphore_signal(barrier, inc=1, device_id=partner, device_id_type=MESH)
    load_psf = pltpu.make_async_copy(psf_hbm, psf_ref, load.at[0])
    load_obs = pltpu.make_async_copy(obs_hbm, obs_ref, load.at[1])
    load_psf.start()
    load_obs.start()
    for partner in partners[len(near_by) :]:
        pl.semaphore_signal(barrier, inc=1, device_id=partner, device_id_type=MESH)

    lane = lax.broadcasted_iota(jnp.int32, (TILE, TILE), 1)
    row = lax.broadcasted_iota(jnp.int32, (TILE, TILE), 0)

    edge_lane, edge_row = lane[0:PAD], row[0:PAD]

    def band(line, shift, back):
        line = pltpu.roll(jnp.broadcast_to(line, (8, TILE)), lax.rem(3 * TILE - shift, TILE), 1)
        line = jnp.where(lane[0:8] < KSIZE, line, 0.0)
        line = pltpu.roll(line, back, 1) if back else line
        line = pltpu.roll(line, 0, 1, stride=1, stride_axis=0)
        rows = [pltpu.roll(line, 8 * g, 1) if g else line for g in range(TILE // 8)]
        return jnp.concatenate(rows, axis=0)

    def build_spread():
        def one(u, packed):
            block = pl.ds(pl.multiple_of(u * TILE, TILE), TILE)
            used = jnp.where(u < KSIZE, 1.0, 0.0)
            out = []
            for t in range(2):
                rows = band(taps[t : t + 1, :], KSIZE * u, 0)
                edge = rows[TILE - PAD :]
                below = edge_lane < edge_row + (TILE - PAD)
                over = jnp.where(below, edge, 0.0) * used
                out.append(packed[t] + pltpu.roll(over, lax.rem(KSIZE * u, TILE), 1))
                main = jnp.concatenate([rows[0 : TILE - PAD], jnp.where(below, 0.0, edge)], axis=0)
                high, low = halves(main)
                spread_w[t, 0:TILE, block] = high
                spread_w[t, TILE : 2 * TILE, block] = high
                spread_w[t, 2 * TILE :, block] = low
            return tuple(out)

        def three(i, packed):
            for k in range(3):
                packed = one(3 * i + k, packed)
            return packed

        packed = lax.fori_loop(0, 4, three, (jnp.zeros((PAD, TILE), F32),) * 2)
        blank = jnp.zeros((TILE - PAD, TILE), BF16)
        for t in range(2):
            high, low = (jnp.concatenate([blank, p], axis=0) for p in halves(packed[t]))
            spread_w[t, 0:TILE, WIDE:] = high
            spread_w[t, TILE : 2 * TILE, WIDE:] = high
            spread_w[t, 2 * TILE :, WIDE:] = low

    def build_gather():
        gather_w[:, 3 * TILE + 3 * PAD :, :] = jnp.zeros((2, TILE - 3 * PAD, WIDE + TILE), BF16)

        def one(u, carry):
            block = pl.ds(pl.multiple_of(u * TILE, TILE), TILE)
            for t in range(2):
                rows = band(taps[2 + t : 3 + t, :], KSIZE * (KSIZE - 1) - KSIZE * u, TILE - RIM)
                edge = rows[0:PAD]
                past = edge_lane > edge_row
                high, low = halves(jnp.where(past, edge, 0.0))
                gather_w[t, 3 * TILE : 3 * TILE + PAD, block] = high
                gather_w[t, 3 * TILE + PAD : 3 * TILE + 2 * PAD, block] = high
                gather_w[t, 3 * TILE + 2 * PAD : 3 * TILE + 3 * PAD, block] = low
                main = jnp.concatenate([jnp.where(past, 0.0, edge), rows[PAD:]], axis=0)
                high, low = halves(main)
                gather_w[t, 0:TILE, block] = high
                gather_w[t, TILE : 2 * TILE, block] = high
                gather_w[t, 2 * TILE : 3 * TILE, block] = low
            return carry

        def three(i, carry):
            for k in range(3):
                one(3 * i + k, carry)
            return carry

        lax.fori_loop(0, 4, three, 0)

    pick_apart[...] = picker((0, TILE), COLS)
    pick_near[...] = picker((0, RIM), TILE)
    load_psf.wait()
    taps[...] = jnp.zeros_like(taps)
    taps[0:2, 0 : KSIZE * KSIZE] = psf_ref[0]
    kernels = orders(taps[...])
    taps[...] = kernels
    build_spread()
    wide[:, 0:PAD, :] = jnp.zeros((2, PAD, WIDE + TILE), F32)
    wide[:, PAD + ROWS :, :] = jnp.zeros((2, PAD, WIDE + TILE), F32)

    def spread(source, out):
        group = band_group(iota((1, TILE), 1))
        spares = []
        for t in range(2):
            high, low = halves(source[:, t * TILE : (t + 1) * TILE])
            left = jnp.concatenate([high, low, high], axis=1)
            for n in range(0, WIDE + TILE, 256):
                wide[t, PAD : PAD + ROWS, n : n + 256] = jnp.dot(
                    left, spread_w[t, :, n : n + 256], preferred_element_type=F32
                )
            total, spare = None, jnp.zeros((EXT_ROWS, TILE), F32)
            for u in range(KSIZE):
                rows = pl.ds(PAD - u, EXT_ROWS)
                piece = wide[t, rows, u * TILE : (u + 1) * TILE]
                total = piece if total is None else total + piece
                spare = jnp.where(group == u, wide[t, rows, WIDE:], spare)
            out[:, t * TILE : (t + 1) * TILE] = total
            spares.append(spare)
        over = picked(jnp.concatenate(spares, axis=1), pick_apart[...])
        out[:, TILE : 2 * TILE] += over[:, 0:TILE]
        out[:, 2 * TILE :] = over[:, TILE:]

    def gather(source, row, t):
        tall_lane = lax.broadcasted_iota(jnp.int32, (EXT_ROWS, TILE), 1)
        high, low = halves(source[row : row + EXT_ROWS, t * TILE : (t + 1) * TILE])
        edge = source[row : row + EXT_ROWS, (t + 1) * TILE : (t + 2) * TILE]
        edge = jnp.where(tall_lane < RIM, edge, 0.0)
        edge_high = edge.astype(BF16).astype(F32)
        edge_low = edge - edge_high
        edge = edge_high + pltpu.roll(edge_low, PAD, 1) + pltpu.roll(edge_high, 2 * PAD, 1)
        left = jnp.concatenate([high, low, high, edge.astype(BF16)], axis=1)
        total = None
        for n in range(0, WIDE, 256):
            width = min(256, WIDE - n)
            tall[t, :, n : n + width] = jnp.dot(
                left, gather_w[t, :, n : n + width], preferred_element_type=F32
            )
        for u in range(KSIZE):
            piece = tall[t, pl.ds(u, ROWS), u * TILE : (u + 1) * TILE]
            total = piece if total is None else total + piece
        return total

    def pack(strip, rows):
        out = None
        for k in range(strip.shape[0] // rows):
            part = strip[rows * k : rows * k + rows]
            part = jnp.where(lane[0:rows] < 2 * RIM, part, 0.0)
            part = pltpu.roll(part, 2 * RIM * k, 1) if k else part
            out = part if out is None else out + part
        return out

    def unpack(packed, groups):
        parts = []
        for k in range(groups):
            part = pltpu.roll(packed, TILE - 2 * RIM * k, 1) if k else packed
            parts.append(jnp.where(lane[0 : packed.shape[0]] < 2 * RIM, part, 0.0))
        return jnp.concatenate(parts, axis=0)

    def start_exchange():
        side = iota((EXT_ROWS, TILE), 1)
        right = jnp.where(side >= TILE - RIM, spill[:, TILE : 2 * TILE], spill[:, 2 * TILE :])
        strips[0] = spill[:, 0:TILE]
        strips[1] = pltpu.roll(right, RIM, 1)
        for i in range(2):
            send_side[i, 0:24] = pack(strips[i], 24)
            send_side[i, 24:] = kernels
            send_up_corner[i, 0:8] = pack(strips[i, 0:24], 8)
            send_up_corner[i, 8:] = kernels
            send_down_corner[i, 0:8] = pack(strips[i, 118:142], 8)
            send_down_corner[i, 8:] = kernels
        for send, at in ((send_up, 0), (send_down, 118)):
            for t in range(2):
                tile = slice(t * TILE, (t + 1) * TILE)
                send[16 * t : 16 * t + 16] = spill[at : at + 16, tile]
                send[32 + 4 * t : 36 + 4 * t] = spill[at + 16 : at + 20, tile]
            send[40:48] = pack(spill[at : at + 24, 2 * TILE :], 8)
            send[48:] = kernels
        plan = {
            (-1, 1): (send_up_corner.at[1], got_up_corner.at[1]),
            (1, -1): (send_down_corner.at[0], got_down_corner.at[0]),
            (-1, -1): (send_up_corner.at[0], got_up_corner.at[0]),
            (1, 1): (send_down_corner.at[1], got_down_corner.at[1]),
            (-1, 0): (send_up, got_up),
            (1, 0): (send_down, got_down),
            (0, -1): (send_side.at[0], got_side.at[0]),
            (0, 1): (send_side.at[1], got_side.at[1]),
        }
        return [
            pltpu.make_async_remote_copy(
                src_ref=source,
                dst_ref=target,
                send_sem=halo_send.at[i],
                recv_sem=halo_recv.at[i],
                device_id=neighbour(*d),
                device_id_type=MESH,
            )
            for i, (d, (source, target)) in enumerate(plan.items())
        ]

    above = jnp.where(rng > 0, 1.0, 0.0)
    below = jnp.where(rng < 15, 1.0, 0.0)
    left_of = jnp.where(azi > 0, 1.0, 0.0)
    right_of = jnp.where(azi < 31, 1.0, 0.0)

    def assemble():
        first, last = slice(0, TILE), slice(2 * TILE, EXT_COLS)
        tall_field[0:PAD] = jnp.zeros((PAD, EXT_COLS), F32)
        tall_field[PAD : PAD + EXT_ROWS] = spill[...]
        tall_field[PAD + EXT_ROWS :] = jnp.zeros((PAD, EXT_COLS), F32)
        for got, at, flag in ((got_down, 6, above), (got_up, 144, below)):
            for t in range(2):
                tile = slice(t * TILE, (t + 1) * TILE)
                tall_field[at : at + 16, tile] += got[16 * t : 16 * t + 16] * flag
                tall_field[at + 16 : at + 20, tile] += got[32 + 4 * t : 36 + 4 * t] * flag
            tall_field[at : at + 24, last] += unpack(got[40:48], 3) * flag

        def from_left(strip, rows, flag):
            strip = pltpu.roll(strip, TILE - RIM, 1) * flag
            near = iota(strip.shape, 1) < TILE // 2
            tall_field[rows, first] += jnp.where(near, strip, 0.0)
            tall_field[rows, last] += jnp.where(near, 0.0, strip)

        def from_right(strip, rows, flag):
            tall_field[rows, last] += strip * flag

        middle, top, bottom = slice(16, 160), slice(6, 30), slice(144, 168)
        from_right(unpack(got_side[0, 0:24], 6), middle, right_of)
        from_left(unpack(got_side[1, 0:24], 6), middle, left_of)
        from_right(unpack(got_down_corner[0, 0:8], 3), top, above * right_of)
        from_left(unpack(got_down_corner[1, 0:8], 3), top, above * left_of)
        from_right(unpack(got_up_corner[0, 0:8], 3), bottom, below * right_of)
        from_left(unpack(got_up_corner[1, 0:8], 3), bottom, below * left_of)
        r, c = iota((TALL_ROWS, EXT_COLS), 0), iota((TALL_ROWS, EXT_COLS), 1)
        inside = (
            (r >= jnp.where(rng == 0, PAD + RADIUS, 0))
            & (r < jnp.where(rng == 15, PAD + RADIUS + ROWS, TALL_ROWS))
            & (c >= jnp.where(azi == 0, RADIUS, 0))
            & (c < jnp.where(azi == 0, 320, EXT_COLS))
            & ((c < jnp.where(azi == 31, RADIUS + COLS, EXT_COLS)) | (c >= 320))
        )
        tall_field[...] = jnp.where(inside, tall_field[...], 0.0)

    def side_kernels(k):
        return tuple(
            (got[1, at + 1 + k : at + 2 + k] * (flag * left_of), got[0, at + k : at + 1 + k] * (flag * right_of))
            for got, at, flag in ((got_down_corner, 8, above), (got_side, 24, 1.0), (got_up_corner, 8, below))
        )

    def side_frames():
        fields = side_fields(tall_field[:, 0:TILE], tall_field[:, 2 * TILE :])
        parts = ((0, 32, 144, 16), (16, 144, 0, 128), (144, 32, 176, 16))
        group = band_group(iota((1, COLS), 1) & (TILE - 1))
        sums = []
        for (start, count, at, rows), (left, right) in zip(parts, side_kernels(2)):
            side_out[at : at + count] = jnp.dot(
                fields[start : start + count], side_gather_weights(left, right), preferred_element_type=F32
            )
            total = jnp.zeros((rows, COLS), F32)
            for u in range(KSIZE):
                total = jnp.where(group == KSIZE - 1 - u, side_out[at + u : at + u + rows], total)
            sums.append(total)
        frames = picked(jnp.concatenate(sums, axis=0), pick_near[...])
        r = iota(frames.shape, 0)
        return jnp.where((r >= 6) & (r < 154), frames, 0.0)

    def side_spread(frames):
        high, low = split_rows(frames)
        packed = (high + pltpu.roll(low, 24, 1) + pltpu.roll(high, 48, 1)).astype(BF16)
        for (start, stop), (left, right) in zip(((0, 16), (16, 144), (144, 160)), side_kernels(0)):
            side_back[start:stop] = jnp.dot(
                packed[start:stop], side_spread_weights(left, right), preferred_element_type=F32
            )
        group = band_group(iota((1, COLS), 1) & (TILE - 1))
        total = jnp.zeros((EXT_ROWS, COLS), F32)
        for u in range(KSIZE):
            total = jnp.where(group == u, side_back[PAD - u : PAD - u + EXT_ROWS], total)
        out = picked(total, pick_apart[...])
        return out[:, 0:TILE], out[:, TILE:]

    def flat_frames(rows, kernels, low_row, at):
        high, low = halves(tall_field[rows, :])
        right = jnp.concatenate([high, low, high, jnp.zeros((32, EXT_COLS), BF16)], axis=0)
        tiles = []
        for t in range(2):
            out = jnp.dot(
                flat_gather_weights(kernels[t], low_row, low_row + RIM, lines.at[at + t]),
                right[:, t * TILE : t * TILE + COLS],
                preferred_element_type=F32,
            )
            total = out[0:PAD]
            for v in range(1, KSIZE):
                total = total + pltpu.roll(out[PAD * v : PAD * v + PAD], COLS - v, 1)
            tiles.append(total[:, 0:TILE])
        return tiles

    def flat_spread(tiles, kernels, shift, at):
        outs = []
        for t in range(2):
            high, low = halves(tiles[t])
            gap = jnp.zeros((PAD, TILE), BF16)
            right = jnp.concatenate([high, gap, low, gap, high, gap, gap, gap], axis=0)
            out = jnp.dot(flat_spread_weights(kernels[t], shift, lines.at[at + t]), right, preferred_element_type=F32)
            near, far = out[0:PAD], None
            for v in range(1, KSIZE):
                piece = pltpu.roll(out[PAD * v : PAD * v + PAD], v, 1)
                past = edge_lane < v
                near = near + jnp.where(past, 0.0, piece)
                piece = jnp.where(past, piece, 0.0)
                far = piece if far is None else far + piece
            total = jnp.concatenate([near, far], axis=1)
            outs.append(total)
        return outs

    def inner(x, y):
        z = x * y
        z = z[:, 0:TILE] + z[:, TILE:]
        while z.shape[0] > 8:
            half = z.shape[0] // 2
            z = z[0:half] + z[half:]
        return jnp.sum(jnp.sum(z, axis=0, keepdims=True), axis=1, keepdims=True)

    def inner_rimmed(x, y):
        r, c = iota((EXT_ROWS, EXT_COLS), 0), iota((EXT_ROWS, EXT_COLS), 1)
        own = (r >= RADIUS) & (r < ROWS + RADIUS) & (c >= RADIUS) & (c < COLS + RADIUS)
        z = jnp.where(own, x * y, 0.0)
        z = z[:, 0:TILE] + z[:, TILE : 2 * TILE] + z[:, 2 * TILE :]
        z = z[0:72] + z[72:]
        z = (z[0:24] + z[24:48]) + z[48:72]
        z = (z[0:8] + z[8:16]) + z[16:24]
        return jnp.sum(jnp.sum(z, axis=0, keepdims=True), axis=1, keepdims=True)

    def own_block(source, row):
        shifted[...] = pltpu.roll(source[row : row + EXT_ROWS, :], EXT_COLS - RADIUS, 1)[:, 0:COLS]
        return shifted[pl.ds(RADIUS, ROWS), :]

    load_obs.wait()
    spread(obs_ref[...], spill)
    copies = start_exchange()
    pl.semaphore_wait(barrier, len(partners))
    for copy in copies:
        copy.start()
    build_gather()
    for copy in copies:
        copy.wait()
    assemble()
    for t in range(2):
        image[0, :, t * TILE : (t + 1) * TILE] = gather(tall_field, PAD, t)
    frames = side_frames()
    kernels_top = [got_down[52 + t : 53 + t] * above for t in range(2)]
    kernels_bottom = [got_up[52 + t : 53 + t] * below for t in range(2)]
    frames_top = flat_frames(slice(0, 32), kernels_top, 6, 0)
    frames_bottom = flat_frames(slice(144, 176), kernels_bottom, 0, 2)
    spread(image[0], field)
    to_left, to_right = side_spread(frames)
    field[:, 0:TILE] += to_left
    field[:, 2 * TILE :] += to_right
    kernels_top = [got_down[54 + t : 55 + t] * above for t in range(2)]
    kernels_bottom = [got_up[54 + t : 55 + t] * below for t in range(2)]
    for t, out in enumerate(flat_spread(frames_top, kernels_top, 6, 4)):
        field[0:PAD, t * TILE : t * TILE + COLS] += out
    for t, out in enumerate(flat_spread(frames_bottom, kernels_bottom, -RIM, 6)):
        field[ROWS:, t * TILE : t * TILE + COLS] += out
    r, c = iota((EXT_ROWS, EXT_COLS), 0), iota((EXT_ROWS, EXT_COLS), 1)
    inside = (
        (r >= jnp.where(rng == 0, RADIUS, 0))
        & (r < jnp.where(rng == 15, ROWS + RADIUS, EXT_ROWS))
        & (c >= jnp.where(azi == 0, RADIUS, 0))
        & (c < jnp.where(azi == 31, COLS + RADIUS, EXT_COLS))
    )
    field[...] = jnp.where(inside, field[...], 0.0)
    for t in range(2):
        image[1, :, t * TILE : (t + 1) * TILE] = gather(field, 0, t)
    store_image = pltpu.make_async_copy(image, image_hbm, load.at[1])
    store_image.start()
    first = tall_field[PAD : PAD + EXT_ROWS, :]
    second = field[...]
    sums = [inner_rimmed(first, first), inner(image[0], image[0])]
    sums += [inner_rimmed(second, second), inner_rimmed(first, second)]
    sums += [inner(image[1], image[1]), inner(image[0], image[1])]
    line = lane[0:1]
    moments[0] = sum(jnp.where(line == i, x, 0.0) for i, x in enumerate(sums))
    for phase, got in enumerate((got_a, got_b)):
        for i, o in enumerate(OFFSETS[phase]):
            pltpu.make_async_remote_copy(
                src_ref=moments.at[phase],
                dst_ref=got.at[i],
                send_sem=sum_send.at[phase],
                recv_sem=sum_recv.at[phase],
                device_id=member(o),
                device_id_type=MESH,
            ).start()
        if phase == 0:
            grad[0] = own_block(tall_field, PAD)
            grad[1] = own_block(field, 0)
            store_grad = pltpu.make_async_copy(grad, grad_hbm, load.at[0])
            store_grad.start()
        pltpu.make_async_copy(got, got, sum_recv.at[phase]).wait()
        moments[phase + 1] = moments[phase] + jnp.sum(got[...], axis=0)
    total = moments[2]
    gg, qq, ww, gw, pp, qp = (total[:, i : i + 1] for i in range(6))
    alpha = gg / qq
    gamma_1 = (gg - alpha * gw) - alpha * (gw - alpha * ww)
    rise = 1.0 + gamma_1 / gg
    delta_1 = rise * (rise * qq - alpha * qp) - alpha * (rise * qp - alpha * pp)
    alpha_1 = gamma_1 / delta_1
    near = alpha + alpha_1 * rise
    far = alpha * alpha_1
    factors[...] = jnp.where(line == 0, near, far)
    for phase, got in enumerate((got_a, got_b)):
        pltpu.make_async_copy(got, got, sum_send.at[phase]).wait()
    store_grad.wait()
    store_image.wait()


def finish(grad_hbm, image_hbm, obs_hbm, factors_hbm, est_hbm, res_hbm, grad, image, obs, factors, sems):
    ins = ((factors_hbm, factors), (grad_hbm, grad), (image_hbm, image), (obs_hbm, obs))
    loads = [pltpu.make_async_copy(a, b, sems.at[i]) for i, (a, b) in enumerate(ins)]
    for load in loads:
        load.start()
    loads[0].wait()
    loads[1].wait()
    near, far = factors[:, 0:1], factors[:, 1:2]
    grad[0] = near * grad[0] - far * grad[1]
    store_est = pltpu.make_async_copy(grad.at[0], est_hbm, sems.at[4])
    store_est.start()
    loads[2].wait()
    loads[3].wait()
    image[0] = obs[...] - near * image[0] + far * image[1]
    store_res = pltpu.make_async_copy(image.at[0], res_hbm, sems.at[5])
    store_res.start()
    store_est.wait()
    store_res.wait()


def body(observed, psf_tiles):
    pair = jax.ShapeDtypeStruct((2, ROWS, COLS), F32)
    hbm = pl.BlockSpec(memory_space=pltpu.HBM)
    grads, images, factors = pl.pallas_call(
        kernel,
        out_shape=(pair, pair, jax.ShapeDtypeStruct((1, TILE), F32)),
        in_specs=[hbm, hbm],
        out_specs=(hbm, hbm, pl.BlockSpec(memory_space=pltpu.VMEM)),
        scratch_shapes=[
            pltpu.VMEM((ROWS, COLS), F32),
            pltpu.VMEM((1, 2, KSIZE * KSIZE), F32),
            pltpu.VMEM((8, TILE), F32),
            pltpu.VMEM((2, 3 * TILE, WIDE + TILE), BF16),
            pltpu.VMEM((2, 4 * TILE, WIDE + TILE), BF16),
            pltpu.VMEM((2, ROWS + 2 * PAD, WIDE + TILE), F32),
            pltpu.VMEM((2, EXT_ROWS, WIDE), F32),
            pltpu.VMEM((EXT_ROWS, EXT_COLS), F32),
            pltpu.VMEM((TALL_ROWS, EXT_COLS), F32),
            pltpu.VMEM((EXT_ROWS, EXT_COLS), F32),
            pltpu.VMEM((2, ROWS, COLS), F32),
            pltpu.VMEM((2, ROWS, COLS), F32),
            pltpu.VMEM((EXT_ROWS, COLS), F32),
            pltpu.VMEM((2, EXT_ROWS, TILE), F32),
            pltpu.VMEM((2, 32, TILE), F32),
            pltpu.VMEM((56, TILE), F32),
            pltpu.VMEM((56, TILE), F32),
            pltpu.VMEM((2, 16, TILE), F32),
            pltpu.VMEM((2, 16, TILE), F32),
            pltpu.VMEM((2, 32, TILE), F32),
            pltpu.VMEM((56, TILE), F32),
            pltpu.VMEM((56, TILE), F32),
            pltpu.VMEM((2, 16, TILE), F32),
            pltpu.VMEM((2, 16, TILE), F32),
            pltpu.VMEM((208, COLS), F32),
            pltpu.VMEM((160, COLS), F32),
            pltpu.VMEM((8, PAD, TILE), F32),
            pltpu.VMEM((4 * TILE, COLS), BF16),
            pltpu.VMEM((4 * TILE, TILE), BF16),
            pltpu.VMEM((3, 1, TILE), F32),
            pltpu.VMEM((len(OFFSETS[0]), 1, TILE), F32),
            pltpu.VMEM((len(OFFSETS[1]), 1, TILE), F32),
            pltpu.SemaphoreType.DMA((8,)),
            pltpu.SemaphoreType.DMA((8,)),
            pltpu.SemaphoreType.DMA((2,)),
            pltpu.SemaphoreType.DMA((2,)),
            pltpu.SemaphoreType.DMA((2,)),
        ],
        compiler_params=pltpu.CompilerParams(
            collective_id=0, has_side_effects=True, vmem_limit_bytes=61 << 20
        ),
    )(observed, psf_tiles)
    block = jax.ShapeDtypeStruct((ROWS, COLS), F32)
    return pl.pallas_call(
        finish,
        out_shape=(block, block),
        in_specs=[pl.BlockSpec(memory_space=pltpu.HBM)] * 4,
        out_specs=(pl.BlockSpec(memory_space=pltpu.HBM),) * 2,
        scratch_shapes=[
            pltpu.VMEM((2, ROWS, COLS), F32),
            pltpu.VMEM((2, ROWS, COLS), F32),
            pltpu.VMEM((ROWS, COLS), F32),
            pltpu.VMEM((1, TILE), F32),
            pltpu.SemaphoreType.DMA((6,)),
        ],
        compiler_params=pltpu.CompilerParams(vmem_limit_bytes=61 << 20),
    )(grads, images, observed, factors)


def solution(mesh):
    return jax.shard_map(
        body,
        mesh=mesh,
        in_specs=(P("rng", "azi"), P("rng", "azi", None)),
        out_specs=(P("rng", "azi"), P("rng", "azi")),
        check_vma=False,
    )
```

```python
import itertools

import jax
import jax.numpy as jnp
from jax import lax
from jax.experimental import pallas as pl
from jax.experimental.pallas import tpu as pltpu
from jax.sharding import PartitionSpec as P

TILE = 128
KSIZE = 11
RADIUS = 5
RIM = 2 * RADIUS
ROWS = 128
COLS = 256
EXT_ROWS = 144
EXT_COLS = 384
TALL_ROWS = 176
PAD = 16
GROUPS = KSIZE * PAD
WIDE = KSIZE * TILE
MESH = pl.DeviceIdType.MESH
F32 = jnp.float32
BF16 = jnp.bfloat16

PARTS = {"x": 4, "y": 4, "z": 16, "c": 2}
PHASES = (("z", "c"), ("x", "y"))
NEIGHBOURS = tuple(
    (dr, da) for dr in (-1, 0, 1) for da in (-1, 0, 1) if (dr, da) != (0, 0)
)


def group_offsets(axes):
    ranges = [range(PARTS[axis]) for axis in axes]
    offsets = [dict(zip(axes, o)) for o in itertools.product(*ranges) if any(o)]
    return sorted(
        offsets,
        key=lambda o: -sum(min(n, PARTS[a] - n) for a, n in o.items() if a != "c"),
    )


OFFSETS = tuple(group_offsets(axes) for axes in PHASES)


def band_group(n):
    return (n * 373) >> 12


def split_rows(x):
    high = x.astype(BF16).astype(F32)
    return high, x - high


def iota(shape, dim):
    return lax.broadcasted_iota(jnp.int32, shape, dim)


def orders(taps):
    a, b = iota((TILE, TILE), 0), iota((TILE, TILE), 1)
    last = KSIZE * KSIZE - 1

    def turned(n):
        return KSIZE * (n - KSIZE * band_group(n)) + band_group(n)

    back = last - b
    wanted = (back, turned(b), jnp.where(back >= 0, turned(jnp.maximum(back, 0)), -1))
    pick = [jnp.where((a == w) & (b <= last), 1.0, 0.0).astype(BF16) for w in wanted]
    first = taps.astype(BF16)
    rest = taps - first.astype(F32)
    second = rest.astype(BF16)
    third = (rest - second.astype(F32)).astype(BF16)
    parts = jnp.concatenate([first, second, third], axis=1)
    out = [taps]
    for p in pick:
        out.append(jnp.dot(parts, jnp.concatenate([p] * 3, axis=0), preferred_element_type=F32))
    row = iota((8, TILE), 0)
    total = out[0]
    for k in range(1, 4):
        total = jnp.where((row >= 2 * k) & (row < 2 * k + 2), pltpu.roll(out[k], 2 * k, 0), total)
    return total


def sloped(line, shift, rows):
    base = pltpu.roll(jnp.broadcast_to(line, (8, TILE)), shift, 1)
    return pltpu.roll(jnp.concatenate([base] * (rows // 8), axis=0), 0, 1, stride=1, stride_axis=0)


def side_gather_weights(left, right):
    i, n = iota((40, TILE), 0), iota((40, TILE), 1)
    j = n - KSIZE * band_group(n)
    halves_ = []
    for kernel_row, start in ((left, 0), (right, 20)):
        band = sloped(kernel_row, TILE - RIM - start, 40)
        c = i - start
        keep = (c >= 0) & (c < 20) & (j < RIM) & (n < 121) & (c - j >= 0) & (c - j < KSIZE)
        halves_.append(jnp.where(keep, band, 0.0))
    high, low = split_rows(jnp.concatenate(halves_, axis=1))
    return jnp.concatenate([high, high, low, jnp.zeros((8, COLS), F32)], axis=0).astype(BF16)


def side_spread_weights(left, right):
    i, n = iota((24, TILE), 0), iota((24, TILE), 1)
    c = n - KSIZE * band_group(n)
    valid = (c < RIM) & (n < 121)
    halves_ = []
    for kernel_row, keep in (
        (left, valid & (i < RIM) & (c <= i)),
        (right, valid & (i >= RIM) & (i < 2 * RIM) & (c >= i - RIM)),
    ):
        band = sloped(kernel_row, TILE - RIM, 24)
        halves_.append(jnp.where(keep, band, 0.0))
    high, low = split_rows(jnp.concatenate(halves_, axis=1))
    return jnp.concatenate([high, high, low, jnp.zeros((TILE - 72, COLS), F32)], axis=0).astype(BF16)


def flat_bands(kernel_row, order, shift, lines):
    lane = iota((PAD, TILE), 1)
    last = KSIZE * (KSIZE - 1)
    base = pltpu.roll(jnp.broadcast_to(kernel_row, (8, TILE)), TILE - last, 1)
    taps = jnp.concatenate(
        [
            pltpu.roll(x, 0, 1, stride=KSIZE, stride_axis=0)
            for x in (base, pltpu.roll(base, 8 * KSIZE, 1))
        ],
        axis=0,
    )
    high, low = split_rows(jnp.where(lane < KSIZE, taps, 0.0))
    taps = high + pltpu.roll(high, 32, 1) + pltpu.roll(low, 64, 1)
    lines[...] = pltpu.roll(taps, shift % TILE, 1) if shift else taps
    blocks = []
    for v in order:
        line = jnp.broadcast_to(lines[v : v + 1, :], (8, TILE))
        line = pltpu.roll(line, 0, 1, stride=1, stride_axis=0)
        blocks += [line, pltpu.roll(line, 8, 1)]
    return jnp.concatenate(blocks, axis=0)


def flat_gather_weights(kernel_row, low_row, high_row, lines):
    band = flat_bands(kernel_row, range(KSIZE - 1, -1, -1), 0, lines)
    r = iota((GROUPS, TILE), 0) & (PAD - 1)
    return jnp.where((r >= low_row) & (r < high_row), band, 0.0).astype(BF16)


def flat_spread_weights(kernel_row, shift, lines):
    band = flat_bands(kernel_row, range(KSIZE), shift, lines)
    lane = iota((GROUPS, TILE), 1)
    keep = ((lane & 31) < PAD) & (lane < 96)
    return jnp.where(keep, band, 0.0).astype(BF16)


def side_fields(near, far):
    lane = iota(near.shape, 1)
    left = jnp.where(lane >= TILE - RIM, far, jnp.where(lane < RIM, near, 0.0))
    right = jnp.where(lane < 20, far, 0.0)
    x = pltpu.roll(left, RIM, 1) + pltpu.roll(right, 20, 1)
    high, low = split_rows(x)
    return (high + pltpu.roll(low, 40, 1) + pltpu.roll(high, 80, 1)).astype(BF16)


def picker(places, width):
    n = iota((TILE, width), 0)
    j = n - KSIZE * band_group(n)
    lane = iota((TILE, width), 1)
    blocks = [
        jnp.where((j < RIM) & (n < 121) & (lane == j + place), 1.0, 0.0).astype(BF16)
        for place in places
    ]
    return jnp.concatenate(blocks * 2, axis=0)


def picked(x, matrix):
    high, low = halves(x)
    return jnp.dot(jnp.concatenate([high, low], axis=1), matrix, preferred_element_type=F32)


def halves(x):
    high = x.astype(BF16)
    low = (x - high.astype(F32)).astype(BF16)
    return high, low


def kernel(
    obs_hbm,
    psf_hbm,
    grad_hbm,
    image_hbm,
    factors,
    obs_ref,
    psf_ref,
    taps,
    spread_w,
    gather_w,
    wide,
    tall,
    spill,
    tall_field,
    field,
    image,
    grad,
    shifted,
    strips,
    send_side,
    send_up,
    send_down,
    send_up_corner,
    send_down_corner,
    got_side,
    got_up,
    got_down,
    got_up_corner,
    got_down_corner,
    side_out,
    side_back,
    lines,
    pick_apart,
    pick_near,
    moments,
    got_a,
    got_b,
    halo_send,
    halo_recv,
    sum_send,
    sum_recv,
    load,
):
    rng = lax.axis_index("rng")
    azi = lax.axis_index("azi")
    place = {
        "x": azi // 8,
        "y": rng // 4,
        "z": (rng % 4) * 4 + (azi // 2) % 4,
        "c": azi % 2,
    }

    def member(offset):
        at = {
            axis: lax.rem(place[axis] + offset[axis], PARTS[axis])
            if axis in offset
            else place[axis]
            for axis in PARTS
        }
        return (at["y"] * 4 + at["z"] // 4, at["x"] * 8 + (at["z"] % 4) * 2 + at["c"])

    def neighbour(dr, da):
        return (lax.rem(rng + dr + 16, 16), lax.rem(azi + da + 32, 32))

    barrier = pltpu.get_barrier_semaphore()
    partners = [neighbour(*d) for d in NEIGHBOURS]
    partners += [member(o) for offsets in OFFSETS for o in offsets]
    for partner in partners:
        pl.semaphore_signal(barrier, inc=1, device_id=partner, device_id_type=MESH)
    load_psf = pltpu.make_async_copy(psf_hbm, psf_ref, load.at[0])
    load_obs = pltpu.make_async_copy(obs_hbm, obs_ref, load.at[1])
    load_psf.start()
    load_obs.start()

    lane = lax.broadcasted_iota(jnp.int32, (TILE, TILE), 1)
    row = lax.broadcasted_iota(jnp.int32, (TILE, TILE), 0)

    edge_lane, edge_row = lane[0:PAD], row[0:PAD]

    def band(line, shift, back):
        line = pltpu.roll(jnp.broadcast_to(line, (8, TILE)), lax.rem(3 * TILE - shift, TILE), 1)
        line = jnp.where(lane[0:8] < KSIZE, line, 0.0)
        line = pltpu.roll(line, back, 1) if back else line
        line = pltpu.roll(line, 0, 1, stride=1, stride_axis=0)
        rows = [pltpu.roll(line, 8 * g, 1) if g else line for g in range(TILE // 8)]
        return jnp.concatenate(rows, axis=0)

    def build_spread():
        def one(u, packed):
            block = pl.ds(pl.multiple_of(u * TILE, TILE), TILE)
            used = jnp.where(u < KSIZE, 1.0, 0.0)
            out = []
            for t in range(2):
                rows = band(taps[t : t + 1, :], KSIZE * u, 0)
                edge = rows[TILE - PAD :]
                below = edge_lane < edge_row + (TILE - PAD)
                over = jnp.where(below, edge, 0.0) * used
                out.append(packed[t] + pltpu.roll(over, lax.rem(KSIZE * u, TILE), 1))
                main = jnp.concatenate([rows[0 : TILE - PAD], jnp.where(below, 0.0, edge)], axis=0)
                high, low = halves(main)
                spread_w[t, 0:TILE, block] = high
                spread_w[t, TILE : 2 * TILE, block] = high
                spread_w[t, 2 * TILE :, block] = low
            return tuple(out)

        def three(i, packed):
            for k in range(3):
                packed = one(3 * i + k, packed)
            return packed

        packed = lax.fori_loop(0, 4, three, (jnp.zeros((PAD, TILE), F32),) * 2)
        blank = jnp.zeros((TILE - PAD, TILE), BF16)
        for t in range(2):
            high, low = (jnp.concatenate([blank, p], axis=0) for p in halves(packed[t]))
            spread_w[t, 0:TILE, WIDE:] = high
            spread_w[t, TILE : 2 * TILE, WIDE:] = high
            spread_w[t, 2 * TILE :, WIDE:] = low

    def build_gather():
        gather_w[:, 3 * TILE + 3 * PAD :, :] = jnp.zeros((2, TILE - 3 * PAD, WIDE + TILE), BF16)

        def one(u, carry):
            block = pl.ds(pl.multiple_of(u * TILE, TILE), TILE)
            for t in range(2):
                rows = band(taps[2 + t : 3 + t, :], KSIZE * (KSIZE - 1) - KSIZE * u, TILE - RIM)
                edge = rows[0:PAD]
                past = edge_lane > edge_row
                high, low = halves(jnp.where(past, edge, 0.0))
                gather_w[t, 3 * TILE : 3 * TILE + PAD, block] = high
                gather_w[t, 3 * TILE + PAD : 3 * TILE + 2 * PAD, block] = high
                gather_w[t, 3 * TILE + 2 * PAD : 3 * TILE + 3 * PAD, block] = low
                main = jnp.concatenate([jnp.where(past, 0.0, edge), rows[PAD:]], axis=0)
                high, low = halves(main)
                gather_w[t, 0:TILE, block] = high
                gather_w[t, TILE : 2 * TILE, block] = high
                gather_w[t, 2 * TILE : 3 * TILE, block] = low
            return carry

        def three(i, carry):
            for k in range(3):
                one(3 * i + k, carry)
            return carry

        lax.fori_loop(0, 4, three, 0)

    pick_apart[...] = picker((0, TILE), COLS)
    pick_near[...] = picker((0, RIM), TILE)
    load_psf.wait()
    taps[...] = jnp.zeros_like(taps)
    taps[0:2, 0 : KSIZE * KSIZE] = psf_ref[0]
    kernels = orders(taps[...])
    taps[...] = kernels
    build_spread()
    wide[:, 0:PAD, :] = jnp.zeros((2, PAD, WIDE + TILE), F32)
    wide[:, PAD + ROWS :, :] = jnp.zeros((2, PAD, WIDE + TILE), F32)

    def spread(source, out):
        group = band_group(iota((1, TILE), 1))
        spares = []
        for t in range(2):
            high, low = halves(source[:, t * TILE : (t + 1) * TILE])
            left = jnp.concatenate([high, low, high], axis=1)
            for n in range(0, WIDE + TILE, 256):
                wide[t, PAD : PAD + ROWS, n : n + 256] = jnp.dot(
                    left, spread_w[t, :, n : n + 256], preferred_element_type=F32
                )
            total, spare = None, jnp.zeros((EXT_ROWS, TILE), F32)
            for u in range(KSIZE):
                rows = pl.ds(PAD - u, EXT_ROWS)
                piece = wide[t, rows, u * TILE : (u + 1) * TILE]
                total = piece if total is None else total + piece
                spare = jnp.where(group == u, wide[t, rows, WIDE:], spare)
            out[:, t * TILE : (t + 1) * TILE] = total
            spares.append(spare)
        over = picked(jnp.concatenate(spares, axis=1), pick_apart[...])
        out[:, TILE : 2 * TILE] += over[:, 0:TILE]
        out[:, 2 * TILE :] = over[:, TILE:]

    def gather(source, row, t):
        tall_lane = lax.broadcasted_iota(jnp.int32, (EXT_ROWS, TILE), 1)
        high, low = halves(source[row : row + EXT_ROWS, t * TILE : (t + 1) * TILE])
        edge = source[row : row + EXT_ROWS, (t + 1) * TILE : (t + 2) * TILE]
        edge = jnp.where(tall_lane < RIM, edge, 0.0)
        edge_high = edge.astype(BF16).astype(F32)
        edge_low = edge - edge_high
        edge = edge_high + pltpu.roll(edge_low, PAD, 1) + pltpu.roll(edge_high, 2 * PAD, 1)
        left = jnp.concatenate([high, low, high, edge.astype(BF16)], axis=1)
        total = None
        for n in range(0, WIDE, 256):
            width = min(256, WIDE - n)
            tall[t, :, n : n + width] = jnp.dot(
                left, gather_w[t, :, n : n + width], preferred_element_type=F32
            )
        for u in range(KSIZE):
            piece = tall[t, pl.ds(u, ROWS), u * TILE : (u + 1) * TILE]
            total = piece if total is None else total + piece
        return total

    def pack(strip, rows):
        out = None
        for k in range(strip.shape[0] // rows):
            part = strip[rows * k : rows * k + rows]
            part = jnp.where(lane[0:rows] < 2 * RIM, part, 0.0)
            part = pltpu.roll(part, 2 * RIM * k, 1) if k else part
            out = part if out is None else out + part
        return out

    def unpack(packed, groups):
        parts = []
        for k in range(groups):
            part = pltpu.roll(packed, TILE - 2 * RIM * k, 1) if k else packed
            parts.append(jnp.where(lane[0 : packed.shape[0]] < 2 * RIM, part, 0.0))
        return jnp.concatenate(parts, axis=0)

    def start_exchange():
        side = iota((EXT_ROWS, TILE), 1)
        right = jnp.where(side >= TILE - RIM, spill[:, TILE : 2 * TILE], spill[:, 2 * TILE :])
        strips[0] = spill[:, 0:TILE]
        strips[1] = pltpu.roll(right, RIM, 1)
        for i in range(2):
            send_side[i, 0:24] = pack(strips[i], 24)
            send_side[i, 24:] = kernels
            send_up_corner[i, 0:8] = pack(strips[i, 0:24], 8)
            send_up_corner[i, 8:] = kernels
            send_down_corner[i, 0:8] = pack(strips[i, 118:142], 8)
            send_down_corner[i, 8:] = kernels
        for send, at in ((send_up, 0), (send_down, 118)):
            for t in range(2):
                tile = slice(t * TILE, (t + 1) * TILE)
                send[16 * t : 16 * t + 16] = spill[at : at + 16, tile]
                send[32 + 4 * t : 36 + 4 * t] = spill[at + 16 : at + 20, tile]
            send[40:48] = pack(spill[at : at + 24, 2 * TILE :], 8)
            send[48:] = kernels
        plan = {
            (-1, 1): (send_up_corner.at[1], got_up_corner.at[1]),
            (1, -1): (send_down_corner.at[0], got_down_corner.at[0]),
            (-1, -1): (send_up_corner.at[0], got_up_corner.at[0]),
            (1, 1): (send_down_corner.at[1], got_down_corner.at[1]),
            (-1, 0): (send_up, got_up),
            (1, 0): (send_down, got_down),
            (0, -1): (send_side.at[0], got_side.at[0]),
            (0, 1): (send_side.at[1], got_side.at[1]),
        }
        return [
            pltpu.make_async_remote_copy(
                src_ref=source,
                dst_ref=target,
                send_sem=halo_send.at[i],
                recv_sem=halo_recv.at[i],
                device_id=neighbour(*d),
                device_id_type=MESH,
            )
            for i, (d, (source, target)) in enumerate(plan.items())
        ]

    above = jnp.where(rng > 0, 1.0, 0.0)
    below = jnp.where(rng < 15, 1.0, 0.0)
    left_of = jnp.where(azi > 0, 1.0, 0.0)
    right_of = jnp.where(azi < 31, 1.0, 0.0)

    def assemble():
        first, last = slice(0, TILE), slice(2 * TILE, EXT_COLS)
        tall_field[0:PAD] = jnp.zeros((PAD, EXT_COLS), F32)
        tall_field[PAD : PAD + EXT_ROWS] = spill[...]
        tall_field[PAD + EXT_ROWS :] = jnp.zeros((PAD, EXT_COLS), F32)
        for got, at, flag in ((got_down, 6, above), (got_up, 144, below)):
            for t in range(2):
                tile = slice(t * TILE, (t + 1) * TILE)
                tall_field[at : at + 16, tile] += got[16 * t : 16 * t + 16] * flag
                tall_field[at + 16 : at + 20, tile] += got[32 + 4 * t : 36 + 4 * t] * flag
            tall_field[at : at + 24, last] += unpack(got[40:48], 3) * flag

        def from_left(strip, rows, flag):
            strip = pltpu.roll(strip, TILE - RIM, 1) * flag
            near = iota(strip.shape, 1) < TILE // 2
            tall_field[rows, first] += jnp.where(near, strip, 0.0)
            tall_field[rows, last] += jnp.where(near, 0.0, strip)

        def from_right(strip, rows, flag):
            tall_field[rows, last] += strip * flag

        middle, top, bottom = slice(16, 160), slice(6, 30), slice(144, 168)
        from_right(unpack(got_side[0, 0:24], 6), middle, right_of)
        from_left(unpack(got_side[1, 0:24], 6), middle, left_of)
        from_right(unpack(got_down_corner[0, 0:8], 3), top, above * right_of)
        from_left(unpack(got_down_corner[1, 0:8], 3), top, above * left_of)
        from_right(unpack(got_up_corner[0, 0:8], 3), bottom, below * right_of)
        from_left(unpack(got_up_corner[1, 0:8], 3), bottom, below * left_of)
        r, c = iota((TALL_ROWS, EXT_COLS), 0), iota((TALL_ROWS, EXT_COLS), 1)
        inside = (
            (r >= jnp.where(rng == 0, PAD + RADIUS, 0))
            & (r < jnp.where(rng == 15, PAD + RADIUS + ROWS, TALL_ROWS))
            & (c >= jnp.where(azi == 0, RADIUS, 0))
            & (c < jnp.where(azi == 0, 320, EXT_COLS))
            & ((c < jnp.where(azi == 31, RADIUS + COLS, EXT_COLS)) | (c >= 320))
        )
        tall_field[...] = jnp.where(inside, tall_field[...], 0.0)

    def side_kernels(k):
        return tuple(
            (got[1, at + 1 + k : at + 2 + k] * (flag * left_of), got[0, at + k : at + 1 + k] * (flag * right_of))
            for got, at, flag in ((got_down_corner, 8, above), (got_side, 24, 1.0), (got_up_corner, 8, below))
        )

    def side_frames():
        fields = side_fields(tall_field[:, 0:TILE], tall_field[:, 2 * TILE :])
        parts = ((0, 32, 144, 16), (16, 144, 0, 128), (144, 32, 176, 16))
        group = band_group(iota((1, COLS), 1) & (TILE - 1))
        sums = []
        for (start, count, at, rows), (left, right) in zip(parts, side_kernels(2)):
            side_out[at : at + count] = jnp.dot(
                fields[start : start + count], side_gather_weights(left, right), preferred_element_type=F32
            )
            total = jnp.zeros((rows, COLS), F32)
            for u in range(KSIZE):
                total = jnp.where(group == KSIZE - 1 - u, side_out[at + u : at + u + rows], total)
            sums.append(total)
        frames = picked(jnp.concatenate(sums, axis=0), pick_near[...])
        r = iota(frames.shape, 0)
        return jnp.where((r >= 6) & (r < 154), frames, 0.0)

    def side_spread(frames):
        high, low = split_rows(frames)
        packed = (high + pltpu.roll(low, 24, 1) + pltpu.roll(high, 48, 1)).astype(BF16)
        for (start, stop), (left, right) in zip(((0, 16), (16, 144), (144, 160)), side_kernels(0)):
            side_back[start:stop] = jnp.dot(
                packed[start:stop], side_spread_weights(left, right), preferred_element_type=F32
            )
        group = band_group(iota((1, COLS), 1) & (TILE - 1))
        total = jnp.zeros((EXT_ROWS, COLS), F32)
        for u in range(KSIZE):
            total = jnp.where(group == u, side_back[PAD - u : PAD - u + EXT_ROWS], total)
        out = picked(total, pick_apart[...])
        return out[:, 0:TILE], out[:, TILE:]

    def flat_frames(rows, kernels, low_row, at):
        high, low = halves(tall_field[rows, :])
        right = jnp.concatenate([high, low, high, jnp.zeros((32, EXT_COLS), BF16)], axis=0)
        tiles = []
        for t in range(2):
            out = jnp.dot(
                flat_gather_weights(kernels[t], low_row, low_row + RIM, lines.at[at + t]),
                right[:, t * TILE : t * TILE + COLS],
                preferred_element_type=F32,
            )
            total = out[0:PAD]
            for v in range(1, KSIZE):
                total = total + pltpu.roll(out[PAD * v : PAD * v + PAD], COLS - v, 1)
            tiles.append(total[:, 0:TILE])
        return tiles

    def flat_spread(tiles, kernels, shift, at):
        outs = []
        for t in range(2):
            high, low = halves(tiles[t])
            gap = jnp.zeros((PAD, TILE), BF16)
            right = jnp.concatenate([high, gap, low, gap, high, gap, gap, gap], axis=0)
            out = jnp.dot(flat_spread_weights(kernels[t], shift, lines.at[at + t]), right, preferred_element_type=F32)
            near, far = out[0:PAD], None
            for v in range(1, KSIZE):
                piece = pltpu.roll(out[PAD * v : PAD * v + PAD], v, 1)
                past = edge_lane < v
                near = near + jnp.where(past, 0.0, piece)
                piece = jnp.where(past, piece, 0.0)
                far = piece if far is None else far + piece
            total = jnp.concatenate([near, far], axis=1)
            outs.append(total)
        return outs

    def inner(x, y):
        z = x * y
        z = z[:, 0:TILE] + z[:, TILE:]
        while z.shape[0] > 8:
            half = z.shape[0] // 2
            z = z[0:half] + z[half:]
        return jnp.sum(jnp.sum(z, axis=0, keepdims=True), axis=1, keepdims=True)

    def inner_rimmed(x, y):
        r, c = iota((EXT_ROWS, EXT_COLS), 0), iota((EXT_ROWS, EXT_COLS), 1)
        own = (r >= RADIUS) & (r < ROWS + RADIUS) & (c >= RADIUS) & (c < COLS + RADIUS)
        z = jnp.where(own, x * y, 0.0)
        z = z[:, 0:TILE] + z[:, TILE : 2 * TILE] + z[:, 2 * TILE :]
        z = z[0:72] + z[72:]
        z = (z[0:24] + z[24:48]) + z[48:72]
        z = (z[0:8] + z[8:16]) + z[16:24]
        return jnp.sum(jnp.sum(z, axis=0, keepdims=True), axis=1, keepdims=True)

    def own_block(source, row):
        shifted[...] = pltpu.roll(source[row : row + EXT_ROWS, :], EXT_COLS - RADIUS, 1)[:, 0:COLS]
        return shifted[pl.ds(RADIUS, ROWS), :]

    load_obs.wait()
    spread(obs_ref[...], spill)
    copies = start_exchange()
    pl.semaphore_wait(barrier, len(partners))
    for copy in copies:
        copy.start()
    build_gather()
    for copy in copies:
        copy.wait()
    assemble()
    for t in range(2):
        image[0, :, t * TILE : (t + 1) * TILE] = gather(tall_field, PAD, t)
    frames = side_frames()
    kernels_top = [got_down[52 + t : 53 + t] * above for t in range(2)]
    kernels_bottom = [got_up[52 + t : 53 + t] * below for t in range(2)]
    frames_top = flat_frames(slice(0, 32), kernels_top, 6, 0)
    frames_bottom = flat_frames(slice(144, 176), kernels_bottom, 0, 2)
    spread(image[0], field)
    to_left, to_right = side_spread(frames)
    field[:, 0:TILE] += to_left
    field[:, 2 * TILE :] += to_right
    kernels_top = [got_down[54 + t : 55 + t] * above for t in range(2)]
    kernels_bottom = [got_up[54 + t : 55 + t] * below for t in range(2)]
    for t, out in enumerate(flat_spread(frames_top, kernels_top, 6, 4)):
        field[0:PAD, t * TILE : t * TILE + COLS] += out
    for t, out in enumerate(flat_spread(frames_bottom, kernels_bottom, -RIM, 6)):
        field[ROWS:, t * TILE : t * TILE + COLS] += out
    r, c = iota((EXT_ROWS, EXT_COLS), 0), iota((EXT_ROWS, EXT_COLS), 1)
    inside = (
        (r >= jnp.where(rng == 0, RADIUS, 0))
        & (r < jnp.where(rng == 15, ROWS + RADIUS, EXT_ROWS))
        & (c >= jnp.where(azi == 0, RADIUS, 0))
        & (c < jnp.where(azi == 31, COLS + RADIUS, EXT_COLS))
    )
    field[...] = jnp.where(inside, field[...], 0.0)
    for t in range(2):
        image[1, :, t * TILE : (t + 1) * TILE] = gather(field, 0, t)
    store_image = pltpu.make_async_copy(image, image_hbm, load.at[1])
    store_image.start()
    first = tall_field[PAD : PAD + EXT_ROWS, :]
    second = field[...]
    sums = [inner_rimmed(first, first), inner(image[0], image[0])]
    sums += [inner_rimmed(second, second), inner_rimmed(first, second)]
    sums += [inner(image[1], image[1]), inner(image[0], image[1])]
    line = lane[0:1]
    moments[0] = sum(jnp.where(line == i, x, 0.0) for i, x in enumerate(sums))
    for phase, got in enumerate((got_a, got_b)):
        for i, o in enumerate(OFFSETS[phase]):
            pltpu.make_async_remote_copy(
                src_ref=moments.at[phase],
                dst_ref=got.at[i],
                send_sem=sum_send.at[phase],
                recv_sem=sum_recv.at[phase],
                device_id=member(o),
                device_id_type=MESH,
            ).start()
        if phase == 0:
            grad[0] = own_block(tall_field, PAD)
            grad[1] = own_block(field, 0)
            store_grad = pltpu.make_async_copy(grad, grad_hbm, load.at[0])
            store_grad.start()
        pltpu.make_async_copy(got, got, sum_recv.at[phase]).wait()
        moments[phase + 1] = moments[phase] + jnp.sum(got[...], axis=0)
    total = moments[2]
    gg, qq, ww, gw, pp, qp = (total[:, i : i + 1] for i in range(6))
    alpha = gg / qq
    gamma_1 = (gg - alpha * gw) - alpha * (gw - alpha * ww)
    rise = 1.0 + gamma_1 / gg
    delta_1 = rise * (rise * qq - alpha * qp) - alpha * (rise * qp - alpha * pp)
    alpha_1 = gamma_1 / delta_1
    near = alpha + alpha_1 * rise
    far = alpha * alpha_1
    factors[...] = jnp.where(line == 0, near, far)
    for phase, got in enumerate((got_a, got_b)):
        pltpu.make_async_copy(got, got, sum_send.at[phase]).wait()
    store_grad.wait()
    store_image.wait()


def finish(grad_hbm, image_hbm, obs_hbm, factors_hbm, est_hbm, res_hbm, grad, image, obs, factors, sems):
    ins = ((factors_hbm, factors), (grad_hbm, grad), (image_hbm, image), (obs_hbm, obs))
    loads = [pltpu.make_async_copy(a, b, sems.at[i]) for i, (a, b) in enumerate(ins)]
    for load in loads:
        load.start()
    loads[0].wait()
    loads[1].wait()
    near, far = factors[:, 0:1], factors[:, 1:2]
    grad[0] = near * grad[0] - far * grad[1]
    store_est = pltpu.make_async_copy(grad.at[0], est_hbm, sems.at[4])
    store_est.start()
    loads[2].wait()
    loads[3].wait()
    image[0] = obs[...] - near * image[0] + far * image[1]
    store_res = pltpu.make_async_copy(image.at[0], res_hbm, sems.at[5])
    store_res.start()
    store_est.wait()
    store_res.wait()


def body(observed, psf_tiles):
    pair = jax.ShapeDtypeStruct((2, ROWS, COLS), F32)
    hbm = pl.BlockSpec(memory_space=pltpu.HBM)
    grads, images, factors = pl.pallas_call(
        kernel,
        out_shape=(pair, pair, jax.ShapeDtypeStruct((1, TILE), F32)),
        in_specs=[hbm, hbm],
        out_specs=(hbm, hbm, pl.BlockSpec(memory_space=pltpu.VMEM)),
        scratch_shapes=[
            pltpu.VMEM((ROWS, COLS), F32),
            pltpu.VMEM((1, 2, KSIZE * KSIZE), F32),
            pltpu.VMEM((8, TILE), F32),
            pltpu.VMEM((2, 3 * TILE, WIDE + TILE), BF16),
            pltpu.VMEM((2, 4 * TILE, WIDE + TILE), BF16),
            pltpu.VMEM((2, ROWS + 2 * PAD, WIDE + TILE), F32),
            pltpu.VMEM((2, EXT_ROWS, WIDE), F32),
            pltpu.VMEM((EXT_ROWS, EXT_COLS), F32),
            pltpu.VMEM((TALL_ROWS, EXT_COLS), F32),
            pltpu.VMEM((EXT_ROWS, EXT_COLS), F32),
            pltpu.VMEM((2, ROWS, COLS), F32),
            pltpu.VMEM((2, ROWS, COLS), F32),
            pltpu.VMEM((EXT_ROWS, COLS), F32),
            pltpu.VMEM((2, EXT_ROWS, TILE), F32),
            pltpu.VMEM((2, 32, TILE), F32),
            pltpu.VMEM((56, TILE), F32),
            pltpu.VMEM((56, TILE), F32),
            pltpu.VMEM((2, 16, TILE), F32),
            pltpu.VMEM((2, 16, TILE), F32),
            pltpu.VMEM((2, 32, TILE), F32),
            pltpu.VMEM((56, TILE), F32),
            pltpu.VMEM((56, TILE), F32),
            pltpu.VMEM((2, 16, TILE), F32),
            pltpu.VMEM((2, 16, TILE), F32),
            pltpu.VMEM((208, COLS), F32),
            pltpu.VMEM((160, COLS), F32),
            pltpu.VMEM((8, PAD, TILE), F32),
            pltpu.VMEM((4 * TILE, COLS), BF16),
            pltpu.VMEM((4 * TILE, TILE), BF16),
            pltpu.VMEM((3, 1, TILE), F32),
            pltpu.VMEM((len(OFFSETS[0]), 1, TILE), F32),
            pltpu.VMEM((len(OFFSETS[1]), 1, TILE), F32),
            pltpu.SemaphoreType.DMA((8,)),
            pltpu.SemaphoreType.DMA((8,)),
            pltpu.SemaphoreType.DMA((2,)),
            pltpu.SemaphoreType.DMA((2,)),
            pltpu.SemaphoreType.DMA((2,)),
        ],
        compiler_params=pltpu.CompilerParams(
            collective_id=0, has_side_effects=True, vmem_limit_bytes=61 << 20
        ),
    )(observed, psf_tiles)
    block = jax.ShapeDtypeStruct((ROWS, COLS), F32)
    return pl.pallas_call(
        finish,
        out_shape=(block, block),
        in_specs=[pl.BlockSpec(memory_space=pltpu.HBM)] * 4,
        out_specs=(pl.BlockSpec(memory_space=pltpu.HBM),) * 2,
        scratch_shapes=[
            pltpu.VMEM((2, ROWS, COLS), F32),
            pltpu.VMEM((2, ROWS, COLS), F32),
            pltpu.VMEM((ROWS, COLS), F32),
            pltpu.VMEM((1, TILE), F32),
            pltpu.SemaphoreType.DMA((6,)),
        ],
        compiler_params=pltpu.CompilerParams(vmem_limit_bytes=61 << 20),
    )(grads, images, observed, factors)


def solution(mesh):
    return jax.shard_map(
        body,
        mesh=mesh,
        in_specs=(P("rng", "azi"), P("rng", "azi", None)),
        out_specs=(P("rng", "azi"), P("rng", "azi")),
        check_vma=False,
    )
```
